256 devices in a mesh: beam: 2 (over z), tm: 16 (over x, core), dm: 8 (over y).
Axes of the slice: x: 8, y: 8, z: 2, core: 2. Of those that a mesh axis runs over, the one named last changes fastest.
The devices are a block of a 8x8x16 slice.
Arguments:
- series: float32 [32, 524288], P(('beam', 'dm'), 'tm'), parts along dimension 0, may hold values from -16 to 16
- cand_start: int32 [32, 8, 8, 16], P(('beam', 'tm'), 'dm'), parts along dimension 0, may hold values from 0 to 1920
- cand_count: int32 [32, 8, 8], P(('beam', 'tm'), 'dm'), parts along dimension 0, may hold values from 0 to 16, as said below
Outputs:
- harmonic_sum: float32 [32, 32768], P(('beam', 'dm'), 'tm'), parts along dimension 0
- sifted: float32 [32, 8, 8, 16, 128], P(('beam', 'tm'), 'dm'), parts along dimension 0
The draws below stay inside these ranges and needn't reach their ends.
There are 2 independent parts, one for each index of `beam`. The reference program is written for one: setup_inputs(seed, part) draws one part's arguments, and reference() takes and returns one part's arrays. A program takes and returns all parts, laid end to end along the dimension named above; each array names one. Nothing has to cross between parts.
Inputs may be any that keep to these rules, and one draw needn't show every extreme that they name: `cand_count`: in every draw some destination band receives 16 live slots from every source band and frequency shard.
All inputs are finite; a program needn't handle non-finite values.
Results may differ from the reference program's by a relative error of at most 0.00015.
Values sent between devices are 32-bit elements; how exact they have to be, the bound alone decides.
A program may use at most 128 MiB of HBM per device.

```python
import jax
import jax.numpy as jnp
from jax import lax

DM_DEV = 2
NT = 524288
N1 = 512
HARM = 8
BW = 128
CAP = 16
NDM = 16
TSHARDS = 16
BANDS = 8
NH = 32768
FL = 2048


def draw_series(key, part):
    noise_key, echo_key, gain_key = jax.random.split(jax.random.fold_in(key, 11), 3)
    echo_lag = NT // N1
    noise = jax.random.truncated_normal(noise_key, -4.0, 4.0, (NDM, NT + echo_lag), jnp.float32)
    echo_level = jax.random.uniform(echo_key, (NDM, 1), jnp.float32, 0.4, 0.8)
    time_ramp = jnp.ones((1, NT), jnp.float32)
    row_gain = jax.random.uniform(gain_key, (NDM, 1), jnp.float32, 0.5, 2.0)
    return (row_gain * time_ramp * (noise[:, echo_lag:] + echo_level * noise[:, :NT])).astype(jnp.float32)


def draw_cand_count(key, part):
    base_key, light_key, chosen_key = jax.random.split(jax.random.fold_in(key, 23), 3)
    counts = jax.random.randint(base_key, (TSHARDS, BANDS, BANDS), 0, CAP + 1)
    lighter = jax.random.randint(light_key, (BANDS,), 0, 2)
    chosen = jax.random.randint(chosen_key, (), 0, BANDS)
    targets = jnp.arange(BANDS, dtype=jnp.int32)
    counts = jnp.where(lighter[None, None, :] == 1, counts // 2, counts)
    counts = jnp.where(targets[None, None, :] == chosen, CAP, counts)
    return counts.astype(jnp.int32)


def place_ends(result, key, least, top_value):
    extent = result.shape
    index_at = [jax.random.randint(jax.random.fold_in(key, axis), (), 0, extent[axis]) for axis in range(len(extent))]
    result = result.at[tuple(index_at)].set(least)
    longest = extent.index(max(extent))
    index_at[longest] = (index_at[longest] + 1) % extent[longest]
    return result.at[tuple(index_at)].set(top_value)


def setup_inputs(seed: int = 0, part: int = 0) -> dict:
    key_of = jax.random.split(jax.random.key(seed), 4)
    own_keys = jax.random.split(jax.random.fold_in(key_of[3], part), 4)
    return {
        "series": draw_series(jax.random.fold_in(jax.random.fold_in(key_of[3], part), 71), part),
        "cand_start": place_ends(jax.random.randint(own_keys[1], (TSHARDS, BANDS, BANDS, CAP), 0, FL - BW + 1), jax.random.fold_in(own_keys[1], 1), 0, FL - BW).astype(jnp.int32),
        "cand_count": draw_cand_count(jax.random.fold_in(jax.random.fold_in(key_of[3], part), 71), part),
    }


EPSILON = 1e-06

def reference(series, cand_start, cand_count):
    spectrum = jnp.fft.rfft(series, axis=-1)[:, :NT // 2]
    power_bins = ((jnp.real(spectrum) ** 2 + jnp.imag(spectrum) ** 2) / NT).astype(jnp.float32)
    row_mean = lax.optimization_barrier(jnp.mean(power_bins, axis=1, keepdims=True))
    deviation = power_bins - row_mean
    spread = lax.optimization_barrier(jnp.mean(deviation * deviation, axis=1, keepdims=True))
    scores = deviation / jnp.sqrt(spread + EPSILON)
    summed = scores[:, :NH]
    for harmonic in range(2, HARM + 1):
        summed = summed + scores[:, 0:harmonic * NH:harmonic]
    banded = summed.reshape(BANDS, DM_DEV, TSHARDS, FL)
    peak_rows = lax.optimization_barrier(jnp.max(banded, axis=1))
    band_level = lax.optimization_barrier(jnp.sum(banded, axis=1)) / DM_DEV
    bin_span = cand_start[..., None] + jnp.arange(BW, dtype=jnp.int32)
    shard_ids = jnp.arange(TSHARDS, dtype=jnp.int32)[:, None, None, None, None]
    source_ids = jnp.arange(BANDS, dtype=jnp.int32)[None, :, None, None, None]
    target_ids = jnp.arange(BANDS, dtype=jnp.int32)[None, None, :, None, None]
    top_values = peak_rows[source_ids, shard_ids, bin_span]
    low_values = band_level[target_ids, shard_ids, bin_span]
    slot_ids = jnp.arange(CAP, dtype=jnp.int32)[None, None, None, :, None]
    live_slots = slot_ids < cand_count[..., None, None]
    sifted = jnp.where(live_slots, top_values - low_values, jnp.float32(0.0))
    sifted = jnp.transpose(sifted, (0, 2, 1, 3, 4))
    return (summed, sifted)
```

```python
import functools
import math

import jax
import jax.numpy as jnp
import numpy as np
from jax import lax
from jax.experimental import pallas as pl
from jax.experimental.pallas import tpu as pltpu
from jax.sharding import PartitionSpec as P

HARM = 8
BW = 128
EPSILON = 1e-06
LANES = 128
RADIX = 16
JOBS = RADIX // 2
LEFT, RIGHT = 128, 256
MESH = pl.DeviceIdType.MESH
SLOT_RESIDUES = (1, 3, 5, 7, 9, 11, 13, 15, 2, 6, 10, 14, 4, 12, 8, 0)
HALF = JOBS


def tables(total):
    def wave(left, right, period):
        angle = 2.0 * math.pi * (np.outer(left, right) % period) / period
        return np.cos(angle), np.sin(angle)

    left, right, radix = np.arange(LEFT), np.arange(RIGHT), np.arange(RADIX)
    parts = [
        *wave(left, left, LEFT),
        *wave(left, right, LEFT * RIGHT),
        *wave(left, right, RIGHT),
        *wave(radix, left, RADIX * LEFT),
        *wave(radix, right, total),
    ]
    rows, offsets = [], []
    for part in parts:
        offsets.append(sum(r.shape[0] for r in rows))
        for lane in range(0, part.shape[1], LANES):
            rows.append(part[:, lane : lane + LANES])
    return np.concatenate(rows).astype(np.float32), offsets


def split(value):
    high = value.astype(jnp.bfloat16)
    return high, (value - high.astype(jnp.float32)).astype(jnp.bfloat16)


def split_exactly(value):
    high, rest = value.astype(jnp.bfloat16), None
    rest = value - high.astype(jnp.float32)
    middle = rest.astype(jnp.bfloat16)
    return high, middle, (rest - middle.astype(jnp.float32)).astype(jnp.bfloat16)


def dot(left, right, dims):
    return lax.dot_general(left, right, (dims, ((), ())), preferred_element_type=jnp.float32)


def dot_split(left, right, dims):
    (lh, ll), (rh, rl) = left, right
    return dot(lh, rh, dims) + (dot(ll, rh, dims) + dot(lh, rl, dims))


def radix_transform(x):
    half, quarter = RADIX // 2, RADIX // 4

    def real_transform(values, count):
        if count == 1:
            return [(values[0], None)]
        low = [values[i] + values[i + count // 2] for i in range(count // 2)]
        high = [values[i] - values[i + count // 2] for i in range(count // 2)]
        out = {2 * i: v for i, v in enumerate(real_transform(low, count // 2))}
        if count == 2:
            out[1] = (high[0], None)
        elif count == 4:
            out[1] = (high[0], -high[1])
        else:
            h, q = count // 2, count // 4
            minus = [None] + [high[i] - high[h - i] for i in range(1, q)]
            plus = [None] + [high[i] + high[h - i] for i in range(1, q)]
            for term in range(1, h, 2):
                re, im = high[0], high[q] * (-math.sin(2 * math.pi * q * term / count))
                for i in range(1, q):
                    re = re + minus[i] * math.cos(2 * math.pi * i * term / count)
                    im = im - plus[i] * math.sin(2 * math.pi * i * term / count)
                out[term] = (re, im)
        return [out[i] for i in range(count // 2 + 1)]

    return real_transform(x, RADIX)


def picks(job):
    pair = (0, RADIX // 2) if job == 0 else (job, RADIX - job)
    found = {}
    for slot, residue in enumerate(SLOT_RESIDUES):
        for harmonic in range(1, HARM + 1):
            product = harmonic * residue
            if product % RADIX in pair:
                found.setdefault(slot, []).append(
                    (pair.index(product % RADIX), harmonic, product // RADIX)
                )
    return found


def search_kernel(
    shards, bands, offsets, total,
    x_ref, start_ref, count_ref, tab_hbm,
    hsum_ref, diff_ref, mark_ref,
    tab, x_in, y_out, y_in, w_hi, w_lo, g_hi, g_lo, t_cos, t_sin, pw,
    h_out, h_in, st_out, st_in, mk_out, mk_in, pk_out, pk_in,
    send_x, recv_x, send_y, recv_y, send_h, recv_h, send_s, recv_s,
    send_m, recv_m, send_p, recv_p, local_sem,
):
    me = lax.axis_index("tm")
    band = lax.axis_index("dm")
    job, row_kept = me // 2, me % 2
    bins = total // 2
    x_rows = x_in.shape[1]

    barrier = pltpu.get_barrier_semaphore()
    for i in range(1, shards):
        pl.semaphore_signal(
            barrier, inc=1, device_id={"tm": lax.rem(me + i, shards)}, device_id_type=MESH
        )
    for i in range(1, bands):
        pl.semaphore_signal(
            barrier, inc=1, device_id={"dm": lax.rem(band + i, bands)}, device_id_type=MESH
        )
    pl.semaphore_wait(barrier, shards + bands - 2)

    def remote(src, dst, send, recv, axis, peer):
        return pltpu.make_async_remote_copy(
            src_ref=src, dst_ref=dst, send_sem=send, recv_sem=recv,
            device_id={axis: peer}, device_id_type=MESH,
        )

    def x_copy(peer, slot):
        rows = pl.ds(pl.multiple_of(peer * x_rows, x_rows), x_rows)
        return remote(x_ref.at[rows], x_in.at[slot], send_x.at[peer], recv_x.at[slot], "tm", peer)

    def y_copy(peer, slot):
        rows = pl.ds(pl.multiple_of(slot * 8, 8), 8)
        return remote(y_out.at[peer], y_in.at[:, rows], send_y.at[peer], recv_y.at[slot], "tm", peer)

    def h_copy(peer, slot, rows):
        part = pl.ds(0, rows)
        return remote(
            h_out.at[peer, part], h_in.at[slot, part], send_h.at[peer], recv_h.at[slot], "tm", peer
        )

    def s_copy(peer, slot):
        return remote(st_out, st_in.at[slot], send_s.at[peer], recv_s.at[slot], "tm", peer)

    def m_copy(peer, slot):
        return remote(mk_out.at[peer], mk_in.at[slot], send_m.at[peer], recv_m.at[slot], "dm", peer)

    def p_copy(peer, slot):
        return remote(pk_out, pk_in.at[slot], send_p.at[peer], recv_p.at[slot], "dm", peer)

    others = [lax.rem(me + i, shards) for i in range(1, shards)]
    other_bands = [lax.rem(band + i, bands) for i in range(1, bands)]

    for peer in others:
        x_copy(peer, me).start()
    own_rows = pl.ds(pl.multiple_of(me * x_rows, x_rows), x_rows)
    own_x = pltpu.make_async_copy(x_ref.at[own_rows], x_in.at[me], local_sem.at[0])
    own_x.start()
    get_tab = pltpu.make_async_copy(tab_hbm, tab, local_sem.at[1])
    get_tab.start()

    slots = start_ref.shape[1]
    starts = start_ref[...].astype(jnp.float32)
    starts = jnp.concatenate(
        [starts, jnp.full((bands, LANES - slots), -1.0, jnp.float32)], axis=1
    )
    lane_row = lax.broadcasted_iota(jnp.int32, (1, LANES), 1)
    for d in range(bands):
        mk_out[d] = jnp.where(lane_row < count_ref[d], starts[d : d + 1], -1.0)
    for peer in other_bands:
        m_copy(peer, band).start()
    mk_in[band] = mk_out[band]

    get_tab.wait()

    def table(index, rows):
        first = offsets[index]
        return tab[first : first + rows, :]

    def wide(index, rows):
        first = offsets[index]
        return jnp.concatenate(
            [tab[first : first + rows, :], tab[first + rows : first + 2 * rows, :]], axis=1
        )

    def wide_row(index, at):
        first = offsets[index]
        return jnp.concatenate(
            [tab[pl.ds(first + at, 1), :], tab[pl.ds(first + RADIX + at, 1), :]], axis=1
        )

    paired = jnp.where(job == 0, 0.0, 1.0).astype(jnp.float32)
    alone = 1.0 - paired
    residues = (job, jnp.where(job == 0, RADIX // 2, RADIX - job))
    waves = []
    for c, residue in enumerate(residues):
        bc, bs = table(0, LEFT), table(1, LEFT)
        vc = tab[pl.ds(offsets[6] + residue, 1), :]
        vs = tab[pl.ds(offsets[7] + residue, 1), :]
        waves.append((bc * vc - bs * vs, bs * vc + bc * vs))
        bc, bs = wide(2, LEFT), wide(3, LEFT)
        vc, vs = wide_row(8, residue), wide_row(9, residue)
        t_cos[c] = bc * vc - bs * vs
        t_sin[c] = bs * vc + bc * vs
    (ca, sa), (cb, sb) = waves
    blocks = (
        (ca, paired * sa),
        (-sa, paired * ca),
        (paired * cb, alone * cb - paired * sb),
        (-paired * sb, -alone * sb - paired * cb),
    )
    for i, block in enumerate(blocks):
        high, low = split(jnp.concatenate(block, axis=1))
        w_hi[LEFT * i : LEFT * (i + 1), :] = high
        w_lo[LEFT * i : LEFT * (i + 1), :] = low
    gc, gs = wide(4, LEFT), wide(5, LEFT)
    for i, block in enumerate(((gc, gs), (-gs, gc))):
        high, low = split(jnp.concatenate(block, axis=1))
        g_hi[LEFT * i : LEFT * (i + 1), :] = high
        g_lo[LEFT * i : LEFT * (i + 1), :] = low

    own_x.wait()
    for i in range(1, shards):
        slot = lax.rem(me + shards - i, shards)
        x_copy(slot, slot).wait_recv()
    for row in range(2):
        for side in range(RIGHT // LANES):
            pick = pl.ds(2 * side + row, 8, stride=4)
            terms = radix_transform([x_in[t, pick, :] for t in range(shards)])
            lanes = slice(side * LANES, (side + 1) * LANES)
            for j in range(JOBS):
                re, im = (terms[0][0], terms[JOBS][0]) if j == 0 else terms[j]
                y_out[2 * j + row, 0, :, lanes] = re
                y_out[2 * j + row, 1, :, lanes] = im
    for peer in others:
        y_copy(peer, me).start()
    y_in[:, pl.ds(pl.multiple_of(me * 8, 8), 8), :] = y_out[me]

    for i in range(1, bands):
        slot = lax.rem(band + bands - i, bands)
        m_copy(slot, slot).wait_recv()
    lane = lax.broadcasted_iota(jnp.int32, (slots, LANES), 1)
    slot_id = lax.broadcasted_iota(jnp.int32, (slots, LANES), 0)
    for d in range(bands):
        spread_row = jnp.broadcast_to(mk_in[d], (slots, LANES))
        column = jnp.sum(jnp.where(lane == slot_id, spread_row, 0.0), axis=1, keepdims=True)
        mark_ref[d] = jnp.broadcast_to(column, (slots, LANES))

    for i in range(1, shards):
        slot = lax.rem(me + shards - i, shards)
        y_copy(slot, slot).wait_recv()

    y = jnp.concatenate([y_in[0], y_in[1]], axis=0)
    u = dot_split((w_hi[...], w_lo[...]), split(y), ((1,), (0,)))
    turned = []
    for c in range(2):
        ur, ui = u[2 * c * LEFT : (2 * c + 1) * LEFT], u[(2 * c + 1) * LEFT : (2 * c + 2) * LEFT]
        turned.append(
            jnp.concatenate(
                [ur * t_cos[c] + ui * t_sin[c], ui * t_cos[c] - ur * t_sin[c]], axis=1
            )
        )
    v = jnp.concatenate(turned, axis=0)
    z = dot_split((g_hi[...], g_lo[...]), split(v), ((1,), (1,)))
    zr, zi = z[:LEFT], z[LEFT:]
    power = (zr * zr + zi * zi) * (1.0 / total)
    pw[0] = power[:, :LEFT]
    pw[1] = power[:, LEFT:]

    groups = LEFT * LEFT // (HARM * LANES)
    lane = lax.broadcasted_iota(jnp.int32, (groups, LANES), 1)

    def decimate(which, harmonic, offset, cache):
        if (which, harmonic) not in cache:
            cache[which, harmonic] = [
                pw[which, pl.ds(b, groups, stride=harmonic), :] if harmonic > 1 else pw[which, pl.ds(0, groups), :]
                for b in range(harmonic)
            ]
        rows = cache[which, harmonic]
        if harmonic == 1:
            return rows[0]
        place = lane * harmonic + offset
        index, block = place & (LANES - 1), place >> 7
        out = jnp.take_along_axis(rows[0], index, axis=1, mode="promise_in_bounds")
        for b in range(1, harmonic):
            got = jnp.take_along_axis(rows[b], index, axis=1, mode="promise_in_bounds")
            out = jnp.where(block == b, got, out)
        return out

    for j in range(JOBS):

        @pl.when(job == j)
        def _(j=j):
            cache = {}
            found = picks(j)
            slot_count = HALF if j % 2 else len(SLOT_RESIDUES)
            for slot in range(slot_count):
                acc = None
                for which, harmonic, offset in found.get(slot, []):
                    got = decimate(which, harmonic, offset, cache)
                    acc = got if acc is None else acc + got
                if acc is None:
                    acc = jnp.zeros((groups, LANES), jnp.float32)
                h_out[:, slot, :] = acc

    odd = job % 2 == 1

    @pl.when(odd)
    def _():
        for peer in others:
            h_copy(peer, me, HALF).start()
        h_in[me, :HALF] = h_out[me, :HALF]

    @pl.when(jnp.logical_not(odd))
    def _():
        for peer in others:
            h_copy(peer, me, 2 * HALF).start()
        h_in[me] = h_out[me]

    count = 2 * LEFT * LEFT
    mean = jnp.sum(power, keepdims=True).reshape(1, 1) * (1.0 / count)
    away = power - mean
    squares = jnp.sum(away * away, keepdims=True).reshape(1, 1)
    st_out[0:1, :] = jnp.broadcast_to(mean, (1, LANES))
    st_out[1:2, :] = jnp.broadcast_to(squares, (1, LANES))
    for peer in others:
        s_copy(peer, me).start()
    st_in[me] = st_out[...]

    for v in range(shards):

        @pl.when(v != me)
        def _(v=v):
            h_copy(v, v, HALF if (v // 2) % 2 else 2 * HALF).wait_recv()
            s_copy(v, v).wait_recv()

    rows_out = []
    for row in range(2):
        sources = [2 * j + row for j in range(JOBS)]
        stats = [st_in[v] for v in sources]
        mean = sum(s[0:1] for s in stats) * (1.0 / JOBS)
        squares = sum(s[1:2] for s in stats)
        between = sum((s[0:1] - mean) * (s[0:1] - mean) for s in stats)
        spread = (squares + between * float(count)) * (1.0 / bins)
        scale = 1.0 / jnp.sqrt(spread + EPSILON)
        first = sum(h_in[v, :HALF, :] for v in sources)
        second = sum(h_in[v, HALF:, :] for v in sources if (v // 2) % 2 == 0)
        summed = jnp.concatenate([first, second], axis=0)
        rows_out.append((summed - float(HARM) * mean) * scale)

    both = jnp.concatenate(rows_out, axis=1)
    stacked = jnp.concatenate([p.astype(jnp.float32) for p in split_exactly(both)], axis=0).astype(jnp.bfloat16)
    places = stacked.shape[0]
    slot_at = lax.broadcasted_iota(jnp.int32, (places, LANES), 0) & (RADIX - 1)
    lane_at = lax.broadcasted_iota(jnp.int32, (places, LANES), 1) & (RADIX - 1)
    residue_of = jnp.where(
        slot_at < 8, 2 * slot_at + 1,
        jnp.where(slot_at < 12, 4 * slot_at - 30, jnp.where(slot_at < 14, 8 * slot_at - 92, jnp.where(slot_at == 14, 8, 0))),
    )
    chosen = (residue_of == lane_at).astype(jnp.float32).astype(jnp.bfloat16)
    laid = dot(stacked, chosen, ((0,), (0,)))
    at = lax.broadcasted_iota(jnp.int32, laid.shape, 0) & (LANES // RADIX - 1)
    lane = lax.broadcasted_iota(jnp.int32, laid.shape, 1) >> 4
    laid = jnp.where(at == lane, laid, 0.0)
    laid = jnp.sum(laid.reshape(2 * groups, LANES // RADIX, LANES), axis=1)
    top, low = laid[:groups], laid[groups:]
    pk_out[...] = jnp.maximum(top, low)
    for peer in other_bands:
        p_copy(peer, band).start()
    hsum_ref[pl.ds(0, groups, stride=2), :] = top
    hsum_ref[pl.ds(1, groups, stride=2), :] = low
    level = (top + low) * 0.5
    pk_in[band] = pk_out[...]
    for i in range(1, bands):
        slot = lax.rem(band + bands - i, bands)
        p_copy(slot, slot).wait_recv()
    for d in range(bands):
        diff_ref[d] = pk_in[d] - level

    for peer in others:
        x_copy(peer, me).wait_send()
        y_copy(peer, me).wait_send()
        s_copy(peer, me).wait_send()

    @pl.when(odd)
    def _():
        for peer in others:
            h_copy(peer, me, HALF).wait_send()

    @pl.when(jnp.logical_not(odd))
    def _():
        for peer in others:
            h_copy(peer, me, 2 * HALF).wait_send()

    for peer in other_bands:
        m_copy(peer, band).wait_send()
        p_copy(peer, band).wait_send()


def sift_kernel(bands, hsum_ref, diff_ref, mark_ref, out_h_ref, out_ref):
    out_h_ref[...] = hsum_ref[...]
    groups = diff_ref.shape[1]
    slots = mark_ref.shape[1]
    lane = lax.broadcasted_iota(jnp.int32, (slots, LANES), 1)
    for d in range(bands):
        mark = mark_ref[d].astype(jnp.int32)
        begin = jnp.maximum(mark, 0)
        row, shift = begin >> 7, begin & (LANES - 1)
        parts = [p.astype(jnp.float32) for p in split_exactly(diff_ref[d])]
        parts.append(jnp.zeros((LANES - 3 * groups, LANES), jnp.float32))
        source = jnp.concatenate(parts, axis=0).astype(jnp.bfloat16)
        live = lane < 3 * groups
        wanted = lane & (groups - 1)
        first = jnp.where(live & (wanted == row), 1.0, 0.0)
        second = jnp.where(live & (wanted == row + 1), 1.0, 0.0)
        choose = jnp.concatenate([first, second], axis=0).astype(jnp.bfloat16)
        pair = dot(choose, source, ((1,), (0,)))
        index = (lane + shift) & (LANES - 1)
        low = jnp.take_along_axis(pair[:slots], index, axis=1, mode="promise_in_bounds")
        high = jnp.take_along_axis(pair[slots:], index, axis=1, mode="promise_in_bounds")
        value = jnp.where(lane + shift < LANES, low, high)
        out_ref[d] = jnp.where(mark >= 0, value, 0.0)


def per_device(series, cand_start, cand_count):
    dm_rows, samples = series.shape
    shards, bands = lax.axis_size("tm"), lax.axis_size("dm")
    total = samples * shards
    slots = cand_start.shape[3]
    fundamentals = total // (2 * HARM) // shards
    assert shards == RADIX and dm_rows == 2 and samples == LEFT * RIGHT
    chunks = samples // LANES
    x = series.reshape(dm_rows, chunks, LANES).transpose(1, 0, 2).reshape(dm_rows * chunks, LANES)
    tab, offsets = tables(total)
    groups = fundamentals // LANES
    f32, bf16 = jnp.float32, jnp.bfloat16
    vmem = pl.BlockSpec(memory_space=pltpu.VMEM)
    hbm = pl.BlockSpec(memory_space=pl.ANY)
    dma = pltpu.SemaphoreType.DMA
    hsum, diff, mark = pl.pallas_call(
        functools.partial(search_kernel, shards, bands, tuple(offsets), total),
        name="search",
        out_shape=(
            jax.ShapeDtypeStruct((dm_rows * groups, LANES), f32),
            jax.ShapeDtypeStruct((bands, groups, LANES), f32),
            jax.ShapeDtypeStruct((bands, slots, LANES), f32),
        ),
        in_specs=[hbm, vmem, pl.BlockSpec(memory_space=pltpu.SMEM), hbm],
        out_specs=[vmem] * 3,
        scratch_shapes=[
            pltpu.VMEM(tab.shape, f32),
            pltpu.VMEM((shards, dm_rows * chunks // shards, LANES), f32),
            pltpu.VMEM((shards, 2, LEFT // shards, RIGHT), f32),
            pltpu.VMEM((2, LEFT, RIGHT), f32),
            pltpu.VMEM((4 * LEFT, 2 * LEFT), bf16),
            pltpu.VMEM((4 * LEFT, 2 * LEFT), bf16),
            pltpu.VMEM((2 * LEFT, 2 * RIGHT), bf16),
            pltpu.VMEM((2 * LEFT, 2 * RIGHT), bf16),
            pltpu.VMEM((2, LEFT, RIGHT), f32),
            pltpu.VMEM((2, LEFT, RIGHT), f32),
            pltpu.VMEM((2, LEFT, LEFT), f32),
            pltpu.VMEM((shards, 2 * HALF, LANES), f32),
            pltpu.VMEM((shards, 2 * HALF, LANES), f32),
            pltpu.VMEM((2, LANES), f32),
            pltpu.VMEM((shards, 2, LANES), f32),
            pltpu.VMEM((bands, 1, LANES), f32),
            pltpu.VMEM((bands, 1, LANES), f32),
            pltpu.VMEM((groups, LANES), f32),
            pltpu.VMEM((bands, groups, LANES), f32),
            *[dma((shards,)) for _ in range(8)],
            *[dma((bands,)) for _ in range(4)],
            dma((2,)),
        ],
        compiler_params=pltpu.CompilerParams(
            collective_id=0, has_side_effects=True, vmem_limit_bytes=32 << 20
        ),
    )(x, cand_start.reshape(bands, slots), cand_count.reshape(bands), jnp.asarray(tab))
    harmonic, sifted = pl.pallas_call(
        functools.partial(sift_kernel, bands),
        name="sift",
        out_shape=(
            jax.ShapeDtypeStruct(hsum.shape, f32),
            jax.ShapeDtypeStruct((bands, slots, BW), f32),
        ),
        in_specs=[vmem] * 3,
        out_specs=[vmem] * 2,
    )(hsum, diff, mark)
    harmonic = harmonic.reshape(groups, dm_rows, LANES).transpose(1, 0, 2)
    return harmonic.reshape(dm_rows, fundamentals), sifted[None, None]


def solution(mesh):
    return jax.shard_map(
        per_device,
        mesh=mesh,
        in_specs=(
            P(("beam", "dm"), "tm"),
            P(("beam", "tm"), "dm", None, None),
            P(("beam", "tm"), "dm", None),
        ),
        out_specs=(P(("beam", "dm"), "tm"), P(("beam", "tm"), "dm", None, None, None)),
        check_vma=False,
    )
```

```python
import functools
import math

import jax
import jax.numpy as jnp
import numpy as np
from jax import lax
from jax.experimental import pallas as pl
from jax.experimental.pallas import tpu as pltpu
from jax.sharding import PartitionSpec as P

HARM = 8
BW = 128
EPSILON = 1e-06
LANES = 128
RADIX = 16
JOBS = RADIX // 2
LEFT, RIGHT = 128, 256
MESH = pl.DeviceIdType.MESH
SLOT_RESIDUES = (1, 3, 5, 7, 9, 11, 13, 15, 2, 6, 10, 14, 4, 12, 8, 0)
HALF = JOBS


def tables(total):
    def wave(left, right, period):
        angle = 2.0 * math.pi * (np.outer(left, right) % period) / period
        return np.cos(angle), np.sin(angle)

    left, right, radix = np.arange(LEFT), np.arange(RIGHT), np.arange(RADIX)
    parts = [
        *wave(left, left, LEFT),
        *wave(left, right, LEFT * RIGHT),
        *wave(left, right, RIGHT),
        *wave(radix, left, RADIX * LEFT),
        *wave(radix, right, total),
    ]
    rows, offsets = [], []
    for part in parts:
        offsets.append(sum(r.shape[0] for r in rows))
        for lane in range(0, part.shape[1], LANES):
            rows.append(part[:, lane : lane + LANES])
    return np.concatenate(rows).astype(np.float32), offsets


def split(value):
    high = value.astype(jnp.bfloat16)
    return high, (value - high.astype(jnp.float32)).astype(jnp.bfloat16)


def split_exactly(value):
    high, rest = value.astype(jnp.bfloat16), None
    rest = value - high.astype(jnp.float32)
    middle = rest.astype(jnp.bfloat16)
    return high, middle, (rest - middle.astype(jnp.float32)).astype(jnp.bfloat16)


def dot(left, right, dims):
    return lax.dot_general(left, right, (dims, ((), ())), preferred_element_type=jnp.float32)


def dot_split(left, right, dims):
    (lh, ll), (rh, rl) = left, right
    return dot(lh, rh, dims) + (dot(ll, rh, dims) + dot(lh, rl, dims))


def radix_transform(x):
    half, quarter = RADIX // 2, RADIX // 4

    def real_transform(values, count):
        if count == 1:
            return [(values[0], None)]
        low = [values[i] + values[i + count // 2] for i in range(count // 2)]
        high = [values[i] - values[i + count // 2] for i in range(count // 2)]
        out = {2 * i: v for i, v in enumerate(real_transform(low, count // 2))}
        if count == 2:
            out[1] = (high[0], None)
        elif count == 4:
            out[1] = (high[0], -high[1])
        else:
            h, q = count // 2, count // 4
            minus = [None] + [high[i] - high[h - i] for i in range(1, q)]
            plus = [None] + [high[i] + high[h - i] for i in range(1, q)]
            for term in range(1, h, 2):
                re, im = high[0], high[q] * (-math.sin(2 * math.pi * q * term / count))
                for i in range(1, q):
                    re = re + minus[i] * math.cos(2 * math.pi * i * term / count)
                    im = im - plus[i] * math.sin(2 * math.pi * i * term / count)
                out[term] = (re, im)
        return [out[i] for i in range(count // 2 + 1)]

    return real_transform(x, RADIX)


def picks(job):
    pair = (0, RADIX // 2) if job == 0 else (job, RADIX - job)
    found = {}
    for slot, residue in enumerate(SLOT_RESIDUES):
        for harmonic in range(1, HARM + 1):
            product = harmonic * residue
            if product % RADIX in pair:
                found.setdefault(slot, []).append(
                    (pair.index(product % RADIX), harmonic, product // RADIX)
                )
    return found


def far_first(count):
    return sorted(range(1, count), key=lambda i: -min(i, count - i))


def sift(bands, groups, slots, differences, marks, out_ref):
    lane = lax.broadcasted_iota(jnp.int32, (slots, LANES), 1)
    live = lane < 3 * groups
    wanted = lane & (groups - 1)
    for d in range(bands):
        mark = marks[d]
        begin = jnp.maximum(mark, 0)
        row, shift = begin >> 7, begin & (LANES - 1)
        parts = [p.astype(jnp.float32) for p in split_exactly(differences[d])]
        parts.append(jnp.zeros((LANES - 3 * groups, LANES), jnp.float32))
        source = jnp.concatenate(parts, axis=0).astype(jnp.bfloat16)
        first = jnp.where(live & (wanted == row), 1.0, 0.0)
        second = jnp.where(live & (wanted == row + 1), 1.0, 0.0)
        choose = jnp.concatenate([first, second], axis=0).astype(jnp.bfloat16)
        pair = dot(choose, source, ((1,), (0,)))
        index = (lane + shift) & (LANES - 1)
        low = jnp.take_along_axis(pair[:slots], index, axis=1, mode="promise_in_bounds")
        high = jnp.take_along_axis(pair[slots:], index, axis=1, mode="promise_in_bounds")
        value = jnp.where(lane + shift < LANES, low, high)
        out_ref[d] = jnp.where(mark >= 0, value, 0.0)


def search_kernel(
    shards, bands, offsets, total,
    x_ref, start_hbm, count_hbm, tab_hbm,
    hsum_ref, out_ref,
    start_ref, count_ref, tab, x_in, y_out, y_in, w_hi, w_lo, g_hi, g_lo, t_cos, t_sin, pw,
    h_out, h_in, st_out, st_in, mk_out, mk_in, pk_out, pk_in,
    send_x, recv_x, send_y, recv_y, send_h, recv_h, send_s, recv_s,
    send_m, recv_m, send_p, recv_p, local_sem, here_shard, here_band,
):
    me = lax.axis_index("tm")
    band = lax.axis_index("dm")
    job, row_kept = me // 2, me % 2
    bins = total // 2
    x_rows = x_in.shape[1]

    first_shard, first_band = me == 0, band == 0
    barrier = pltpu.get_barrier_semaphore()
    others = [lax.rem(me + i, shards) for i in far_first(shards)]
    other_bands = [lax.rem(band + i, bands) for i in far_first(bands)]

    def greet(semaphore, axis, peers):
        for peer in peers:
            pl.semaphore_signal(semaphore, inc=1, device_id={axis: peer}, device_id_type=MESH)

    @pl.when(jnp.logical_not(first_shard))
    def _():
        greet(barrier, "tm", others)

    @pl.when(jnp.logical_not(first_band))
    def _():
        greet(barrier, "dm", other_bands)

    late = first_shard.astype(jnp.int32) + first_band.astype(jnp.int32)
    pl.semaphore_wait(barrier, shards + bands - 4 + late)

    @pl.when(first_shard)
    def _():
        greet(here_shard, "tm", others)

    def remote(src, dst, send, recv, axis, peer):
        return pltpu.make_async_remote_copy(
            src_ref=src, dst_ref=dst, send_sem=send, recv_sem=recv,
            device_id={axis: peer}, device_id_type=MESH,
        )

    def x_copy(peer, slot):
        rows = pl.ds(pl.multiple_of(peer * x_rows, x_rows), x_rows)
        return remote(x_ref.at[rows], x_in.at[slot], send_x.at[peer], recv_x.at[slot], "tm", peer)

    def y_copy(peer, slot):
        rows = pl.ds(pl.multiple_of(slot * 8, 8), 8)
        return remote(y_out.at[peer], y_in.at[:, rows], send_y.at[peer], recv_y.at[slot], "tm", peer)

    def h_copy(peer, slot, rows):
        part = pl.ds(0, rows)
        return remote(
            h_out.at[peer, part], h_in.at[slot, part], send_h.at[peer], recv_h.at[slot], "tm", peer
        )

    def s_copy(peer, slot):
        return remote(st_out, st_in.at[slot], send_s.at[peer], recv_s.at[slot], "tm", peer)

    def m_copy(peer, slot):
        return remote(mk_out.at[peer], mk_in.at[slot], send_m.at[peer], recv_m.at[slot], "dm", peer)

    def p_copy(peer, slot):
        return remote(pk_out, pk_in.at[slot], send_p.at[peer], recv_p.at[slot], "dm", peer)

    for peer in others:

        @pl.when(peer != 0)
        def _(peer=peer):
            x_copy(peer, me).start()

    own_rows = pl.ds(pl.multiple_of(me * x_rows, x_rows), x_rows)
    own_x = pltpu.make_async_copy(x_ref.at[own_rows], x_in.at[me], local_sem.at[0])
    own_x.start()
    get_starts = pltpu.make_async_copy(start_hbm, start_ref, local_sem.at[1])
    get_starts.start()
    get_counts = pltpu.make_async_copy(count_hbm, count_ref, local_sem.at[2])
    get_counts.start()
    get_tab = pltpu.make_async_copy(tab_hbm, tab, local_sem.at[3])
    get_tab.start()

    @pl.when(first_band)
    def _():
        greet(here_band, "dm", other_bands)

    @pl.when(jnp.logical_not(first_shard))
    def _():
        pl.semaphore_wait(here_shard, 1)
        x_copy(0, me).start()

    slots = start_ref.shape[1]
    get_starts.wait()
    get_counts.wait()
    starts = start_ref[...].astype(jnp.float32)
    starts = jnp.concatenate(
        [starts, jnp.full((bands, LANES - slots), -1.0, jnp.float32)], axis=1
    )
    lane_row = lax.broadcasted_iota(jnp.int32, (1, LANES), 1)
    for d in range(bands):
        mk_out[d] = jnp.where(lane_row < count_ref[d], starts[d : d + 1], -1.0)
    for peer in other_bands:

        @pl.when(peer != 0)
        def _(peer=peer):
            m_copy(peer, band).start()

    mk_in[band] = mk_out[band]

    get_tab.wait()

    def table(index, rows):
        first = offsets[index]
        return tab[first : first + rows, :]

    def wide(index, rows):
        first = offsets[index]
        return jnp.concatenate(
            [tab[first : first + rows, :], tab[first + rows : first + 2 * rows, :]], axis=1
        )

    def wide_row(index, at):
        first = offsets[index]
        return jnp.concatenate(
            [tab[pl.ds(first + at, 1), :], tab[pl.ds(first + RADIX + at, 1), :]], axis=1
        )

    paired = jnp.where(job == 0, 0.0, 1.0).astype(jnp.float32)
    alone = 1.0 - paired
    residues = (job, jnp.where(job == 0, RADIX // 2, RADIX - job))
    waves = []
    for c, residue in enumerate(residues):
        bc, bs = table(0, LEFT), table(1, LEFT)
        vc = tab[pl.ds(offsets[6] + residue, 1), :]
        vs = tab[pl.ds(offsets[7] + residue, 1), :]
        waves.append((bc * vc - bs * vs, bs * vc + bc * vs))
        bc, bs = wide(2, LEFT), wide(3, LEFT)
        vc, vs = wide_row(8, residue), wide_row(9, residue)
        t_cos[c] = bc * vc - bs * vs
        t_sin[c] = bs * vc + bc * vs
    (ca, sa), (cb, sb) = waves
    blocks = (
        (ca, paired * sa),
        (-sa, paired * ca),
        (paired * cb, alone * cb - paired * sb),
        (-paired * sb, -alone * sb - paired * cb),
    )
    for i, block in enumerate(blocks):
        high, low = split(jnp.concatenate(block, axis=1))
        w_hi[LEFT * i : LEFT * (i + 1), :] = high
        w_lo[LEFT * i : LEFT * (i + 1), :] = low
    gc, gs = wide(4, LEFT), wide(5, LEFT)
    for i, block in enumerate(((gc, gs), (-gs, gc))):
        high, low = split(jnp.concatenate(block, axis=1))
        g_hi[LEFT * i : LEFT * (i + 1), :] = high
        g_lo[LEFT * i : LEFT * (i + 1), :] = low

    own_x.wait()
    for i in range(1, shards):
        slot = lax.rem(me + shards - i, shards)
        x_copy(slot, slot).wait_recv()
    for row in range(2):
        for side in range(RIGHT // LANES):
            pick = pl.ds(2 * side + row, 8, stride=4)
            terms = radix_transform([x_in[t, pick, :] for t in range(shards)])
            lanes = slice(side * LANES, (side + 1) * LANES)
            for j in range(JOBS):
                re, im = (terms[0][0], terms[JOBS][0]) if j == 0 else terms[j]
                y_out[2 * j + row, 0, :, lanes] = re
                y_out[2 * j + row, 1, :, lanes] = im
    for peer in others:
        y_copy(peer, me).start()
    y_in[:, pl.ds(pl.multiple_of(me * 8, 8), 8), :] = y_out[me]

    @pl.when(jnp.logical_not(first_band))
    def _():
        pl.semaphore_wait(here_band, 1)
        m_copy(0, band).start()

    for i in range(1, shards):
        slot = lax.rem(me + shards - i, shards)
        y_copy(slot, slot).wait_recv()

    y = jnp.concatenate([y_in[0], y_in[1]], axis=0)
    u = dot_split((w_hi[...], w_lo[...]), split(y), ((1,), (0,)))
    turned = []
    for c in range(2):
        ur, ui = u[2 * c * LEFT : (2 * c + 1) * LEFT], u[(2 * c + 1) * LEFT : (2 * c + 2) * LEFT]
        turned.append(
            jnp.concatenate(
                [ur * t_cos[c] + ui * t_sin[c], ui * t_cos[c] - ur * t_sin[c]], axis=1
            )
        )
    v = jnp.concatenate(turned, axis=0)
    z = dot_split((g_hi[...], g_lo[...]), split(v), ((1,), (1,)))
    zr, zi = z[:LEFT], z[LEFT:]
    power = (zr * zr + zi * zi) * (1.0 / total)
    pw[0] = power[:, :LEFT]
    pw[1] = power[:, LEFT:]

    groups = LEFT * LEFT // (HARM * LANES)
    lane = lax.broadcasted_iota(jnp.int32, (groups, LANES), 1)

    def decimate(which, harmonic, offset, cache):
        if (which, harmonic) not in cache:
            cache[which, harmonic] = [
                pw[which, pl.ds(b, groups, stride=harmonic), :] if harmonic > 1 else pw[which, pl.ds(0, groups), :]
                for b in range(harmonic)
            ]
        rows = cache[which, harmonic]
        if harmonic == 1:
            return rows[0]
        place = lane * harmonic + offset
        index, block = place & (LANES - 1), place >> 7
        out = jnp.take_along_axis(rows[0], index, axis=1, mode="promise_in_bounds")
        for b in range(1, harmonic):
            got = jnp.take_along_axis(rows[b], index, axis=1, mode="promise_in_bounds")
            out = jnp.where(block == b, got, out)
        return out

    for j in range(JOBS):

        @pl.when(job == j)
        def _(j=j):
            cache = {}
            found = picks(j)
            slot_count = HALF if j % 2 else len(SLOT_RESIDUES)
            for slot in range(slot_count):
                acc = None
                for which, harmonic, offset in found.get(slot, []):
                    got = decimate(which, harmonic, offset, cache)
                    acc = got if acc is None else acc + got
                if acc is None:
                    acc = jnp.zeros((groups, LANES), jnp.float32)
                h_out[:, slot, :] = acc

    odd = job % 2 == 1

    @pl.when(odd)
    def _():
        for peer in others:
            h_copy(peer, me, HALF).start()
        h_in[me, :HALF] = h_out[me, :HALF]

    @pl.when(jnp.logical_not(odd))
    def _():
        for peer in others:
            h_copy(peer, me, 2 * HALF).start()
        h_in[me] = h_out[me]

    count = 2 * LEFT * LEFT
    mean = jnp.sum(power, keepdims=True).reshape(1, 1) * (1.0 / count)
    away = power - mean
    squares = jnp.sum(away * away, keepdims=True).reshape(1, 1)
    st_out[0:1, :] = jnp.broadcast_to(mean, (1, LANES))
    st_out[1:2, :] = jnp.broadcast_to(squares, (1, LANES))
    for peer in others:
        s_copy(peer, me).start()
    st_in[me] = st_out[...]

    for v in range(shards):

        @pl.when(v != me)
        def _(v=v):
            h_copy(v, v, HALF if (v // 2) % 2 else 2 * HALF).wait_recv()
            s_copy(v, v).wait_recv()

    rows_out = []
    for row in range(2):
        sources = [2 * j + row for j in range(JOBS)]
        stats = [st_in[v] for v in sources]
        mean = sum(s[0:1] for s in stats) * (1.0 / JOBS)
        squares = sum(s[1:2] for s in stats)
        between = sum((s[0:1] - mean) * (s[0:1] - mean) for s in stats)
        spread = (squares + between * float(count)) * (1.0 / bins)
        scale = 1.0 / jnp.sqrt(spread + EPSILON)
        first = sum(h_in[v, :HALF, :] for v in sources)
        second = sum(h_in[v, HALF:, :] for v in sources if (v // 2) % 2 == 0)
        summed = jnp.concatenate([first, second], axis=0)
        rows_out.append((summed - float(HARM) * mean) * scale)

    both = jnp.concatenate(rows_out, axis=1)
    stacked = jnp.concatenate([p.astype(jnp.float32) for p in split_exactly(both)], axis=0).astype(jnp.bfloat16)
    places = stacked.shape[0]
    slot_at = lax.broadcasted_iota(jnp.int32, (places, LANES), 0) & (RADIX - 1)
    lane_at = lax.broadcasted_iota(jnp.int32, (places, LANES), 1) & (RADIX - 1)
    residue_of = jnp.where(
        slot_at < 8, 2 * slot_at + 1,
        jnp.where(slot_at < 12, 4 * slot_at - 30, jnp.where(slot_at < 14, 8 * slot_at - 92, jnp.where(slot_at == 14, 8, 0))),
    )
    chosen = (residue_of == lane_at).astype(jnp.float32).astype(jnp.bfloat16)
    laid = dot(stacked, chosen, ((0,), (0,)))
    at = lax.broadcasted_iota(jnp.int32, laid.shape, 0) & (LANES // RADIX - 1)
    lane = lax.broadcasted_iota(jnp.int32, laid.shape, 1) >> 4
    laid = jnp.where(at == lane, laid, 0.0)
    laid = jnp.sum(laid.reshape(2 * groups, LANES // RADIX, LANES), axis=1)
    top, low = laid[:groups], laid[groups:]
    pk_out[...] = jnp.maximum(top, low)
    for peer in other_bands:
        p_copy(peer, band).start()
    hsum_ref[pl.ds(0, groups, stride=2), :] = top
    hsum_ref[pl.ds(1, groups, stride=2), :] = low
    level = (top + low) * 0.5
    pk_in[band] = pk_out[...]

    for i in range(1, bands):
        slot = lax.rem(band + bands - i, bands)
        m_copy(slot, slot).wait_recv()
    lane = lax.broadcasted_iota(jnp.int32, (slots, LANES), 1)
    slot_id = lax.broadcasted_iota(jnp.int32, (slots, LANES), 0)
    marks = []
    for d in range(bands):
        spread_row = jnp.broadcast_to(mk_in[d], (slots, LANES))
        column = jnp.sum(jnp.where(lane == slot_id, spread_row, 0.0), axis=1, keepdims=True)
        marks.append(jnp.broadcast_to(column, (slots, LANES)).astype(jnp.int32))

    for i in range(1, bands):
        slot = lax.rem(band + bands - i, bands)
        p_copy(slot, slot).wait_recv()
    sift(bands, groups, slots, [pk_in[d] - level for d in range(bands)], marks, out_ref)

    for peer in others:
        x_copy(peer, me).wait_send()
        y_copy(peer, me).wait_send()
        s_copy(peer, me).wait_send()

    @pl.when(odd)
    def _():
        for peer in others:
            h_copy(peer, me, HALF).wait_send()

    @pl.when(jnp.logical_not(odd))
    def _():
        for peer in others:
            h_copy(peer, me, 2 * HALF).wait_send()

    for peer in other_bands:
        m_copy(peer, band).wait_send()
        p_copy(peer, band).wait_send()


def per_device(series, cand_start, cand_count):
    dm_rows, samples = series.shape
    shards, bands = lax.axis_size("tm"), lax.axis_size("dm")
    total = samples * shards
    slots = cand_start.shape[3]
    fundamentals = total // (2 * HARM) // shards
    assert shards == RADIX and dm_rows == 2 and samples == LEFT * RIGHT
    chunks = samples // LANES
    x = series.reshape(dm_rows, chunks, LANES).transpose(1, 0, 2).reshape(dm_rows * chunks, LANES)
    tab, offsets = tables(total)
    groups = fundamentals // LANES
    f32, bf16 = jnp.float32, jnp.bfloat16
    vmem = pl.BlockSpec(memory_space=pltpu.VMEM)
    hbm = pl.BlockSpec(memory_space=pl.ANY)
    dma = pltpu.SemaphoreType.DMA
    hsum, sifted = pl.pallas_call(
        functools.partial(search_kernel, shards, bands, tuple(offsets), total),
        name="search",
        out_shape=(
            jax.ShapeDtypeStruct((dm_rows * groups, LANES), f32),
            jax.ShapeDtypeStruct((bands, slots, BW), f32),
        ),
        in_specs=[hbm] * 4,
        out_specs=[vmem] * 2,
        scratch_shapes=[
            pltpu.VMEM((bands, slots), jnp.int32),
            pltpu.SMEM((bands,), jnp.int32),
            pltpu.VMEM(tab.shape, f32),
            pltpu.VMEM((shards, dm_rows * chunks // shards, LANES), f32),
            pltpu.VMEM((shards, 2, LEFT // shards, RIGHT), f32),
            pltpu.VMEM((2, LEFT, RIGHT), f32),
            pltpu.VMEM((4 * LEFT, 2 * LEFT), bf16),
            pltpu.VMEM((4 * LEFT, 2 * LEFT), bf16),
            pltpu.VMEM((2 * LEFT, 2 * RIGHT), bf16),
            pltpu.VMEM((2 * LEFT, 2 * RIGHT), bf16),
            pltpu.VMEM((2, LEFT, RIGHT), f32),
            pltpu.VMEM((2, LEFT, RIGHT), f32),
            pltpu.VMEM((2, LEFT, LEFT), f32),
            pltpu.VMEM((shards, 2 * HALF, LANES), f32),
            pltpu.VMEM((shards, 2 * HALF, LANES), f32),
            pltpu.VMEM((2, LANES), f32),
            pltpu.VMEM((shards, 2, LANES), f32),
            pltpu.VMEM((bands, 1, LANES), f32),
            pltpu.VMEM((bands, 1, LANES), f32),
            pltpu.VMEM((groups, LANES), f32),
            pltpu.VMEM((bands, groups, LANES), f32),
            *[dma((shards,)) for _ in range(8)],
            *[dma((bands,)) for _ in range(4)],
            dma((4,)),
            pltpu.SemaphoreType.REGULAR,
            pltpu.SemaphoreType.REGULAR,
        ],
        compiler_params=pltpu.CompilerParams(
            collective_id=0, has_side_effects=True, vmem_limit_bytes=60 << 20
        ),
    )(x, cand_start.reshape(bands, slots), cand_count.reshape(bands), jnp.asarray(tab))
    harmonic = hsum.reshape(groups, dm_rows, LANES).transpose(1, 0, 2)
    return harmonic.reshape(dm_rows, fundamentals), sifted[None, None]


def solution(mesh):
    return jax.shard_map(
        per_device,
        mesh=mesh,
        in_specs=(
            P(("beam", "dm"), "tm"),
            P(("beam", "tm"), "dm", None, None),
            P(("beam", "tm"), "dm", None),
        ),
        out_specs=(P(("beam", "dm"), "tm"), P(("beam", "tm"), "dm", None, None, None)),
        check_vma=False,
    )
```

```python
import functools
import math

import jax
import jax.numpy as jnp
import numpy as np
from jax import lax
from jax.experimental import pallas as pl
from jax.experimental.pallas import tpu as pltpu
from jax.sharding import PartitionSpec as P

HARM = 8
BW = 128
EPSILON = 1e-06
LANES = 128
RADIX = 16
JOBS = RADIX // 2
LEFT, RIGHT = 128, 256
MESH = pl.DeviceIdType.MESH
SLOT_RESIDUES = (1, 3, 5, 7, 9, 11, 13, 15, 2, 6, 10, 14, 4, 12, 8, 0)
HALF = JOBS


def tables(total):
    def wave(left, right, period):
        angle = 2.0 * math.pi * (np.outer(left, right) % period) / period
        return np.cos(angle), np.sin(angle)

    left, right, radix = np.arange(LEFT), np.arange(RIGHT), np.arange(RADIX)
    parts = [
        *wave(left, left, LEFT),
        *wave(left, right, LEFT * RIGHT),
        *wave(left, right, RIGHT),
        *wave(radix, left, RADIX * LEFT),
        *wave(radix, right, total),
    ]
    rows, offsets = [], []
    for part in parts:
        offsets.append(sum(r.shape[0] for r in rows))
        for lane in range(0, part.shape[1], LANES):
            rows.append(part[:, lane : lane + LANES])
    return np.concatenate(rows).astype(np.float32), offsets


def split(value):
    high = value.astype(jnp.bfloat16)
    return high, (value - high.astype(jnp.float32)).astype(jnp.bfloat16)


def split_exactly(value):
    high, rest = value.astype(jnp.bfloat16), None
    rest = value - high.astype(jnp.float32)
    middle = rest.astype(jnp.bfloat16)
    return high, middle, (rest - middle.astype(jnp.float32)).astype(jnp.bfloat16)


def dot(left, right, dims):
    return lax.dot_general(left, right, (dims, ((), ())), preferred_element_type=jnp.float32)


def dot_split(left, right, dims):
    (lh, ll), (rh, rl) = left, right
    return dot(lh, rh, dims) + (dot(ll, rh, dims) + dot(lh, rl, dims))


def radix_transform(x):
    half, quarter = RADIX // 2, RADIX // 4

    def real_transform(values, count):
        if count == 1:
            return [(values[0], None)]
        low = [values[i] + values[i + count // 2] for i in range(count // 2)]
        high = [values[i] - values[i + count // 2] for i in range(count // 2)]
        out = {2 * i: v for i, v in enumerate(real_transform(low, count // 2))}
        if count == 2:
            out[1] = (high[0], None)
        elif count == 4:
            out[1] = (high[0], -high[1])
        else:
            h, q = count // 2, count // 4
            minus = [None] + [high[i] - high[h - i] for i in range(1, q)]
            plus = [None] + [high[i] + high[h - i] for i in range(1, q)]
            for term in range(1, h, 2):
                re, im = high[0], high[q] * (-math.sin(2 * math.pi * q * term / count))
                for i in range(1, q):
                    re = re + minus[i] * math.cos(2 * math.pi * i * term / count)
                    im = im - plus[i] * math.sin(2 * math.pi * i * term / count)
                out[term] = (re, im)
        return [out[i] for i in range(count // 2 + 1)]

    return real_transform(x, RADIX)


def picks(job):
    pair = (0, RADIX // 2) if job == 0 else (job, RADIX - job)
    found = {}
    for slot, residue in enumerate(SLOT_RESIDUES):
        for harmonic in range(1, HARM + 1):
            product = harmonic * residue
            if product % RADIX in pair:
                found.setdefault(slot, []).append(
                    (pair.index(product % RADIX), harmonic, product // RADIX)
                )
    return found


def far_first(count):
    return sorted(range(1, count), key=lambda i: -min(i, count - i))


def sift(bands, groups, slots, differences, marks, out_ref):
    lane = lax.broadcasted_iota(jnp.int32, (slots, LANES), 1)
    live = lane < 3 * groups
    wanted = lane & (groups - 1)
    for d in range(bands):
        mark = marks[d]
        begin = jnp.maximum(mark, 0)
        row, shift = begin >> 7, begin & (LANES - 1)
        parts = [p.astype(jnp.float32) for p in split_exactly(differences[d])]
        parts.append(jnp.zeros((LANES - 3 * groups, LANES), jnp.float32))
        source = jnp.concatenate(parts, axis=0).astype(jnp.bfloat16)
        first = jnp.where(live & (wanted == row), 1.0, 0.0)
        second = jnp.where(live & (wanted == row + 1), 1.0, 0.0)
        choose = jnp.concatenate([first, second], axis=0).astype(jnp.bfloat16)
        pair = dot(choose, source, ((1,), (0,)))
        index = (lane + shift) & (LANES - 1)
        low = jnp.take_along_axis(pair[:slots], index, axis=1, mode="promise_in_bounds")
        high = jnp.take_along_axis(pair[slots:], index, axis=1, mode="promise_in_bounds")
        value = jnp.where(lane + shift < LANES, low, high)
        out_ref[d] = jnp.where(mark >= 0, value, 0.0)


def search_kernel(
    shards, bands, offsets, total,
    x_ref, start_hbm, count_hbm, tab_hbm,
    hsum_ref, out_ref,
    start_ref, count_ref, tab, x_in, y_out, y_in, w_hi, w_lo, g_hi, g_lo, t_cos, t_sin, pw,
    h_out, h_in, st_out, st_in, mk_out, mk_in, pk_out, pk_in,
    send_x, recv_x, send_y, recv_y, send_h, recv_h, send_s, recv_s,
    send_m, recv_m, send_p, recv_p, local_sem, here_shard, here_band,
):
    me = lax.axis_index("tm")
    band = lax.axis_index("dm")
    job, row_kept = me // 2, me % 2
    bins = total // 2
    x_rows = x_in.shape[1]

    barrier = pltpu.get_barrier_semaphore()
    others = [lax.rem(me + i, shards) for i in far_first(shards)]
    other_bands = [lax.rem(band + i, bands) for i in far_first(bands)]

    def rank(index, count):
        return jnp.where(index == 0, count, index)

    my_rank, band_rank = rank(me, shards), rank(band, bands)

    def greet(semaphore, axis, peer, wanted):
        @pl.when(wanted)
        def _():
            pl.semaphore_signal(semaphore, inc=1, device_id={axis: peer}, device_id_type=MESH)

    for peer in others:
        greet(barrier, "tm", peer, rank(peer, shards) > my_rank)
    for peer in other_bands:
        greet(barrier, "dm", peer, rank(peer, bands) > band_rank)
    lowers = my_rank + band_rank - 2

    @pl.when(lowers > 0)
    def _():
        pl.semaphore_wait(barrier, lowers)

    for peer in others:
        greet(here_shard.at[me], "tm", peer, rank(peer, shards) < my_rank)

    def remote(src, dst, send, recv, axis, peer):
        return pltpu.make_async_remote_copy(
            src_ref=src, dst_ref=dst, send_sem=send, recv_sem=recv,
            device_id={axis: peer}, device_id_type=MESH,
        )

    def x_copy(peer, slot):
        rows = pl.ds(pl.multiple_of(peer * x_rows, x_rows), x_rows)
        return remote(x_ref.at[rows], x_in.at[slot], send_x.at[peer], recv_x.at[slot], "tm", peer)

    def y_copy(peer, slot):
        rows = pl.ds(pl.multiple_of(slot * 8, 8), 8)
        return remote(y_out.at[peer], y_in.at[:, rows], send_y.at[peer], recv_y.at[slot], "tm", peer)

    def h_copy(peer, slot, rows):
        part = pl.ds(0, rows)
        return remote(
            h_out.at[peer, part], h_in.at[slot, part], send_h.at[peer], recv_h.at[slot], "tm", peer
        )

    def s_copy(peer, slot):
        return remote(st_out, st_in.at[slot], send_s.at[peer], recv_s.at[slot], "tm", peer)

    def m_copy(peer, slot):
        return remote(mk_out.at[peer], mk_in.at[slot], send_m.at[peer], recv_m.at[slot], "dm", peer)

    def p_copy(peer, slot):
        return remote(pk_out, pk_in.at[slot], send_p.at[peer], recv_p.at[slot], "dm", peer)

    for peer in others:

        @pl.when(rank(peer, shards) < my_rank)
        def _(peer=peer):
            x_copy(peer, me).start()

    own_rows = pl.ds(pl.multiple_of(me * x_rows, x_rows), x_rows)
    own_x = pltpu.make_async_copy(x_ref.at[own_rows], x_in.at[me], local_sem.at[0])
    own_x.start()
    get_starts = pltpu.make_async_copy(start_hbm, start_ref, local_sem.at[1])
    get_starts.start()
    get_counts = pltpu.make_async_copy(count_hbm, count_ref, local_sem.at[2])
    get_counts.start()
    get_tab = pltpu.make_async_copy(tab_hbm, tab, local_sem.at[3])
    get_tab.start()

    for peer in other_bands:
        greet(here_band.at[band], "dm", peer, rank(peer, bands) < band_rank)
    for i in range(1, shards):
        peer = lax.rem(me + i, shards)

        @pl.when(rank(peer, shards) > my_rank)
        def _(peer=peer):
            pl.semaphore_wait(here_shard.at[peer], 1)
            x_copy(peer, me).start()

    slots = start_ref.shape[1]
    get_starts.wait()
    get_counts.wait()
    starts = start_ref[...].astype(jnp.float32)
    starts = jnp.concatenate(
        [starts, jnp.full((bands, LANES - slots), -1.0, jnp.float32)], axis=1
    )
    lane_row = lax.broadcasted_iota(jnp.int32, (1, LANES), 1)
    for d in range(bands):
        mk_out[d] = jnp.where(lane_row < count_ref[d], starts[d : d + 1], -1.0)
    mk_in[band] = mk_out[band]

    get_tab.wait()

    def table(index, rows):
        first = offsets[index]
        return tab[first : first + rows, :]

    def wide(index, rows):
        first = offsets[index]
        return jnp.concatenate(
            [tab[first : first + rows, :], tab[first + rows : first + 2 * rows, :]], axis=1
        )

    def wide_row(index, at):
        first = offsets[index]
        return jnp.concatenate(
            [tab[pl.ds(first + at, 1), :], tab[pl.ds(first + RADIX + at, 1), :]], axis=1
        )

    paired = jnp.where(job == 0, 0.0, 1.0).astype(jnp.float32)
    alone = 1.0 - paired
    residues = (job, jnp.where(job == 0, RADIX // 2, RADIX - job))
    waves = []
    for c, residue in enumerate(residues):
        bc, bs = table(0, LEFT), table(1, LEFT)
        vc = tab[pl.ds(offsets[6] + residue, 1), :]
        vs = tab[pl.ds(offsets[7] + residue, 1), :]
        waves.append((bc * vc - bs * vs, bs * vc + bc * vs))
        bc, bs = wide(2, LEFT), wide(3, LEFT)
        vc, vs = wide_row(8, residue), wide_row(9, residue)
        t_cos[c] = bc * vc - bs * vs
        t_sin[c] = bs * vc + bc * vs
    (ca, sa), (cb, sb) = waves
    blocks = (
        (ca, paired * sa),
        (-sa, paired * ca),
        (paired * cb, alone * cb - paired * sb),
        (-paired * sb, -alone * sb - paired * cb),
    )
    for i, block in enumerate(blocks):
        high, low = split(jnp.concatenate(block, axis=1))
        w_hi[LEFT * i : LEFT * (i + 1), :] = high
        w_lo[LEFT * i : LEFT * (i + 1), :] = low
    gc, gs = wide(4, LEFT), wide(5, LEFT)
    for i, block in enumerate(((gc, gs), (-gs, gc))):
        high, low = split(jnp.concatenate(block, axis=1))
        g_hi[LEFT * i : LEFT * (i + 1), :] = high
        g_lo[LEFT * i : LEFT * (i + 1), :] = low

    own_x.wait()
    for i in range(1, shards):
        slot = lax.rem(me + shards - i, shards)
        x_copy(slot, slot).wait_recv()
    for row in range(2):
        for side in range(RIGHT // LANES):
            pick = pl.ds(2 * side + row, 8, stride=4)
            terms = radix_transform([x_in[t, pick, :] for t in range(shards)])
            lanes = slice(side * LANES, (side + 1) * LANES)
            for j in range(JOBS):
                re, im = (terms[0][0], terms[JOBS][0]) if j == 0 else terms[j]
                y_out[2 * j + row, 0, :, lanes] = re
                y_out[2 * j + row, 1, :, lanes] = im
    for peer in others:
        y_copy(peer, me).start()
    y_in[:, pl.ds(pl.multiple_of(me * 8, 8), 8), :] = y_out[me]

    for i in range(1, shards):
        slot = lax.rem(me + shards - i, shards)
        y_copy(slot, slot).wait_recv()

    y = jnp.concatenate([y_in[0], y_in[1]], axis=0)
    u = dot_split((w_hi[...], w_lo[...]), split(y), ((1,), (0,)))
    turned = []
    for c in range(2):
        ur, ui = u[2 * c * LEFT : (2 * c + 1) * LEFT], u[(2 * c + 1) * LEFT : (2 * c + 2) * LEFT]
        turned.append(
            jnp.concatenate(
                [ur * t_cos[c] + ui * t_sin[c], ui * t_cos[c] - ur * t_sin[c]], axis=1
            )
        )
    v = jnp.concatenate(turned, axis=0)
    z = dot_split((g_hi[...], g_lo[...]), split(v), ((1,), (1,)))
    zr, zi = z[:LEFT], z[LEFT:]
    power = (zr * zr + zi * zi) * (1.0 / total)
    pw[0] = power[:, :LEFT]
    pw[1] = power[:, LEFT:]

    groups = LEFT * LEFT // (HARM * LANES)
    lane = lax.broadcasted_iota(jnp.int32, (groups, LANES), 1)

    def decimate(which, harmonic, offset, cache):
        if (which, harmonic) not in cache:
            cache[which, harmonic] = [
                pw[which, pl.ds(b, groups, stride=harmonic), :] if harmonic > 1 else pw[which, pl.ds(0, groups), :]
                for b in range(harmonic)
            ]
        rows = cache[which, harmonic]
        if harmonic == 1:
            return rows[0]
        place = lane * harmonic + offset
        index, block = place & (LANES - 1), place >> 7
        out = jnp.take_along_axis(rows[0], index, axis=1, mode="promise_in_bounds")
        for b in range(1, harmonic):
            got = jnp.take_along_axis(rows[b], index, axis=1, mode="promise_in_bounds")
            out = jnp.where(block == b, got, out)
        return out

    for j in range(JOBS):

        @pl.when(job == j)
        def _(j=j):
            cache = {}
            found = picks(j)
            slot_count = HALF if j % 2 else len(SLOT_RESIDUES)
            for slot in range(slot_count):
                acc = None
                for which, harmonic, offset in found.get(slot, []):
                    got = decimate(which, harmonic, offset, cache)
                    acc = got if acc is None else acc + got
                if acc is None:
                    acc = jnp.zeros((groups, LANES), jnp.float32)
                h_out[:, slot, :] = acc

    odd = job % 2 == 1

    @pl.when(odd)
    def _():
        for peer in others:
            h_copy(peer, me, HALF).start()
        h_in[me, :HALF] = h_out[me, :HALF]

    @pl.when(jnp.logical_not(odd))
    def _():
        for peer in others:
            h_copy(peer, me, 2 * HALF).start()
        h_in[me] = h_out[me]

    count = 2 * LEFT * LEFT
    mean = jnp.sum(power, keepdims=True).reshape(1, 1) * (1.0 / count)
    away = power - mean
    squares = jnp.sum(away * away, keepdims=True).reshape(1, 1)
    st_out[0:1, :] = jnp.broadcast_to(mean, (1, LANES))
    st_out[1:2, :] = jnp.broadcast_to(squares, (1, LANES))
    for peer in others:
        s_copy(peer, me).start()
    st_in[me] = st_out[...]

    for peer in other_bands:

        @pl.when(rank(peer, bands) > band_rank)
        def _(peer=peer):
            pl.semaphore_wait(here_band.at[peer], 1)

        m_copy(peer, band).start()

    for v in range(shards):

        @pl.when(v != me)
        def _(v=v):
            h_copy(v, v, HALF if (v // 2) % 2 else 2 * HALF).wait_recv()
            s_copy(v, v).wait_recv()

    rows_out = []
    for row in range(2):
        sources = [2 * j + row for j in range(JOBS)]
        stats = [st_in[v] for v in sources]
        mean = sum(s[0:1] for s in stats) * (1.0 / JOBS)
        squares = sum(s[1:2] for s in stats)
        between = sum((s[0:1] - mean) * (s[0:1] - mean) for s in stats)
        spread = (squares + between * float(count)) * (1.0 / bins)
        scale = 1.0 / jnp.sqrt(spread + EPSILON)
        first = sum(h_in[v, :HALF, :] for v in sources)
        second = sum(h_in[v, HALF:, :] for v in sources if (v // 2) % 2 == 0)
        summed = jnp.concatenate([first, second], axis=0)
        rows_out.append((summed - float(HARM) * mean) * scale)

    both = jnp.concatenate(rows_out, axis=1)
    stacked = jnp.concatenate([p.astype(jnp.float32) for p in split_exactly(both)], axis=0).astype(jnp.bfloat16)
    places = stacked.shape[0]
    slot_at = lax.broadcasted_iota(jnp.int32, (places, LANES), 0) & (RADIX - 1)
    lane_at = lax.broadcasted_iota(jnp.int32, (places, LANES), 1) & (RADIX - 1)
    residue_of = jnp.where(
        slot_at < 8, 2 * slot_at + 1,
        jnp.where(slot_at < 12, 4 * slot_at - 30, jnp.where(slot_at < 14, 8 * slot_at - 92, jnp.where(slot_at == 14, 8, 0))),
    )
    chosen = (residue_of == lane_at).astype(jnp.float32).astype(jnp.bfloat16)
    laid = dot(stacked, chosen, ((0,), (0,)))
    at = lax.broadcasted_iota(jnp.int32, laid.shape, 0) & (LANES // RADIX - 1)
    lane = lax.broadcasted_iota(jnp.int32, laid.shape, 1) >> 4
    laid = jnp.where(at == lane, laid, 0.0)
    laid = jnp.sum(laid.reshape(2 * groups, LANES // RADIX, LANES), axis=1)
    top, low = laid[:groups], laid[groups:]
    pk_out[...] = jnp.maximum(top, low)
    for peer in other_bands:
        p_copy(peer, band).start()
    hsum_ref[pl.ds(0, groups, stride=2), :] = top
    hsum_ref[pl.ds(1, groups, stride=2), :] = low
    level = (top + low) * 0.5
    pk_in[band] = pk_out[...]

    for i in range(1, bands):
        slot = lax.rem(band + bands - i, bands)
        m_copy(slot, slot).wait_recv()
    lane = lax.broadcasted_iota(jnp.int32, (slots, LANES), 1)
    slot_id = lax.broadcasted_iota(jnp.int32, (slots, LANES), 0)
    marks = []
    for d in range(bands):
        spread_row = jnp.broadcast_to(mk_in[d], (slots, LANES))
        column = jnp.sum(jnp.where(lane == slot_id, spread_row, 0.0), axis=1, keepdims=True)
        marks.append(jnp.broadcast_to(column, (slots, LANES)).astype(jnp.int32))

    for peer in others:
        x_copy(peer, me).wait_send()
        y_copy(peer, me).wait_send()
        s_copy(peer, me).wait_send()

    @pl.when(odd)
    def _():
        for peer in others:
            h_copy(peer, me, HALF).wait_send()

    @pl.when(jnp.logical_not(odd))
    def _():
        for peer in others:
            h_copy(peer, me, 2 * HALF).wait_send()

    for peer in other_bands:
        m_copy(peer, band).wait_send()

    for i in range(1, bands):
        slot = lax.rem(band + bands - i, bands)
        p_copy(slot, slot).wait_recv()
    sift(bands, groups, slots, [pk_in[d] - level for d in range(bands)], marks, out_ref)

    for peer in other_bands:
        p_copy(peer, band).wait_send()


def per_device(series, cand_start, cand_count):
    dm_rows, samples = series.shape
    shards, bands = lax.axis_size("tm"), lax.axis_size("dm")
    total = samples * shards
    slots = cand_start.shape[3]
    fundamentals = total // (2 * HARM) // shards
    assert shards == RADIX and dm_rows == 2 and samples == LEFT * RIGHT
    chunks = samples // LANES
    x = series.reshape(dm_rows, chunks, LANES).transpose(1, 0, 2).reshape(dm_rows * chunks, LANES)
    tab, offsets = tables(total)
    groups = fundamentals // LANES
    f32, bf16 = jnp.float32, jnp.bfloat16
    vmem = pl.BlockSpec(memory_space=pltpu.VMEM)
    hbm = pl.BlockSpec(memory_space=pltpu.HBM)
    dma = pltpu.SemaphoreType.DMA
    hsum, sifted = pl.pallas_call(
        functools.partial(search_kernel, shards, bands, tuple(offsets), total),
        name="search",
        out_shape=(
            jax.ShapeDtypeStruct((dm_rows * groups, LANES), f32),
            jax.ShapeDtypeStruct((bands, slots, BW), f32),
        ),
        in_specs=[hbm] * 4,
        out_specs=[vmem] * 2,
        scratch_shapes=[
            pltpu.VMEM((bands, slots), jnp.int32),
            pltpu.SMEM((bands,), jnp.int32),
            pltpu.VMEM(tab.shape, f32),
            pltpu.VMEM((shards, dm_rows * chunks // shards, LANES), f32),
            pltpu.VMEM((shards, 2, LEFT // shards, RIGHT), f32),
            pltpu.VMEM((2, LEFT, RIGHT), f32),
            pltpu.VMEM((4 * LEFT, 2 * LEFT), bf16),
            pltpu.VMEM((4 * LEFT, 2 * LEFT), bf16),
            pltpu.VMEM((2 * LEFT, 2 * RIGHT), bf16),
            pltpu.VMEM((2 * LEFT, 2 * RIGHT), bf16),
            pltpu.VMEM((2, LEFT, RIGHT), f32),
            pltpu.VMEM((2, LEFT, RIGHT), f32),
            pltpu.VMEM((2, LEFT, LEFT), f32),
            pltpu.VMEM((shards, 2 * HALF, LANES), f32),
            pltpu.VMEM((shards, 2 * HALF, LANES), f32),
            pltpu.VMEM((2, LANES), f32),
            pltpu.VMEM((shards, 2, LANES), f32),
            pltpu.VMEM((bands, 1, LANES), f32),
            pltpu.VMEM((bands, 1, LANES), f32),
            pltpu.VMEM((groups, LANES), f32),
            pltpu.VMEM((bands, groups, LANES), f32),
            *[dma((shards,)) for _ in range(8)],
            *[dma((bands,)) for _ in range(4)],
            dma((4,)),
            pltpu.SemaphoreType.REGULAR((shards,)),
            pltpu.SemaphoreType.REGULAR((bands,)),
        ],
        compiler_params=pltpu.CompilerParams(
            collective_id=0, has_side_effects=True, vmem_limit_bytes=24 << 20
        ),
    )(*[pltpu.with_memory_space_constraint(a, pltpu.HBM) for a in (x, cand_start.reshape(bands, slots), cand_count.reshape(bands), jnp.asarray(tab))])
    harmonic = hsum.reshape(groups, dm_rows, LANES).transpose(1, 0, 2)
    return harmonic.reshape(dm_rows, fundamentals), sifted[None, None]


def solution(mesh):
    return jax.shard_map(
        per_device,
        mesh=mesh,
        in_specs=(
            P(("beam", "dm"), "tm"),
            P(("beam", "tm"), "dm", None, None),
            P(("beam", "tm"), "dm", None),
        ),
        out_specs=(P(("beam", "dm"), "tm"), P(("beam", "tm"), "dm", None, None, None)),
        check_vma=False,
    )
```

```python
import functools
import math

import jax
import jax.numpy as jnp
import numpy as np
from jax import lax
from jax.experimental import pallas as pl
from jax.experimental.pallas import tpu as pltpu
from jax.sharding import PartitionSpec as P

HARM = 8
BW = 128
EPSILON = 1e-06
LANES = 128
RADIX = 16
JOBS = RADIX // 2
LEFT, RIGHT = 128, 256
MESH = pl.DeviceIdType.MESH
SLOT_RESIDUES = (1, 3, 5, 7, 9, 11, 13, 15, 2, 6, 10, 14, 4, 12, 8, 0)
HALF = JOBS


def tables(total):
    def wave(left, right, period):
        angle = 2.0 * math.pi * (np.outer(left, right) % period) / period
        return np.cos(angle), np.sin(angle)

    left, right, radix = np.arange(LEFT), np.arange(RIGHT), np.arange(RADIX)
    parts = [
        *wave(left, left, LEFT),
        *wave(left, right, LEFT * RIGHT),
        *wave(left, right, RIGHT),
        *wave(radix, left, RADIX * LEFT),
        *wave(radix, right, total),
    ]
    rows, offsets = [], []
    for part in parts:
        offsets.append(sum(r.shape[0] for r in rows))
        for lane in range(0, part.shape[1], LANES):
            rows.append(part[:, lane : lane + LANES])
    return np.concatenate(rows).astype(np.float32), offsets


def split(value):
    high = value.astype(jnp.bfloat16)
    return high, (value - high.astype(jnp.float32)).astype(jnp.bfloat16)


def split_exactly(value):
    high, rest = value.astype(jnp.bfloat16), None
    rest = value - high.astype(jnp.float32)
    middle = rest.astype(jnp.bfloat16)
    return high, middle, (rest - middle.astype(jnp.float32)).astype(jnp.bfloat16)


def dot(left, right, dims):
    return lax.dot_general(left, right, (dims, ((), ())), preferred_element_type=jnp.float32)


def dot_split(left, right, dims):
    (lh, ll), (rh, rl) = left, right
    return dot(lh, rh, dims) + (dot(ll, rh, dims) + dot(lh, rl, dims))


def radix_transform(x):
    half, quarter = RADIX // 2, RADIX // 4

    def real_transform(values, count):
        if count == 1:
            return [(values[0], None)]
        low = [values[i] + values[i + count // 2] for i in range(count // 2)]
        high = [values[i] - values[i + count // 2] for i in range(count // 2)]
        out = {2 * i: v for i, v in enumerate(real_transform(low, count // 2))}
        if count == 2:
            out[1] = (high[0], None)
        elif count == 4:
            out[1] = (high[0], -high[1])
        else:
            h, q = count // 2, count // 4
            minus = [None] + [high[i] - high[h - i] for i in range(1, q)]
            plus = [None] + [high[i] + high[h - i] for i in range(1, q)]
            for term in range(1, h, 2):
                re, im = high[0], high[q] * (-math.sin(2 * math.pi * q * term / count))
                for i in range(1, q):
                    re = re + minus[i] * math.cos(2 * math.pi * i * term / count)
                    im = im - plus[i] * math.sin(2 * math.pi * i * term / count)
                out[term] = (re, im)
        return [out[i] for i in range(count // 2 + 1)]

    return real_transform(x, RADIX)


def picks(job):
    pair = (0, RADIX // 2) if job == 0 else (job, RADIX - job)
    found = {}
    for slot, residue in enumerate(SLOT_RESIDUES):
        for harmonic in range(1, HARM + 1):
            product = harmonic * residue
            if product % RADIX in pair:
                found.setdefault(slot, []).append(
                    (pair.index(product % RADIX), harmonic, product // RADIX)
                )
    return found


def far_first(count):
    return sorted(range(1, count), key=lambda i: -min(i, count - i))


def sift(bands, groups, slots, differences, marks, out_ref):
    lane = lax.broadcasted_iota(jnp.int32, (slots, LANES), 1)
    live = lane < 3 * groups
    wanted = lane & (groups - 1)
    for d in range(bands):
        mark = marks[d]
        begin = jnp.maximum(mark, 0)
        row, shift = begin >> 7, begin & (LANES - 1)
        parts = [p.astype(jnp.float32) for p in split_exactly(differences[d])]
        parts.append(jnp.zeros((LANES - 3 * groups, LANES), jnp.float32))
        source = jnp.concatenate(parts, axis=0).astype(jnp.bfloat16)
        first = jnp.where(live & (wanted == row), 1.0, 0.0)
        second = jnp.where(live & (wanted == row + 1), 1.0, 0.0)
        choose = jnp.concatenate([first, second], axis=0).astype(jnp.bfloat16)
        pair = dot(choose, source, ((1,), (0,)))
        index = (lane + shift) & (LANES - 1)
        low = jnp.take_along_axis(pair[:slots], index, axis=1, mode="promise_in_bounds")
        high = jnp.take_along_axis(pair[slots:], index, axis=1, mode="promise_in_bounds")
        value = jnp.where(lane + shift < LANES, low, high)
        out_ref[d] = jnp.where(mark >= 0, value, 0.0)


def search_kernel(
    shards, bands, offsets, total,
    x_ref, start_hbm, count_hbm, tab_hbm,
    hsum_ref, out_ref,
    start_ref, count_ref, tab, x_in, y_out, y_in, w_hi, w_lo, g_hi, g_lo, t_cos, t_sin, pw,
    h_out, h_in, st_out, st_in, mk_out, mk_in, pk_out, pk_in,
    send_x, recv_x, send_y, recv_y, send_h, recv_h, send_s, recv_s,
    send_m, recv_m, send_p, recv_p, local_sem,
    z_in, z_out, f_out, f_in, send_z, recv_z, send_w, send_f, recv_f, here_shard, here_band,
):
    me = lax.axis_index("tm")
    band = lax.axis_index("dm")
    job, row_kept = me // 2, me % 2
    bins = total // 2
    x_rows = x_in.shape[1]

    barrier = pltpu.get_barrier_semaphore()
    stand = shards // 2
    others = [lax.rem(me + i, shards) for i in far_first(shards)]
    other_bands = [lax.rem(band + i, bands) for i in far_first(bands)]

    def rank(index, count):
        return jnp.where(index == 0, count, index)

    def band_order(index):
        return jnp.where((index == 0) & (me == 0), bands, index)

    my_rank, band_rank = rank(me, shards), band_order(band)

    def greet(semaphore, axis, peer, wanted):
        @pl.when(wanted)
        def _():
            pl.semaphore_signal(semaphore, inc=1, device_id={axis: peer}, device_id_type=MESH)

    for peer in others:
        greet(barrier, "tm", peer, rank(peer, shards) > my_rank)
    for peer in other_bands:
        greet(barrier, "dm", peer, band_order(peer) > band_rank)
    lowers = my_rank - 1 + band_rank - jnp.where(me == 0, 1, 0)

    @pl.when(lowers > 0)
    def _():
        pl.semaphore_wait(barrier, lowers)

    for peer in others:
        greet(here_shard.at[me], "tm", peer, rank(peer, shards) < my_rank)

    def remote(src, dst, send, recv, axis, peer):
        return pltpu.make_async_remote_copy(
            src_ref=src, dst_ref=dst, send_sem=send, recv_sem=recv,
            device_id={axis: peer}, device_id_type=MESH,
        )

    def x_copy(peer, slot):
        rows = pl.ds(pl.multiple_of(peer * x_rows, x_rows), x_rows)
        return remote(x_ref.at[rows], x_in.at[slot], send_x.at[peer], recv_x.at[slot], "tm", peer)

    def y_copy(peer, slot):
        rows = pl.ds(pl.multiple_of(slot * 8, 8), 8)
        return remote(y_out.at[peer], y_in.at[:, rows], send_y.at[peer], recv_y.at[slot], "tm", peer)

    def z_copy(slot):
        rows = pl.ds(0, x_rows)
        return remote(x_ref.at[rows], z_in.at[slot], send_z.at[0], recv_z.at[slot], "tm", stand)

    def w_copy(peer):
        rows = pl.ds(0, 8)
        return remote(z_out.at[peer], y_in.at[:, rows], send_w.at[peer], recv_y.at[0], "tm", peer)

    def f_copy(peer):
        return remote(f_out.at[lax.rem(peer, 2)], f_in, send_f.at[peer], recv_f.at[0], "tm", peer)

    def h_copy(peer, slot, rows):
        part = pl.ds(0, rows)
        return remote(
            h_out.at[peer, part], h_in.at[slot, part], send_h.at[peer], recv_h.at[slot], "tm", peer
        )

    def s_copy(peer, slot):
        return remote(st_out, st_in.at[slot], send_s.at[peer], recv_s.at[slot], "tm", peer)

    def m_copy(peer, slot):
        return remote(mk_out.at[peer], mk_in.at[slot], send_m.at[peer], recv_m.at[slot], "dm", peer)

    def p_copy(peer, slot):
        return remote(pk_out, pk_in.at[slot], send_p.at[peer], recv_p.at[slot], "dm", peer)

    for peer in others:

        @pl.when(rank(peer, shards) < my_rank)
        def _(peer=peer):
            x_copy(peer, me).start()

    own_rows = pl.ds(pl.multiple_of(me * x_rows, x_rows), x_rows)
    own_x = pltpu.make_async_copy(x_ref.at[own_rows], x_in.at[me], local_sem.at[0])
    own_x.start()
    get_starts = pltpu.make_async_copy(start_hbm, start_ref, local_sem.at[1])
    get_starts.start()
    get_counts = pltpu.make_async_copy(count_hbm, count_ref, local_sem.at[2])
    get_counts.start()
    get_tab = pltpu.make_async_copy(tab_hbm, tab, local_sem.at[3])
    get_tab.start()

    for peer in other_bands:
        greet(here_band.at[band], "dm", peer, band_order(peer) < band_rank)
    for i in range(1, shards):
        peer = lax.rem(me + i, shards)

        @pl.when((rank(peer, shards) > my_rank) & (peer != 0))
        def _(peer=peer):
            pl.semaphore_wait(here_shard.at[peer], 1)
            x_copy(peer, me).start()

    @pl.when((me != 0) & (me != stand))
    def _():
        z_copy(me).start()

    @pl.when(me == 0)
    def _():
        own_x.wait()
        for row in range(2):
            for side in range(RIGHT // LANES):
                pick = pl.ds(2 * side + row, 8, stride=4)
                f_out[row, :, side * LANES : (side + 1) * LANES] = x_in[0, pick, :]
        for peer in others:
            f_copy(peer).start()
        f_in[...] = f_out[0]

    slots = start_ref.shape[1]
    get_starts.wait()
    get_counts.wait()
    starts = start_ref[...].astype(jnp.float32)
    starts = jnp.concatenate(
        [starts, jnp.full((bands, LANES - slots), -1.0, jnp.float32)], axis=1
    )
    lane_row = lax.broadcasted_iota(jnp.int32, (1, LANES), 1)
    for d in range(bands):
        mk_out[d] = jnp.where(lane_row < count_ref[d], starts[d : d + 1], -1.0)
    mk_in[band] = mk_out[band]

    get_tab.wait()

    def table(index, rows):
        first = offsets[index]
        return tab[first : first + rows, :]

    def wide(index, rows):
        first = offsets[index]
        return jnp.concatenate(
            [tab[first : first + rows, :], tab[first + rows : first + 2 * rows, :]], axis=1
        )

    def wide_row(index, at):
        first = offsets[index]
        return jnp.concatenate(
            [tab[pl.ds(first + at, 1), :], tab[pl.ds(first + RADIX + at, 1), :]], axis=1
        )

    paired = jnp.where(job == 0, 0.0, 1.0).astype(jnp.float32)
    alone = 1.0 - paired
    residues = (job, jnp.where(job == 0, RADIX // 2, RADIX - job))
    waves = []
    for c, residue in enumerate(residues):
        bc, bs = table(0, LEFT), table(1, LEFT)
        vc = tab[pl.ds(offsets[6] + residue, 1), :]
        vs = tab[pl.ds(offsets[7] + residue, 1), :]
        waves.append((bc * vc - bs * vs, bs * vc + bc * vs))
        bc, bs = wide(2, LEFT), wide(3, LEFT)
        vc, vs = wide_row(8, residue), wide_row(9, residue)
        t_cos[c] = bc * vc - bs * vs
        t_sin[c] = bs * vc + bc * vs
    (ca, sa), (cb, sb) = waves
    blocks = (
        (ca, paired * sa),
        (-sa, paired * ca),
        (paired * cb, alone * cb - paired * sb),
        (-paired * sb, -alone * sb - paired * cb),
    )
    for i, block in enumerate(blocks):
        high, low = split(jnp.concatenate(block, axis=1))
        w_hi[LEFT * i : LEFT * (i + 1), :] = high
        w_lo[LEFT * i : LEFT * (i + 1), :] = low
    gc, gs = wide(4, LEFT), wide(5, LEFT)
    for i, block in enumerate(((gc, gs), (-gs, gc))):
        high, low = split(jnp.concatenate(block, axis=1))
        g_hi[LEFT * i : LEFT * (i + 1), :] = high
        g_lo[LEFT * i : LEFT * (i + 1), :] = low

    def across(source, first, target):
        for row in range(2):
            for side in range(RIGHT // LANES):
                pick = pl.ds(2 * side + row, 8, stride=4)
                arrays = [source[t, pick, :] for t in range(first, shards)]
                if first:
                    arrays = [jnp.zeros_like(arrays[0])] * first + arrays
                terms = radix_transform(arrays)
                lanes = slice(side * LANES, (side + 1) * LANES)
                for j in range(JOBS):
                    re, im = (terms[0][0], terms[JOBS][0]) if j == 0 else terms[j]
                    target[2 * j + row, 0, :, lanes] = re
                    target[2 * j + row, 1, :, lanes] = im

    @pl.when(me == stand)
    def _():
        own_z = pltpu.make_async_copy(x_ref.at[pl.ds(0, x_rows)], z_in.at[stand], local_sem.at[4])
        own_z.start()
        own_z.wait()
        for t in range(1, shards):
            if t != stand:
                z_copy(t).wait_recv()
        across(z_in, 1, z_out)
        for peer in range(1, shards):
            if peer != stand:
                w_copy(peer).start()
        y_in[:, :8, :] = z_out[stand]

    @pl.when(me != 0)
    def _():
        own_x.wait()
        for i in range(1, shards):
            slot = lax.rem(me + shards - i, shards)
            x_copy(slot, slot).wait_recv()
        across(x_in, 0, y_out)
        pl.semaphore_wait(here_shard.at[0], 1)
        for peer in others:
            y_copy(peer, me).start()
        y_in[:, pl.ds(pl.multiple_of(me * 8, 8), 8), :] = y_out[me]

    @pl.when(me == stand)
    def _():
        w_copy(0).start()

    @pl.when(me != 0)
    def _():
        f_copy(0).wait_recv()

    @pl.when(me != stand)
    def _():
        w_copy(0).wait_recv()

    for u in range(1, shards):

        @pl.when(me != u)
        def _(u=u):
            y_copy(u, u).wait_recv()

    y_in[0, :8, :] = y_in[0, :8, :] + f_in[...]
    y_in[1, :8, :] = y_in[1, :8, :] + alone * f_in[...]

    y = jnp.concatenate([y_in[0], y_in[1]], axis=0)
    u = dot_split((w_hi[...], w_lo[...]), split(y), ((1,), (0,)))
    turned = []
    for c in range(2):
        ur, ui = u[2 * c * LEFT : (2 * c + 1) * LEFT], u[(2 * c + 1) * LEFT : (2 * c + 2) * LEFT]
        turned.append(
            jnp.concatenate(
                [ur * t_cos[c] + ui * t_sin[c], ui * t_cos[c] - ur * t_sin[c]], axis=1
            )
        )
    v = jnp.concatenate(turned, axis=0)
    z = dot_split((g_hi[...], g_lo[...]), split(v), ((1,), (1,)))
    zr, zi = z[:LEFT], z[LEFT:]
    power = (zr * zr + zi * zi) * (1.0 / total)
    pw[0] = power[:, :LEFT]
    pw[1] = power[:, LEFT:]

    groups = LEFT * LEFT // (HARM * LANES)
    lane = lax.broadcasted_iota(jnp.int32, (groups, LANES), 1)

    def decimate(which, harmonic, offset, cache):
        if (which, harmonic) not in cache:
            cache[which, harmonic] = [
                pw[which, pl.ds(b, groups, stride=harmonic), :] if harmonic > 1 else pw[which, pl.ds(0, groups), :]
                for b in range(harmonic)
            ]
        rows = cache[which, harmonic]
        if harmonic == 1:
            return rows[0]
        place = lane * harmonic + offset
        index, block = place & (LANES - 1), place >> 7
        out = jnp.take_along_axis(rows[0], index, axis=1, mode="promise_in_bounds")
        for b in range(1, harmonic):
            got = jnp.take_along_axis(rows[b], index, axis=1, mode="promise_in_bounds")
            out = jnp.where(block == b, got, out)
        return out

    for j in range(JOBS):

        @pl.when(job == j)
        def _(j=j):
            cache = {}
            found = picks(j)
            slot_count = HALF if j % 2 else len(SLOT_RESIDUES)
            for slot in range(slot_count):
                acc = None
                for which, harmonic, offset in found.get(slot, []):
                    got = decimate(which, harmonic, offset, cache)
                    acc = got if acc is None else acc + got
                if acc is None:
                    acc = jnp.zeros((groups, LANES), jnp.float32)
                h_out[:, slot, :] = acc

    odd = job % 2 == 1

    @pl.when(odd)
    def _():
        for peer in others:
            h_copy(peer, me, HALF).start()
        h_in[me, :HALF] = h_out[me, :HALF]

    @pl.when(jnp.logical_not(odd))
    def _():
        for peer in others:
            h_copy(peer, me, 2 * HALF).start()
        h_in[me] = h_out[me]

    count = 2 * LEFT * LEFT
    mean = jnp.sum(power, keepdims=True).reshape(1, 1) * (1.0 / count)
    away = power - mean
    squares = jnp.sum(away * away, keepdims=True).reshape(1, 1)
    st_out[0:1, :] = jnp.broadcast_to(mean, (1, LANES))
    st_out[1:2, :] = jnp.broadcast_to(squares, (1, LANES))
    for peer in others:
        s_copy(peer, me).start()
    st_in[me] = st_out[...]

    for peer in other_bands:

        @pl.when(band_order(peer) > band_rank)
        def _(peer=peer):
            pl.semaphore_wait(here_band.at[peer], 1)

        m_copy(peer, band).start()

    for v in range(shards):

        @pl.when(v != me)
        def _(v=v):
            h_copy(v, v, HALF if (v // 2) % 2 else 2 * HALF).wait_recv()
            s_copy(v, v).wait_recv()

    rows_out = []
    for row in range(2):
        sources = [2 * j + row for j in range(JOBS)]
        stats = [st_in[v] for v in sources]
        mean = sum(s[0:1] for s in stats) * (1.0 / JOBS)
        squares = sum(s[1:2] for s in stats)
        between = sum((s[0:1] - mean) * (s[0:1] - mean) for s in stats)
        spread = (squares + between * float(count)) * (1.0 / bins)
        scale = 1.0 / jnp.sqrt(spread + EPSILON)
        first = sum(h_in[v, :HALF, :] for v in sources)
        second = sum(h_in[v, HALF:, :] for v in sources if (v // 2) % 2 == 0)
        summed = jnp.concatenate([first, second], axis=0)
        rows_out.append((summed - float(HARM) * mean) * scale)

    both = jnp.concatenate(rows_out, axis=1)
    stacked = jnp.concatenate([p.astype(jnp.float32) for p in split_exactly(both)], axis=0).astype(jnp.bfloat16)
    places = stacked.shape[0]
    slot_at = lax.broadcasted_iota(jnp.int32, (places, LANES), 0) & (RADIX - 1)
    lane_at = lax.broadcasted_iota(jnp.int32, (places, LANES), 1) & (RADIX - 1)
    residue_of = jnp.where(
        slot_at < 8, 2 * slot_at + 1,
        jnp.where(slot_at < 12, 4 * slot_at - 30, jnp.where(slot_at < 14, 8 * slot_at - 92, jnp.where(slot_at == 14, 8, 0))),
    )
    chosen = (residue_of == lane_at).astype(jnp.float32).astype(jnp.bfloat16)
    laid = dot(stacked, chosen, ((0,), (0,)))
    at = lax.broadcasted_iota(jnp.int32, laid.shape, 0) & (LANES // RADIX - 1)
    lane = lax.broadcasted_iota(jnp.int32, laid.shape, 1) >> 4
    laid = jnp.where(at == lane, laid, 0.0)
    laid = jnp.sum(laid.reshape(2 * groups, LANES // RADIX, LANES), axis=1)
    top, low = laid[:groups], laid[groups:]
    pk_out[...] = jnp.maximum(top, low)
    for peer in other_bands:
        p_copy(peer, band).start()
    hsum_ref[pl.ds(0, groups, stride=2), :] = top
    hsum_ref[pl.ds(1, groups, stride=2), :] = low
    level = (top + low) * 0.5
    pk_in[band] = pk_out[...]

    for i in range(1, bands):
        slot = lax.rem(band + bands - i, bands)
        m_copy(slot, slot).wait_recv()
    lane = lax.broadcasted_iota(jnp.int32, (slots, LANES), 1)
    slot_id = lax.broadcasted_iota(jnp.int32, (slots, LANES), 0)
    marks = []
    for d in range(bands):
        spread_row = jnp.broadcast_to(mk_in[d], (slots, LANES))
        column = jnp.sum(jnp.where(lane == slot_id, spread_row, 0.0), axis=1, keepdims=True)
        marks.append(jnp.broadcast_to(column, (slots, LANES)).astype(jnp.int32))

    for peer in others:

        @pl.when(peer != 0)
        def _(peer=peer):
            x_copy(peer, me).wait_send()

        s_copy(peer, me).wait_send()

    @pl.when(me != 0)
    def _():
        for peer in others:
            y_copy(peer, me).wait_send()

    @pl.when((me != 0) & (me != stand))
    def _():
        z_copy(me).wait_send()

    @pl.when(me == stand)
    def _():
        for peer in range(shards):
            if peer != stand:
                w_copy(peer).wait_send()

    @pl.when(me == 0)
    def _():
        for peer in others:
            f_copy(peer).wait_send()

    @pl.when(odd)
    def _():
        for peer in others:
            h_copy(peer, me, HALF).wait_send()

    @pl.when(jnp.logical_not(odd))
    def _():
        for peer in others:
            h_copy(peer, me, 2 * HALF).wait_send()

    for peer in other_bands:
        m_copy(peer, band).wait_send()

    for i in range(1, bands):
        slot = lax.rem(band + bands - i, bands)
        p_copy(slot, slot).wait_recv()
    sift(bands, groups, slots, [pk_in[d] - level for d in range(bands)], marks, out_ref)

    for peer in other_bands:
        p_copy(peer, band).wait_send()


def per_device(series, cand_start, cand_count):
    dm_rows, samples = series.shape
    shards, bands = lax.axis_size("tm"), lax.axis_size("dm")
    total = samples * shards
    slots = cand_start.shape[3]
    fundamentals = total // (2 * HARM) // shards
    assert shards == RADIX and dm_rows == 2 and samples == LEFT * RIGHT
    chunks = samples // LANES
    x = series.reshape(dm_rows, chunks, LANES).transpose(1, 0, 2).reshape(dm_rows * chunks, LANES)
    tab, offsets = tables(total)
    groups = fundamentals // LANES
    f32, bf16 = jnp.float32, jnp.bfloat16
    vmem = pl.BlockSpec(memory_space=pltpu.VMEM)
    hbm = pl.BlockSpec(memory_space=pltpu.HBM)
    dma = pltpu.SemaphoreType.DMA
    hsum, sifted = pl.pallas_call(
        functools.partial(search_kernel, shards, bands, tuple(offsets), total),
        name="search",
        out_shape=(
            jax.ShapeDtypeStruct((dm_rows * groups, LANES), f32),
            jax.ShapeDtypeStruct((bands, slots, BW), f32),
        ),
        in_specs=[hbm] * 4,
        out_specs=[vmem] * 2,
        scratch_shapes=[
            pltpu.VMEM((bands, slots), jnp.int32),
            pltpu.SMEM((bands,), jnp.int32),
            pltpu.VMEM(tab.shape, f32),
            pltpu.VMEM((shards, dm_rows * chunks // shards, LANES), f32),
            pltpu.VMEM((shards, 2, LEFT // shards, RIGHT), f32),
            pltpu.VMEM((2, LEFT, RIGHT), f32),
            pltpu.VMEM((4 * LEFT, 2 * LEFT), bf16),
            pltpu.VMEM((4 * LEFT, 2 * LEFT), bf16),
            pltpu.VMEM((2 * LEFT, 2 * RIGHT), bf16),
            pltpu.VMEM((2 * LEFT, 2 * RIGHT), bf16),
            pltpu.VMEM((2, LEFT, RIGHT), f32),
            pltpu.VMEM((2, LEFT, RIGHT), f32),
            pltpu.VMEM((2, LEFT, LEFT), f32),
            pltpu.VMEM((shards, 2 * HALF, LANES), f32),
            pltpu.VMEM((shards, 2 * HALF, LANES), f32),
            pltpu.VMEM((2, LANES), f32),
            pltpu.VMEM((shards, 2, LANES), f32),
            pltpu.VMEM((bands, 1, LANES), f32),
            pltpu.VMEM((bands, 1, LANES), f32),
            pltpu.VMEM((groups, LANES), f32),
            pltpu.VMEM((bands, groups, LANES), f32),
            *[dma((shards,)) for _ in range(8)],
            *[dma((bands,)) for _ in range(4)],
            dma((5,)),
            pltpu.VMEM((shards, dm_rows * chunks // shards, LANES), f32),
            pltpu.VMEM((shards, 2, LEFT // shards, RIGHT), f32),
            pltpu.VMEM((2, LEFT // shards, RIGHT), f32),
            pltpu.VMEM((LEFT // shards, RIGHT), f32),
            dma((1,)),
            dma((shards,)),
            dma((shards,)),
            dma((shards,)),
            dma((1,)),
            pltpu.SemaphoreType.REGULAR((shards,)),
            pltpu.SemaphoreType.REGULAR((bands,)),
        ],
        compiler_params=pltpu.CompilerParams(
            collective_id=0, has_side_effects=True, vmem_limit_bytes=24 << 20
        ),
    )(*[pltpu.with_memory_space_constraint(a, pltpu.HBM) for a in (x, cand_start.reshape(bands, slots), cand_count.reshape(bands), jnp.asarray(tab))])
    harmonic = hsum.reshape(groups, dm_rows, LANES).transpose(1, 0, 2)
    return harmonic.reshape(dm_rows, fundamentals), sifted[None, None]


def solution(mesh):
    return jax.shard_map(
        per_device,
        mesh=mesh,
        in_specs=(
            P(("beam", "dm"), "tm"),
            P(("beam", "tm"), "dm", None, None),
            P(("beam", "tm"), "dm", None),
        ),
        out_specs=(P(("beam", "dm"), "tm"), P(("beam", "tm"), "dm", None, None, None)),
        check_vma=False,
    )
```

```python
import functools
import math

import jax
import jax.numpy as jnp
import numpy as np
from jax import lax
from jax.experimental import pallas as pl
from jax.experimental.pallas import tpu as pltpu
from jax.sharding import PartitionSpec as P

HARM = 8
BW = 128
EPSILON = 1e-06
LANES = 128
RADIX = 16
JOBS = RADIX // 2
LEFT, RIGHT = 128, 256
MESH = pl.DeviceIdType.MESH
SLOT_RESIDUES = (1, 3, 5, 7, 9, 11, 13, 15, 2, 6, 10, 14, 4, 12, 8, 0)
HALF = JOBS


def tables(total):
    def wave(left, right, period):
        angle = 2.0 * math.pi * (np.outer(left, right) % period) / period
        return np.cos(angle), np.sin(angle)

    left, right, radix = np.arange(LEFT), np.arange(RIGHT), np.arange(RADIX)
    parts = [
        *wave(left, left, LEFT),
        *wave(left, right, LEFT * RIGHT),
        *wave(left, right, RIGHT),
        *wave(radix, left, RADIX * LEFT),
        *wave(radix, right, total),
    ]
    rows, offsets = [], []
    for part in parts:
        offsets.append(sum(r.shape[0] for r in rows))
        for lane in range(0, part.shape[1], LANES):
            rows.append(part[:, lane : lane + LANES])
    return np.concatenate(rows).astype(np.float32), offsets


def split(value):
    high = value.astype(jnp.bfloat16)
    return high, (value - high.astype(jnp.float32)).astype(jnp.bfloat16)


def split_exactly(value):
    high, rest = value.astype(jnp.bfloat16), None
    rest = value - high.astype(jnp.float32)
    middle = rest.astype(jnp.bfloat16)
    return high, middle, (rest - middle.astype(jnp.float32)).astype(jnp.bfloat16)


def dot(left, right, dims):
    return lax.dot_general(left, right, (dims, ((), ())), preferred_element_type=jnp.float32)


def dot_split(left, right, dims):
    (lh, ll), (rh, rl) = left, right
    return dot(lh, rh, dims) + (dot(ll, rh, dims) + dot(lh, rl, dims))


def radix_transform(x):
    half, quarter = RADIX // 2, RADIX // 4

    def real_transform(values, count):
        if count == 1:
            return [(values[0], None)]
        low = [values[i] + values[i + count // 2] for i in range(count // 2)]
        high = [values[i] - values[i + count // 2] for i in range(count // 2)]
        out = {2 * i: v for i, v in enumerate(real_transform(low, count // 2))}
        if count == 2:
            out[1] = (high[0], None)
        elif count == 4:
            out[1] = (high[0], -high[1])
        else:
            h, q = count // 2, count // 4
            minus = [None] + [high[i] - high[h - i] for i in range(1, q)]
            plus = [None] + [high[i] + high[h - i] for i in range(1, q)]
            for term in range(1, h, 2):
                re, im = high[0], high[q] * (-math.sin(2 * math.pi * q * term / count))
                for i in range(1, q):
                    re = re + minus[i] * math.cos(2 * math.pi * i * term / count)
                    im = im - plus[i] * math.sin(2 * math.pi * i * term / count)
                out[term] = (re, im)
        return [out[i] for i in range(count // 2 + 1)]

    return real_transform(x, RADIX)


def picks(job):
    pair = (0, RADIX // 2) if job == 0 else (job, RADIX - job)
    found = {}
    for slot, residue in enumerate(SLOT_RESIDUES):
        for harmonic in range(1, HARM + 1):
            product = harmonic * residue
            if product % RADIX in pair:
                found.setdefault(slot, []).append(
                    (pair.index(product % RADIX), harmonic, product // RADIX)
                )
    return found


def far_first(count):
    return sorted(range(1, count), key=lambda i: -min(i, count - i))


def sift(bands, groups, slots, differences, marks, out_ref):
    lane = lax.broadcasted_iota(jnp.int32, (slots, LANES), 1)
    live = lane < 3 * groups
    wanted = lane & (groups - 1)
    for d in range(bands):
        mark = marks[d]
        begin = jnp.maximum(mark, 0)
        row, shift = begin >> 7, begin & (LANES - 1)
        parts = [p.astype(jnp.float32) for p in split_exactly(differences[d])]
        parts.append(jnp.zeros((LANES - 3 * groups, LANES), jnp.float32))
        source = jnp.concatenate(parts, axis=0).astype(jnp.bfloat16)
        first = jnp.where(live & (wanted == row), 1.0, 0.0)
        second = jnp.where(live & (wanted == row + 1), 1.0, 0.0)
        choose = jnp.concatenate([first, second], axis=0).astype(jnp.bfloat16)
        pair = dot(choose, source, ((1,), (0,)))
        index = (lane + shift) & (LANES - 1)
        low = jnp.take_along_axis(pair[:slots], index, axis=1, mode="promise_in_bounds")
        high = jnp.take_along_axis(pair[slots:], index, axis=1, mode="promise_in_bounds")
        value = jnp.where(lane + shift < LANES, low, high)
        out_ref[d] = jnp.where(mark >= 0, value, 0.0)


def search_kernel(
    shards, bands, offsets, total,
    x_ref, start_hbm, count_hbm, tab_hbm,
    hsum_ref, out_ref,
    start_ref, count_ref, tab, x_in, y_out, y_in, w_hi, w_lo, g_hi, g_lo, t_cos, t_sin, pw,
    h_out, h_in, st_out, st_in, mk_out, mk_in, pk_out, pk_in,
    send_x, recv_x, send_y, recv_y, send_h, recv_h, send_s, recv_s,
    send_m, recv_m, send_p, recv_p, local_sem,
    z_in, z_out, f_out, f_in, send_z, recv_z, send_w, send_f, recv_f, here_shard, here_band,
):
    me = lax.axis_index("tm")
    band = lax.axis_index("dm")
    job, row_kept = me // 2, me % 2
    bins = total // 2
    x_rows = x_in.shape[1]

    barrier = pltpu.get_barrier_semaphore()
    stand = shards // 2
    others = [lax.rem(me + i, shards) for i in far_first(shards)]
    other_bands = [lax.rem(band + i, bands) for i in far_first(bands)]

    first_row = band == 0
    handles = (me != 0) | jnp.logical_not(first_row)

    def rank(index, count):
        return jnp.where((index == 0) & first_row, count, index)

    def band_order(index):
        return jnp.where((index == 0) & (me == 0), bands, index)

    my_rank, band_rank = rank(me, shards), band_order(band)

    def greet(semaphore, axis, peer, wanted):
        @pl.when(wanted)
        def _():
            pl.semaphore_signal(semaphore, inc=1, device_id={axis: peer}, device_id_type=MESH)

    for peer in others:
        greet(barrier, "tm", peer, rank(peer, shards) > my_rank)
    for peer in other_bands:
        greet(barrier, "dm", peer, band_order(peer) > band_rank)
    lowers = my_rank + band_rank - jnp.where(first_row, 1, 0) - jnp.where(me == 0, 1, 0)

    @pl.when(lowers > 0)
    def _():
        pl.semaphore_wait(barrier, lowers)

    for peer in others:
        greet(here_shard.at[me], "tm", peer, rank(peer, shards) < my_rank)

    def remote(src, dst, send, recv, axis, peer):
        return pltpu.make_async_remote_copy(
            src_ref=src, dst_ref=dst, send_sem=send, recv_sem=recv,
            device_id={axis: peer}, device_id_type=MESH,
        )

    def x_copy(peer, slot):
        rows = pl.ds(pl.multiple_of(peer * x_rows, x_rows), x_rows)
        return remote(x_ref.at[rows], x_in.at[slot], send_x.at[peer], recv_x.at[slot], "tm", peer)

    def y_copy(peer, slot):
        rows = pl.ds(pl.multiple_of(slot * 8, 8), 8)
        return remote(y_out.at[peer], y_in.at[:, rows], send_y.at[peer], recv_y.at[slot], "tm", peer)

    def z_copy(slot):
        rows = pl.ds(0, x_rows)
        return remote(x_ref.at[rows], z_in.at[slot], send_z.at[0], recv_z.at[slot], "tm", stand)

    def w_copy(peer):
        rows = pl.ds(0, 8)
        return remote(z_out.at[peer], y_in.at[:, rows], send_w.at[peer], recv_y.at[0], "tm", peer)

    def f_copy(peer):
        return remote(f_out.at[lax.rem(peer, 2)], f_in, send_f.at[peer], recv_f.at[0], "tm", peer)

    def h_copy(peer, slot, rows):
        part = pl.ds(0, rows)
        return remote(
            h_out.at[peer, part], h_in.at[slot, part], send_h.at[peer], recv_h.at[slot], "tm", peer
        )

    def s_copy(peer, slot):
        return remote(st_out, st_in.at[slot], send_s.at[peer], recv_s.at[slot], "tm", peer)

    def m_copy(peer, slot):
        return remote(mk_out.at[peer], mk_in.at[slot], send_m.at[peer], recv_m.at[slot], "dm", peer)

    def p_copy(peer, slot):
        return remote(pk_out, pk_in.at[slot], send_p.at[peer], recv_p.at[slot], "dm", peer)

    for peer in others:

        @pl.when(rank(peer, shards) < my_rank)
        def _(peer=peer):
            x_copy(peer, me).start()

    own_rows = pl.ds(pl.multiple_of(me * x_rows, x_rows), x_rows)
    own_x = pltpu.make_async_copy(x_ref.at[own_rows], x_in.at[me], local_sem.at[0])
    own_x.start()
    get_starts = pltpu.make_async_copy(start_hbm, start_ref, local_sem.at[1])
    get_starts.start()
    get_counts = pltpu.make_async_copy(count_hbm, count_ref, local_sem.at[2])
    get_counts.start()
    get_tab = pltpu.make_async_copy(tab_hbm, tab, local_sem.at[3])
    get_tab.start()

    for peer in other_bands:
        greet(here_band.at[band], "dm", peer, band_order(peer) < band_rank)
    for i in range(1, shards):
        peer = lax.rem(me + i, shards)

        @pl.when((rank(peer, shards) > my_rank) & (peer != 0))
        def _(peer=peer):
            pl.semaphore_wait(here_shard.at[peer], 1)
            x_copy(peer, me).start()

    @pl.when(first_row & (me != 0) & (me != stand))
    def _():
        z_copy(me).start()

    @pl.when(first_row & (me == 0))
    def _():
        own_x.wait()
        for row in range(2):
            for side in range(RIGHT // LANES):
                pick = pl.ds(2 * side + row, 8, stride=4)
                f_out[row, :, side * LANES : (side + 1) * LANES] = x_in[0, pick, :]
        for peer in others:
            f_copy(peer).start()
        f_in[...] = f_out[0]

    slots = start_ref.shape[1]
    get_starts.wait()
    get_counts.wait()
    starts = start_ref[...].astype(jnp.float32)
    starts = jnp.concatenate(
        [starts, jnp.full((bands, LANES - slots), -1.0, jnp.float32)], axis=1
    )
    lane_row = lax.broadcasted_iota(jnp.int32, (1, LANES), 1)
    for d in range(bands):
        mk_out[d] = jnp.where(lane_row < count_ref[d], starts[d : d + 1], -1.0)
    mk_in[band] = mk_out[band]

    get_tab.wait()

    def table(index, rows):
        first = offsets[index]
        return tab[first : first + rows, :]

    def wide(index, rows):
        first = offsets[index]
        return jnp.concatenate(
            [tab[first : first + rows, :], tab[first + rows : first + 2 * rows, :]], axis=1
        )

    def wide_row(index, at):
        first = offsets[index]
        return jnp.concatenate(
            [tab[pl.ds(first + at, 1), :], tab[pl.ds(first + RADIX + at, 1), :]], axis=1
        )

    paired = jnp.where(job == 0, 0.0, 1.0).astype(jnp.float32)
    alone = 1.0 - paired
    residues = (job, jnp.where(job == 0, RADIX // 2, RADIX - job))
    waves = []
    for c, residue in enumerate(residues):
        bc, bs = table(0, LEFT), table(1, LEFT)
        vc = tab[pl.ds(offsets[6] + residue, 1), :]
        vs = tab[pl.ds(offsets[7] + residue, 1), :]
        waves.append((bc * vc - bs * vs, bs * vc + bc * vs))
        bc, bs = wide(2, LEFT), wide(3, LEFT)
        vc, vs = wide_row(8, residue), wide_row(9, residue)
        t_cos[c] = bc * vc - bs * vs
        t_sin[c] = bs * vc + bc * vs
    (ca, sa), (cb, sb) = waves
    blocks = (
        (ca, paired * sa),
        (-sa, paired * ca),
        (paired * cb, alone * cb - paired * sb),
        (-paired * sb, -alone * sb - paired * cb),
    )
    for i, block in enumerate(blocks):
        high, low = split(jnp.concatenate(block, axis=1))
        w_hi[LEFT * i : LEFT * (i + 1), :] = high
        w_lo[LEFT * i : LEFT * (i + 1), :] = low
    gc, gs = wide(4, LEFT), wide(5, LEFT)
    for i, block in enumerate(((gc, gs), (-gs, gc))):
        high, low = split(jnp.concatenate(block, axis=1))
        g_hi[LEFT * i : LEFT * (i + 1), :] = high
        g_lo[LEFT * i : LEFT * (i + 1), :] = low

    def across(source, first, target):
        for row in range(2):
            for side in range(RIGHT // LANES):
                pick = pl.ds(2 * side + row, 8, stride=4)
                arrays = [source[t, pick, :] for t in range(first, shards)]
                if first:
                    arrays = [jnp.zeros_like(arrays[0])] * first + arrays
                terms = radix_transform(arrays)
                lanes = slice(side * LANES, (side + 1) * LANES)
                for j in range(JOBS):
                    re, im = (terms[0][0], terms[JOBS][0]) if j == 0 else terms[j]
                    target[2 * j + row, 0, :, lanes] = re
                    target[2 * j + row, 1, :, lanes] = im

    @pl.when(first_row & (me == stand))
    def _():
        own_z = pltpu.make_async_copy(x_ref.at[pl.ds(0, x_rows)], z_in.at[stand], local_sem.at[4])
        own_z.start()
        own_z.wait()
        for t in range(1, shards):
            if t != stand:
                z_copy(t).wait_recv()
        across(z_in, 1, z_out)
        for peer in range(1, shards):
            if peer != stand:
                w_copy(peer).start()
        y_in[:, :8, :] = z_out[stand]

    @pl.when(handles)
    def _():
        own_x.wait()
        for i in range(1, shards):
            slot = lax.rem(me + shards - i, shards)
            x_copy(slot, slot).wait_recv()
        across(x_in, 0, y_out)

        @pl.when(first_row)
        def _():
            pl.semaphore_wait(here_shard.at[0], 1)

        @pl.when(first_row & (me == stand))
        def _():
            w_copy(0).start()

        for peer in others:
            y_copy(peer, me).start()
        y_in[:, pl.ds(pl.multiple_of(me * 8, 8), 8), :] = y_out[me]

    @pl.when(first_row & (me != 0))
    def _():
        f_copy(0).wait_recv()

    @pl.when(me != jnp.where(first_row, stand, 0))
    def _():
        w_copy(0).wait_recv()

    for u in range(1, shards):

        @pl.when(me != u)
        def _(u=u):
            y_copy(u, u).wait_recv()

    @pl.when(first_row)
    def _():
        y_in[0, :8, :] = y_in[0, :8, :] + f_in[...]
        y_in[1, :8, :] = y_in[1, :8, :] + alone * f_in[...]

    y = jnp.concatenate([y_in[0], y_in[1]], axis=0)
    u = dot_split((w_hi[...], w_lo[...]), split(y), ((1,), (0,)))
    turned = []
    for c in range(2):
        ur, ui = u[2 * c * LEFT : (2 * c + 1) * LEFT], u[(2 * c + 1) * LEFT : (2 * c + 2) * LEFT]
        turned.append(
            jnp.concatenate(
                [ur * t_cos[c] + ui * t_sin[c], ui * t_cos[c] - ur * t_sin[c]], axis=1
            )
        )
    v = jnp.concatenate(turned, axis=0)
    z = dot_split((g_hi[...], g_lo[...]), split(v), ((1,), (1,)))
    zr, zi = z[:LEFT], z[LEFT:]
    power = (zr * zr + zi * zi) * (1.0 / total)
    pw[0] = power[:, :LEFT]
    pw[1] = power[:, LEFT:]

    groups = LEFT * LEFT // (HARM * LANES)
    lane = lax.broadcasted_iota(jnp.int32, (groups, LANES), 1)

    def decimate(which, harmonic, offset, cache):
        if (which, harmonic) not in cache:
            cache[which, harmonic] = [
                pw[which, pl.ds(b, groups, stride=harmonic), :] if harmonic > 1 else pw[which, pl.ds(0, groups), :]
                for b in range(harmonic)
            ]
        rows = cache[which, harmonic]
        if harmonic == 1:
            return rows[0]
        place = lane * harmonic + offset
        index, block = place & (LANES - 1), place >> 7
        out = jnp.take_along_axis(rows[0], index, axis=1, mode="promise_in_bounds")
        for b in range(1, harmonic):
            got = jnp.take_along_axis(rows[b], index, axis=1, mode="promise_in_bounds")
            out = jnp.where(block == b, got, out)
        return out

    for j in range(JOBS):

        @pl.when(job == j)
        def _(j=j):
            cache = {}
            found = picks(j)
            slot_count = HALF if j % 2 else len(SLOT_RESIDUES)
            for slot in range(slot_count):
                acc = None
                for which, harmonic, offset in found.get(slot, []):
                    got = decimate(which, harmonic, offset, cache)
                    acc = got if acc is None else acc + got
                if acc is None:
                    acc = jnp.zeros((groups, LANES), jnp.float32)
                h_out[:, slot, :] = acc

    odd = job % 2 == 1

    @pl.when(odd)
    def _():
        for peer in others:
            h_copy(peer, me, HALF).start()
        h_in[me, :HALF] = h_out[me, :HALF]

    @pl.when(jnp.logical_not(odd))
    def _():
        for peer in others:
            h_copy(peer, me, 2 * HALF).start()
        h_in[me] = h_out[me]

    count = 2 * LEFT * LEFT
    mean = jnp.sum(power, keepdims=True).reshape(1, 1) * (1.0 / count)
    away = power - mean
    squares = jnp.sum(away * away, keepdims=True).reshape(1, 1)
    st_out[0:1, :] = jnp.broadcast_to(mean, (1, LANES))
    st_out[1:2, :] = jnp.broadcast_to(squares, (1, LANES))
    for peer in others:
        s_copy(peer, me).start()
    st_in[me] = st_out[...]

    for peer in other_bands:

        @pl.when(band_order(peer) > band_rank)
        def _(peer=peer):
            pl.semaphore_wait(here_band.at[peer], 1)

        m_copy(peer, band).start()

    for v in range(shards):

        @pl.when(v != me)
        def _(v=v):
            h_copy(v, v, HALF if (v // 2) % 2 else 2 * HALF).wait_recv()
            s_copy(v, v).wait_recv()

    rows_out = []
    for row in range(2):
        sources = [2 * j + row for j in range(JOBS)]
        stats = [st_in[v] for v in sources]
        mean = sum(s[0:1] for s in stats) * (1.0 / JOBS)
        squares = sum(s[1:2] for s in stats)
        between = sum((s[0:1] - mean) * (s[0:1] - mean) for s in stats)
        spread = (squares + between * float(count)) * (1.0 / bins)
        scale = 1.0 / jnp.sqrt(spread + EPSILON)
        first = sum(h_in[v, :HALF, :] for v in sources)
        second = sum(h_in[v, HALF:, :] for v in sources if (v // 2) % 2 == 0)
        summed = jnp.concatenate([first, second], axis=0)
        rows_out.append((summed - float(HARM) * mean) * scale)

    both = jnp.concatenate(rows_out, axis=1)
    stacked = jnp.concatenate([p.astype(jnp.float32) for p in split_exactly(both)], axis=0).astype(jnp.bfloat16)
    places = stacked.shape[0]
    slot_at = lax.broadcasted_iota(jnp.int32, (places, LANES), 0) & (RADIX - 1)
    lane_at = lax.broadcasted_iota(jnp.int32, (places, LANES), 1) & (RADIX - 1)
    residue_of = jnp.where(
        slot_at < 8, 2 * slot_at + 1,
        jnp.where(slot_at < 12, 4 * slot_at - 30, jnp.where(slot_at < 14, 8 * slot_at - 92, jnp.where(slot_at == 14, 8, 0))),
    )
    chosen = (residue_of == lane_at).astype(jnp.float32).astype(jnp.bfloat16)
    laid = dot(stacked, chosen, ((0,), (0,)))
    at = lax.broadcasted_iota(jnp.int32, laid.shape, 0) & (LANES // RADIX - 1)
    lane = lax.broadcasted_iota(jnp.int32, laid.shape, 1) >> 4
    laid = jnp.where(at == lane, laid, 0.0)
    laid = jnp.sum(laid.reshape(2 * groups, LANES // RADIX, LANES), axis=1)
    top, low = laid[:groups], laid[groups:]
    pk_out[...] = jnp.maximum(top, low)
    for peer in other_bands:
        p_copy(peer, band).start()
    hsum_ref[pl.ds(0, groups, stride=2), :] = top
    hsum_ref[pl.ds(1, groups, stride=2), :] = low
    level = (top + low) * 0.5
    pk_in[band] = pk_out[...]

    for i in range(1, bands):
        slot = lax.rem(band + bands - i, bands)
        m_copy(slot, slot).wait_recv()
    lane = lax.broadcasted_iota(jnp.int32, (slots, LANES), 1)
    slot_id = lax.broadcasted_iota(jnp.int32, (slots, LANES), 0)
    marks = []
    for d in range(bands):
        spread_row = jnp.broadcast_to(mk_in[d], (slots, LANES))
        column = jnp.sum(jnp.where(lane == slot_id, spread_row, 0.0), axis=1, keepdims=True)
        marks.append(jnp.broadcast_to(column, (slots, LANES)).astype(jnp.int32))

    for peer in others:

        @pl.when((peer != 0) | jnp.logical_not(first_row))
        def _(peer=peer):
            x_copy(peer, me).wait_send()

        s_copy(peer, me).wait_send()

    @pl.when(handles)
    def _():
        for peer in others:
            y_copy(peer, me).wait_send()

    @pl.when(first_row & (me != 0) & (me != stand))
    def _():
        z_copy(me).wait_send()

    @pl.when(first_row & (me == stand))
    def _():
        for peer in range(shards):
            if peer != stand:
                w_copy(peer).wait_send()

    @pl.when(first_row & (me == 0))
    def _():
        for peer in others:
            f_copy(peer).wait_send()

    @pl.when(odd)
    def _():
        for peer in others:
            h_copy(peer, me, HALF).wait_send()

    @pl.when(jnp.logical_not(odd))
    def _():
        for peer in others:
            h_copy(peer, me, 2 * HALF).wait_send()

    for peer in other_bands:
        m_copy(peer, band).wait_send()

    for i in range(1, bands):
        slot = lax.rem(band + bands - i, bands)
        p_copy(slot, slot).wait_recv()
    sift(bands, groups, slots, [pk_in[d] - level for d in range(bands)], marks, out_ref)

    for peer in other_bands:
        p_copy(peer, band).wait_send()


def per_device(series, cand_start, cand_count):
    dm_rows, samples = series.shape
    shards, bands = lax.axis_size("tm"), lax.axis_size("dm")
    total = samples * shards
    slots = cand_start.shape[3]
    fundamentals = total // (2 * HARM) // shards
    assert shards == RADIX and dm_rows == 2 and samples == LEFT * RIGHT
    chunks = samples // LANES
    x = series.reshape(dm_rows, chunks, LANES).transpose(1, 0, 2).reshape(dm_rows * chunks, LANES)
    tab, offsets = tables(total)
    groups = fundamentals // LANES
    f32, bf16 = jnp.float32, jnp.bfloat16
    vmem = pl.BlockSpec(memory_space=pltpu.VMEM)
    hbm = pl.BlockSpec(memory_space=pltpu.HBM)
    dma = pltpu.SemaphoreType.DMA
    hsum, sifted = pl.pallas_call(
        functools.partial(search_kernel, shards, bands, tuple(offsets), total),
        name="search",
        out_shape=(
            jax.ShapeDtypeStruct((dm_rows * groups, LANES), f32),
            jax.ShapeDtypeStruct((bands, slots, BW), f32),
        ),
        in_specs=[hbm] * 4,
        out_specs=[vmem] * 2,
        scratch_shapes=[
            pltpu.VMEM((bands, slots), jnp.int32),
            pltpu.SMEM((bands,), jnp.int32),
            pltpu.VMEM(tab.shape, f32),
            pltpu.VMEM((shards, dm_rows * chunks // shards, LANES), f32),
            pltpu.VMEM((shards, 2, LEFT // shards, RIGHT), f32),
            pltpu.VMEM((2, LEFT, RIGHT), f32),
            pltpu.VMEM((4 * LEFT, 2 * LEFT), bf16),
            pltpu.VMEM((4 * LEFT, 2 * LEFT), bf16),
            pltpu.VMEM((2 * LEFT, 2 * RIGHT), bf16),
            pltpu.VMEM((2 * LEFT, 2 * RIGHT), bf16),
            pltpu.VMEM((2, LEFT, RIGHT), f32),
            pltpu.VMEM((2, LEFT, RIGHT), f32),
            pltpu.VMEM((2, LEFT, LEFT), f32),
            pltpu.VMEM((shards, 2 * HALF, LANES), f32),
            pltpu.VMEM((shards, 2 * HALF, LANES), f32),
            pltpu.VMEM((2, LANES), f32),
            pltpu.VMEM((shards, 2, LANES), f32),
            pltpu.VMEM((bands, 1, LANES), f32),
            pltpu.VMEM((bands, 1, LANES), f32),
            pltpu.VMEM((groups, LANES), f32),
            pltpu.VMEM((bands, groups, LANES), f32),
            *[dma((shards,)) for _ in range(8)],
            *[dma((bands,)) for _ in range(4)],
            dma((5,)),
            pltpu.VMEM((shards, dm_rows * chunks // shards, LANES), f32),
            pltpu.VMEM((shards, 2, LEFT // shards, RIGHT), f32),
            pltpu.VMEM((2, LEFT // shards, RIGHT), f32),
            pltpu.VMEM((LEFT // shards, RIGHT), f32),
            dma((1,)),
            dma((shards,)),
            dma((shards,)),
            dma((shards,)),
            dma((1,)),
            pltpu.SemaphoreType.REGULAR((shards,)),
            pltpu.SemaphoreType.REGULAR((bands,)),
        ],
        compiler_params=pltpu.CompilerParams(
            collective_id=0, has_side_effects=True, vmem_limit_bytes=24 << 20
        ),
    )(*[pltpu.with_memory_space_constraint(a, pltpu.HBM) for a in (x, cand_start.reshape(bands, slots), cand_count.reshape(bands), jnp.asarray(tab))])
    harmonic = hsum.reshape(groups, dm_rows, LANES).transpose(1, 0, 2)
    return harmonic.reshape(dm_rows, fundamentals), sifted[None, None]


def solution(mesh):
    return jax.shard_map(
        per_device,
        mesh=mesh,
        in_specs=(
            P(("beam", "dm"), "tm"),
            P(("beam", "tm"), "dm", None, None),
            P(("beam", "tm"), "dm", None),
        ),
        out_specs=(P(("beam", "dm"), "tm"), P(("beam", "tm"), "dm", None, None, None)),
        check_vma=False,
    )
```

```python
import functools
import math

import jax
import jax.numpy as jnp
import numpy as np
from jax import lax
from jax.experimental import pallas as pl
from jax.experimental.pallas import tpu as pltpu
from jax.sharding import PartitionSpec as P

HARM = 8
BW = 128
EPSILON = 1e-06
LANES = 128
RADIX = 16
JOBS = RADIX // 2
LEFT, RIGHT = 128, 256
MESH = pl.DeviceIdType.MESH
SLOT_RESIDUES = (1, 3, 5, 7, 9, 11, 13, 15, 2, 6, 10, 14, 4, 12, 8, 0)
HALF = JOBS


def tables(total):
    def wave(left, right, period):
        angle = 2.0 * math.pi * (np.outer(left, right) % period) / period
        return np.cos(angle), np.sin(angle)

    left, right, radix = np.arange(LEFT), np.arange(RIGHT), np.arange(RADIX)
    parts = [
        *wave(left, left, LEFT),
        *wave(left, right, LEFT * RIGHT),
        *wave(left, right, RIGHT),
        *wave(radix, left, RADIX * LEFT),
        *wave(radix, right, total),
    ]
    rows, offsets = [], []
    for part in parts:
        offsets.append(sum(r.shape[0] for r in rows))
        for lane in range(0, part.shape[1], LANES):
            rows.append(part[:, lane : lane + LANES])
    return np.concatenate(rows).astype(np.float32), offsets


def split(value):
    high = value.astype(jnp.bfloat16)
    return high, (value - high.astype(jnp.float32)).astype(jnp.bfloat16)


def split_exactly(value):
    high, rest = value.astype(jnp.bfloat16), None
    rest = value - high.astype(jnp.float32)
    middle = rest.astype(jnp.bfloat16)
    return high, middle, (rest - middle.astype(jnp.float32)).astype(jnp.bfloat16)


def dot(left, right, dims):
    return lax.dot_general(left, right, (dims, ((), ())), preferred_element_type=jnp.float32)


def dot_split(left, right, dims):
    (lh, ll), (rh, rl) = left, right
    return dot(lh, rh, dims) + (dot(ll, rh, dims) + dot(lh, rl, dims))


def radix_transform(x):
    half, quarter = RADIX // 2, RADIX // 4

    def real_transform(values, count):
        if count == 1:
            return [(values[0], None)]
        low = [values[i] + values[i + count // 2] for i in range(count // 2)]
        high = [values[i] - values[i + count // 2] for i in range(count // 2)]
        out = {2 * i: v for i, v in enumerate(real_transform(low, count // 2))}
        if count == 2:
            out[1] = (high[0], None)
        elif count == 4:
            out[1] = (high[0], -high[1])
        else:
            h, q = count // 2, count // 4
            minus = [None] + [high[i] - high[h - i] for i in range(1, q)]
            plus = [None] + [high[i] + high[h - i] for i in range(1, q)]
            for term in range(1, h, 2):
                re, im = high[0], high[q] * (-math.sin(2 * math.pi * q * term / count))
                for i in range(1, q):
                    re = re + minus[i] * math.cos(2 * math.pi * i * term / count)
                    im = im - plus[i] * math.sin(2 * math.pi * i * term / count)
                out[term] = (re, im)
        return [out[i] for i in range(count // 2 + 1)]

    return real_transform(x, RADIX)


def picks(job):
    pair = (0, RADIX // 2) if job == 0 else (job, RADIX - job)
    found = {}
    for slot, residue in enumerate(SLOT_RESIDUES):
        for harmonic in range(1, HARM + 1):
            product = harmonic * residue
            if product % RADIX in pair:
                found.setdefault(slot, []).append(
                    (pair.index(product % RADIX), harmonic, product // RADIX)
                )
    return found


def far_first(count):
    return sorted(range(1, count), key=lambda i: -min(i, count - i))


def sift(bands, groups, slots, differences, marks, out_ref):
    lane = lax.broadcasted_iota(jnp.int32, (slots, LANES), 1)
    live = lane < 3 * groups
    wanted = lane & (groups - 1)
    for d in range(bands):
        mark = marks[d]
        begin = jnp.maximum(mark, 0)
        row, shift = begin >> 7, begin & (LANES - 1)
        parts = [p.astype(jnp.float32) for p in split_exactly(differences[d])]
        parts.append(jnp.zeros((LANES - 3 * groups, LANES), jnp.float32))
        source = jnp.concatenate(parts, axis=0).astype(jnp.bfloat16)
        first = jnp.where(live & (wanted == row), 1.0, 0.0)
        second = jnp.where(live & (wanted == row + 1), 1.0, 0.0)
        choose = jnp.concatenate([first, second], axis=0).astype(jnp.bfloat16)
        pair = dot(choose, source, ((1,), (0,)))
        index = (lane + shift) & (LANES - 1)
        low = jnp.take_along_axis(pair[:slots], index, axis=1, mode="promise_in_bounds")
        high = jnp.take_along_axis(pair[slots:], index, axis=1, mode="promise_in_bounds")
        value = jnp.where(lane + shift < LANES, low, high)
        out_ref[d] = jnp.where(mark >= 0, value, 0.0)


def search_kernel(
    shards, bands, offsets, total,
    x_ref, start_hbm, count_hbm, tab_hbm,
    hsum_ref, out_ref,
    start_ref, count_ref, tab, x_in, y_out, y_in, w_hi, w_lo, g_hi, g_lo, t_cos, t_sin, pw,
    h_out, h_in, st_out, st_in, mk_out, mk_in, pk_out, pk_in,
    send_x, recv_x, send_y, recv_y, send_h, recv_h, send_s, recv_s,
    send_m, recv_m, send_p, recv_p, local_sem,
    relay_buf, relay_sem, z_in, z_out, f_out, f_in, send_z, recv_z, send_w, send_f, recv_f, here_shard, here_band,
):
    me = lax.axis_index("tm")
    band = lax.axis_index("dm")
    job, row_kept = me // 2, me % 2
    bins = total // 2
    x_rows = x_in.shape[1]

    barrier = pltpu.get_barrier_semaphore()
    stand = shards // 2
    others = [lax.rem(me + i, shards) for i in far_first(shards)]
    other_bands = [lax.rem(band + i, bands) for i in far_first(bands)]

    first_row = band == 0
    handles = (me != 0) | jnp.logical_not(first_row)

    def rank(index, count):
        return jnp.where((index == 0) & first_row, count, index)

    def band_order(index):
        return jnp.where((index == 0) & (me == 0), bands, index)

    my_rank, band_rank = rank(me, shards), band_order(band)

    def greet(semaphore, axis, peer, wanted):
        @pl.when(wanted)
        def _():
            pl.semaphore_signal(semaphore, inc=1, device_id={axis: peer}, device_id_type=MESH)

    for peer in others:
        greet(barrier, "tm", peer, rank(peer, shards) > my_rank)
    for peer in other_bands:
        greet(barrier, "dm", peer, band_order(peer) > band_rank)
    lowers = my_rank + band_rank - jnp.where(first_row, 1, 0) - jnp.where(me == 0, 1, 0)

    @pl.when(lowers > 0)
    def _():
        pl.semaphore_wait(barrier, lowers)

    for peer in others:
        greet(here_shard.at[me], "tm", peer, rank(peer, shards) < my_rank)

    def remote(src, dst, send, recv, axis, peer):
        return pltpu.make_async_remote_copy(
            src_ref=src, dst_ref=dst, send_sem=send, recv_sem=recv,
            device_id={axis: peer}, device_id_type=MESH,
        )

    def x_copy(peer, slot):
        rows = pl.ds(pl.multiple_of(peer * x_rows, x_rows), x_rows)
        return remote(x_ref.at[rows], x_in.at[slot], send_x.at[peer], recv_x.at[slot], "tm", peer)

    def y_copy(peer, slot):
        rows = pl.ds(pl.multiple_of(slot * 8, 8), 8)
        return remote(y_out.at[peer], y_in.at[:, rows], send_y.at[peer], recv_y.at[slot], "tm", peer)

    far, quarter = shards // 2, shards // 4
    relay = lax.rem(me + shards - quarter, shards)
    origin = lax.rem(me + quarter, shards)
    origin_handles = (origin != 0) | jnp.logical_not(first_row)

    def r_copy():
        opposite = lax.rem(me + far, shards)
        return remote(y_out.at[opposite], relay_buf, send_y.at[opposite], relay_sem.at[0], "tm", relay)

    def fwd_copy():
        rows = pl.ds(pl.multiple_of(origin * 8, 8), 8)
        return remote(relay_buf, y_in.at[:, rows], relay_sem.at[1], recv_y.at[origin], "tm", relay)

    def z_copy(slot):
        rows = pl.ds(0, x_rows)
        return remote(x_ref.at[rows], z_in.at[slot], send_z.at[0], recv_z.at[slot], "tm", stand)

    def w_copy(peer):
        rows = pl.ds(0, 8)
        return remote(z_out.at[peer], y_in.at[:, rows], send_w.at[peer], recv_y.at[0], "tm", peer)

    def f_copy(peer):
        return remote(f_out.at[lax.rem(peer, 2)], f_in, send_f.at[peer], recv_f.at[0], "tm", peer)

    def h_copy(peer, slot, rows):
        part = pl.ds(0, rows)
        return remote(
            h_out.at[peer, part], h_in.at[slot, part], send_h.at[peer], recv_h.at[slot], "tm", peer
        )

    def s_copy(peer, slot):
        return remote(st_out, st_in.at[slot], send_s.at[peer], recv_s.at[slot], "tm", peer)

    def m_copy(peer, slot):
        return remote(mk_out.at[peer], mk_in.at[slot], send_m.at[peer], recv_m.at[slot], "dm", peer)

    def p_copy(peer, slot):
        return remote(pk_out, pk_in.at[slot], send_p.at[peer], recv_p.at[slot], "dm", peer)

    for peer in others:

        @pl.when(rank(peer, shards) < my_rank)
        def _(peer=peer):
            x_copy(peer, me).start()

    own_rows = pl.ds(pl.multiple_of(me * x_rows, x_rows), x_rows)
    own_x = pltpu.make_async_copy(x_ref.at[own_rows], x_in.at[me], local_sem.at[0])
    own_x.start()
    get_starts = pltpu.make_async_copy(start_hbm, start_ref, local_sem.at[1])
    get_starts.start()
    get_counts = pltpu.make_async_copy(count_hbm, count_ref, local_sem.at[2])
    get_counts.start()
    get_tab = pltpu.make_async_copy(tab_hbm, tab, local_sem.at[3])
    get_tab.start()

    for peer in other_bands:
        greet(here_band.at[band], "dm", peer, band_order(peer) < band_rank)
    for i in range(1, shards):
        peer = lax.rem(me + i, shards)

        @pl.when((rank(peer, shards) > my_rank) & (peer != 0))
        def _(peer=peer):
            pl.semaphore_wait(here_shard.at[peer], 1)
            x_copy(peer, me).start()

    @pl.when(first_row & (me != 0) & (me != stand))
    def _():
        z_copy(me).start()

    @pl.when(first_row & (me == 0))
    def _():
        own_x.wait()
        for row in range(2):
            for side in range(RIGHT // LANES):
                pick = pl.ds(2 * side + row, 8, stride=4)
                f_out[row, :, side * LANES : (side + 1) * LANES] = x_in[0, pick, :]
        for peer in others:
            f_copy(peer).start()
        f_in[...] = f_out[0]

    slots = start_ref.shape[1]
    get_starts.wait()
    get_counts.wait()
    starts = start_ref[...].astype(jnp.float32)
    starts = jnp.concatenate(
        [starts, jnp.full((bands, LANES - slots), -1.0, jnp.float32)], axis=1
    )
    lane_row = lax.broadcasted_iota(jnp.int32, (1, LANES), 1)
    for d in range(bands):
        mk_out[d] = jnp.where(lane_row < count_ref[d], starts[d : d + 1], -1.0)
    mk_in[band] = mk_out[band]

    get_tab.wait()

    def table(index, rows):
        first = offsets[index]
        return tab[first : first + rows, :]

    def wide(index, rows):
        first = offsets[index]
        return jnp.concatenate(
            [tab[first : first + rows, :], tab[first + rows : first + 2 * rows, :]], axis=1
        )

    def wide_row(index, at):
        first = offsets[index]
        return jnp.concatenate(
            [tab[pl.ds(first + at, 1), :], tab[pl.ds(first + RADIX + at, 1), :]], axis=1
        )

    paired = jnp.where(job == 0, 0.0, 1.0).astype(jnp.float32)
    alone = 1.0 - paired
    residues = (job, jnp.where(job == 0, RADIX // 2, RADIX - job))
    waves = []
    for c, residue in enumerate(residues):
        bc, bs = table(0, LEFT), table(1, LEFT)
        vc = tab[pl.ds(offsets[6] + residue, 1), :]
        vs = tab[pl.ds(offsets[7] + residue, 1), :]
        waves.append((bc * vc - bs * vs, bs * vc + bc * vs))
        bc, bs = wide(2, LEFT), wide(3, LEFT)
        vc, vs = wide_row(8, residue), wide_row(9, residue)
        t_cos[c] = bc * vc - bs * vs
        t_sin[c] = bs * vc + bc * vs
    (ca, sa), (cb, sb) = waves
    blocks = (
        (ca, paired * sa),
        (-sa, paired * ca),
        (paired * cb, alone * cb - paired * sb),
        (-paired * sb, -alone * sb - paired * cb),
    )
    for i, block in enumerate(blocks):
        high, low = split(jnp.concatenate(block, axis=1))
        w_hi[LEFT * i : LEFT * (i + 1), :] = high
        w_lo[LEFT * i : LEFT * (i + 1), :] = low
    gc, gs = wide(4, LEFT), wide(5, LEFT)
    for i, block in enumerate(((gc, gs), (-gs, gc))):
        high, low = split(jnp.concatenate(block, axis=1))
        g_hi[LEFT * i : LEFT * (i + 1), :] = high
        g_lo[LEFT * i : LEFT * (i + 1), :] = low

    def across(source, first, target):
        for row in range(2):
            for side in range(RIGHT // LANES):
                pick = pl.ds(2 * side + row, 8, stride=4)
                arrays = [source[t, pick, :] for t in range(first, shards)]
                if first:
                    arrays = [jnp.zeros_like(arrays[0])] * first + arrays
                terms = radix_transform(arrays)
                lanes = slice(side * LANES, (side + 1) * LANES)
                for j in range(JOBS):
                    re, im = (terms[0][0], terms[JOBS][0]) if j == 0 else terms[j]
                    target[2 * j + row, 0, :, lanes] = re
                    target[2 * j + row, 1, :, lanes] = im

    @pl.when(first_row & (me == stand))
    def _():
        own_z = pltpu.make_async_copy(x_ref.at[pl.ds(0, x_rows)], z_in.at[stand], local_sem.at[4])
        own_z.start()
        own_z.wait()
        for t in range(1, shards):
            if t != stand:
                z_copy(t).wait_recv()
        across(z_in, 1, z_out)
        for peer in range(1, shards):
            if peer != stand:
                w_copy(peer).start()
        y_in[:, :8, :] = z_out[stand]

    @pl.when(handles)
    def _():
        own_x.wait()
        for i in range(1, shards):
            slot = lax.rem(me + shards - i, shards)
            x_copy(slot, slot).wait_recv()
        across(x_in, 0, y_out)

        @pl.when(first_row)
        def _():
            pl.semaphore_wait(here_shard.at[0], 1)

        @pl.when(first_row & (me == stand))
        def _():
            w_copy(0).start()

        r_copy().start()
        for i in far_first(shards)[1:]:
            y_copy(lax.rem(me + i, shards), me).start()
        y_in[:, pl.ds(pl.multiple_of(me * 8, 8), 8), :] = y_out[me]

    @pl.when(origin_handles)
    def _():
        r_copy().wait_recv()
        fwd_copy().start()

    @pl.when(first_row & (me != 0))
    def _():
        f_copy(0).wait_recv()

    @pl.when(me != jnp.where(first_row, stand, 0))
    def _():
        w_copy(0).wait_recv()

    for u in range(1, shards):

        @pl.when(me != u)
        def _(u=u):
            y_copy(u, u).wait_recv()

    @pl.when(first_row)
    def _():
        y_in[0, :8, :] = y_in[0, :8, :] + f_in[...]
        y_in[1, :8, :] = y_in[1, :8, :] + alone * f_in[...]

    y = jnp.concatenate([y_in[0], y_in[1]], axis=0)
    u = dot_split((w_hi[...], w_lo[...]), split(y), ((1,), (0,)))
    turned = []
    for c in range(2):
        ur, ui = u[2 * c * LEFT : (2 * c + 1) * LEFT], u[(2 * c + 1) * LEFT : (2 * c + 2) * LEFT]
        turned.append(
            jnp.concatenate(
                [ur * t_cos[c] + ui * t_sin[c], ui * t_cos[c] - ur * t_sin[c]], axis=1
            )
        )
    v = jnp.concatenate(turned, axis=0)
    z = dot_split((g_hi[...], g_lo[...]), split(v), ((1,), (1,)))
    zr, zi = z[:LEFT], z[LEFT:]
    power = (zr * zr + zi * zi) * (1.0 / total)
    pw[0] = power[:, :LEFT]
    pw[1] = power[:, LEFT:]

    groups = LEFT * LEFT // (HARM * LANES)
    lane = lax.broadcasted_iota(jnp.int32, (groups, LANES), 1)

    def decimate(which, harmonic, offset, cache):
        if (which, harmonic) not in cache:
            cache[which, harmonic] = [
                pw[which, pl.ds(b, groups, stride=harmonic), :] if harmonic > 1 else pw[which, pl.ds(0, groups), :]
                for b in range(harmonic)
            ]
        rows = cache[which, harmonic]
        if harmonic == 1:
            return rows[0]
        place = lane * harmonic + offset
        index, block = place & (LANES - 1), place >> 7
        out = jnp.take_along_axis(rows[0], index, axis=1, mode="promise_in_bounds")
        for b in range(1, harmonic):
            got = jnp.take_along_axis(rows[b], index, axis=1, mode="promise_in_bounds")
            out = jnp.where(block == b, got, out)
        return out

    for j in range(JOBS):

        @pl.when(job == j)
        def _(j=j):
            cache = {}
            found = picks(j)
            slot_count = HALF if j % 2 else len(SLOT_RESIDUES)
            for slot in range(slot_count):
                acc = None
                for which, harmonic, offset in found.get(slot, []):
                    got = decimate(which, harmonic, offset, cache)
                    acc = got if acc is None else acc + got
                if acc is None:
                    acc = jnp.zeros((groups, LANES), jnp.float32)
                h_out[:, slot, :] = acc

    odd = job % 2 == 1

    @pl.when(odd)
    def _():
        for peer in others:
            h_copy(peer, me, HALF).start()
        h_in[me, :HALF] = h_out[me, :HALF]

    @pl.when(jnp.logical_not(odd))
    def _():
        for peer in others:
            h_copy(peer, me, 2 * HALF).start()
        h_in[me] = h_out[me]

    count = 2 * LEFT * LEFT
    mean = jnp.sum(power, keepdims=True).reshape(1, 1) * (1.0 / count)
    away = power - mean
    squares = jnp.sum(away * away, keepdims=True).reshape(1, 1)
    st_out[0:1, :] = jnp.broadcast_to(mean, (1, LANES))
    st_out[1:2, :] = jnp.broadcast_to(squares, (1, LANES))
    for peer in others:
        s_copy(peer, me).start()
    st_in[me] = st_out[...]

    for peer in other_bands:

        @pl.when(band_order(peer) > band_rank)
        def _(peer=peer):
            pl.semaphore_wait(here_band.at[peer], 1)

        m_copy(peer, band).start()

    for v in range(shards):

        @pl.when(v != me)
        def _(v=v):
            h_copy(v, v, HALF if (v // 2) % 2 else 2 * HALF).wait_recv()
            s_copy(v, v).wait_recv()

    rows_out = []
    for row in range(2):
        sources = [2 * j + row for j in range(JOBS)]
        stats = [st_in[v] for v in sources]
        mean = sum(s[0:1] for s in stats) * (1.0 / JOBS)
        squares = sum(s[1:2] for s in stats)
        between = sum((s[0:1] - mean) * (s[0:1] - mean) for s in stats)
        spread = (squares + between * float(count)) * (1.0 / bins)
        scale = 1.0 / jnp.sqrt(spread + EPSILON)
        first = sum(h_in[v, :HALF, :] for v in sources)
        second = sum(h_in[v, HALF:, :] for v in sources if (v // 2) % 2 == 0)
        summed = jnp.concatenate([first, second], axis=0)
        rows_out.append((summed - float(HARM) * mean) * scale)

    both = jnp.concatenate(rows_out, axis=1)
    stacked = jnp.concatenate([p.astype(jnp.float32) for p in split_exactly(both)], axis=0).astype(jnp.bfloat16)
    places = stacked.shape[0]
    slot_at = lax.broadcasted_iota(jnp.int32, (places, LANES), 0) & (RADIX - 1)
    lane_at = lax.broadcasted_iota(jnp.int32, (places, LANES), 1) & (RADIX - 1)
    residue_of = jnp.where(
        slot_at < 8, 2 * slot_at + 1,
        jnp.where(slot_at < 12, 4 * slot_at - 30, jnp.where(slot_at < 14, 8 * slot_at - 92, jnp.where(slot_at == 14, 8, 0))),
    )
    chosen = (residue_of == lane_at).astype(jnp.float32).astype(jnp.bfloat16)
    laid = dot(stacked, chosen, ((0,), (0,)))
    at = lax.broadcasted_iota(jnp.int32, laid.shape, 0) & (LANES // RADIX - 1)
    lane = lax.broadcasted_iota(jnp.int32, laid.shape, 1) >> 4
    laid = jnp.where(at == lane, laid, 0.0)
    laid = jnp.sum(laid.reshape(2 * groups, LANES // RADIX, LANES), axis=1)
    top, low = laid[:groups], laid[groups:]
    pk_out[...] = jnp.maximum(top, low)
    for peer in other_bands:
        p_copy(peer, band).start()
    hsum_ref[pl.ds(0, groups, stride=2), :] = top
    hsum_ref[pl.ds(1, groups, stride=2), :] = low
    level = (top + low) * 0.5
    pk_in[band] = pk_out[...]

    for i in range(1, bands):
        slot = lax.rem(band + bands - i, bands)
        m_copy(slot, slot).wait_recv()
    lane = lax.broadcasted_iota(jnp.int32, (slots, LANES), 1)
    slot_id = lax.broadcasted_iota(jnp.int32, (slots, LANES), 0)
    marks = []
    for d in range(bands):
        spread_row = jnp.broadcast_to(mk_in[d], (slots, LANES))
        column = jnp.sum(jnp.where(lane == slot_id, spread_row, 0.0), axis=1, keepdims=True)
        marks.append(jnp.broadcast_to(column, (slots, LANES)).astype(jnp.int32))

    for peer in others:

        @pl.when((peer != 0) | jnp.logical_not(first_row))
        def _(peer=peer):
            x_copy(peer, me).wait_send()

        s_copy(peer, me).wait_send()

    @pl.when(handles)
    def _():
        r_copy().wait_send()
        for i in far_first(shards)[1:]:
            y_copy(lax.rem(me + i, shards), me).wait_send()

    @pl.when(origin_handles)
    def _():
        fwd_copy().wait_send()

    @pl.when(first_row & (me != 0) & (me != stand))
    def _():
        z_copy(me).wait_send()

    @pl.when(first_row & (me == stand))
    def _():
        for peer in range(shards):
            if peer != stand:
                w_copy(peer).wait_send()

    @pl.when(first_row & (me == 0))
    def _():
        for peer in others:
            f_copy(peer).wait_send()

    @pl.when(odd)
    def _():
        for peer in others:
            h_copy(peer, me, HALF).wait_send()

    @pl.when(jnp.logical_not(odd))
    def _():
        for peer in others:
            h_copy(peer, me, 2 * HALF).wait_send()

    for peer in other_bands:
        m_copy(peer, band).wait_send()

    for i in range(1, bands):
        slot = lax.rem(band + bands - i, bands)
        p_copy(slot, slot).wait_recv()
    sift(bands, groups, slots, [pk_in[d] - level for d in range(bands)], marks, out_ref)

    for peer in other_bands:
        p_copy(peer, band).wait_send()


def per_device(series, cand_start, cand_count):
    dm_rows, samples = series.shape
    shards, bands = lax.axis_size("tm"), lax.axis_size("dm")
    total = samples * shards
    slots = cand_start.shape[3]
    fundamentals = total // (2 * HARM) // shards
    assert shards == RADIX and dm_rows == 2 and samples == LEFT * RIGHT
    chunks = samples // LANES
    x = series.reshape(dm_rows, chunks, LANES).transpose(1, 0, 2).reshape(dm_rows * chunks, LANES)
    tab, offsets = tables(total)
    groups = fundamentals // LANES
    f32, bf16 = jnp.float32, jnp.bfloat16
    vmem = pl.BlockSpec(memory_space=pltpu.VMEM)
    hbm = pl.BlockSpec(memory_space=pltpu.HBM)
    dma = pltpu.SemaphoreType.DMA
    hsum, sifted = pl.pallas_call(
        functools.partial(search_kernel, shards, bands, tuple(offsets), total),
        name="search",
        out_shape=(
            jax.ShapeDtypeStruct((dm_rows * groups, LANES), f32),
            jax.ShapeDtypeStruct((bands, slots, BW), f32),
        ),
        in_specs=[hbm] * 4,
        out_specs=[vmem] * 2,
        scratch_shapes=[
            pltpu.VMEM((bands, slots), jnp.int32),
            pltpu.SMEM((bands,), jnp.int32),
            pltpu.VMEM(tab.shape, f32),
            pltpu.VMEM((shards, dm_rows * chunks // shards, LANES), f32),
            pltpu.VMEM((shards, 2, LEFT // shards, RIGHT), f32),
            pltpu.VMEM((2, LEFT, RIGHT), f32),
            pltpu.VMEM((4 * LEFT, 2 * LEFT), bf16),
            pltpu.VMEM((4 * LEFT, 2 * LEFT), bf16),
            pltpu.VMEM((2 * LEFT, 2 * RIGHT), bf16),
            pltpu.VMEM((2 * LEFT, 2 * RIGHT), bf16),
            pltpu.VMEM((2, LEFT, RIGHT), f32),
            pltpu.VMEM((2, LEFT, RIGHT), f32),
            pltpu.VMEM((2, LEFT, LEFT), f32),
            pltpu.VMEM((shards, 2 * HALF, LANES), f32),
            pltpu.VMEM((shards, 2 * HALF, LANES), f32),
            pltpu.VMEM((2, LANES), f32),
            pltpu.VMEM((shards, 2, LANES), f32),
            pltpu.VMEM((bands, 1, LANES), f32),
            pltpu.VMEM((bands, 1, LANES), f32),
            pltpu.VMEM((groups, LANES), f32),
            pltpu.VMEM((bands, groups, LANES), f32),
            *[dma((shards,)) for _ in range(8)],
            *[dma((bands,)) for _ in range(4)],
            dma((5,)),
            pltpu.VMEM((2, LEFT // shards, RIGHT), f32),
            dma((2,)),
            pltpu.VMEM((shards, dm_rows * chunks // shards, LANES), f32),
            pltpu.VMEM((shards, 2, LEFT // shards, RIGHT), f32),
            pltpu.VMEM((2, LEFT // shards, RIGHT), f32),
            pltpu.VMEM((LEFT // shards, RIGHT), f32),
            dma((1,)),
            dma((shards,)),
            dma((shards,)),
            dma((shards,)),
            dma((1,)),
            pltpu.SemaphoreType.REGULAR((shards,)),
            pltpu.SemaphoreType.REGULAR((bands,)),
        ],
        compiler_params=pltpu.CompilerParams(
            collective_id=0, has_side_effects=True, vmem_limit_bytes=24 << 20
        ),
    )(*[pltpu.with_memory_space_constraint(a, pltpu.HBM) for a in (x, cand_start.reshape(bands, slots), cand_count.reshape(bands), jnp.asarray(tab))])
    harmonic = hsum.reshape(groups, dm_rows, LANES).transpose(1, 0, 2)
    return harmonic.reshape(dm_rows, fundamentals), sifted[None, None]


def solution(mesh):
    return jax.shard_map(
        per_device,
        mesh=mesh,
        in_specs=(
            P(("beam", "dm"), "tm"),
            P(("beam", "tm"), "dm", None, None),
            P(("beam", "tm"), "dm", None),
        ),
        out_specs=(P(("beam", "dm"), "tm"), P(("beam", "tm"), "dm", None, None, None)),
        check_vma=False,
    )
```

```python
import functools
import math

import jax
import jax.numpy as jnp
import numpy as np
from jax import lax
from jax.experimental import pallas as pl
from jax.experimental.pallas import tpu as pltpu
from jax.sharding import PartitionSpec as P

HARM = 8
BW = 128
EPSILON = 1e-06
LANES = 128
RADIX = 16
JOBS = RADIX // 2
LEFT, RIGHT = 128, 256
MESH = pl.DeviceIdType.MESH
SLOT_RESIDUES = (1, 3, 5, 7, 9, 11, 13, 15, 2, 6, 10, 14, 4, 12, 8, 0)
HALF = JOBS


def tables(total):
    def wave(left, right, period):
        angle = 2.0 * math.pi * (np.outer(left, right) % period) / period
        return np.cos(angle), np.sin(angle)

    left, right, radix = np.arange(LEFT), np.arange(RIGHT), np.arange(RADIX)
    parts = [
        *wave(left, left, LEFT),
        *wave(left, right, LEFT * RIGHT),
        *wave(left, right, RIGHT),
        *wave(radix, left, RADIX * LEFT),
        *wave(radix, right, total),
    ]
    rows, offsets = [], []
    for part in parts:
        offsets.append(sum(r.shape[0] for r in rows))
        for lane in range(0, part.shape[1], LANES):
            rows.append(part[:, lane : lane + LANES])
    return np.concatenate(rows).astype(np.float32), offsets


def split(value):
    high = value.astype(jnp.bfloat16)
    return high, (value - high.astype(jnp.float32)).astype(jnp.bfloat16)


def split_exactly(value):
    high, rest = value.astype(jnp.bfloat16), None
    rest = value - high.astype(jnp.float32)
    middle = rest.astype(jnp.bfloat16)
    return high, middle, (rest - middle.astype(jnp.float32)).astype(jnp.bfloat16)


def dot(left, right, dims):
    return lax.dot_general(left, right, (dims, ((), ())), preferred_element_type=jnp.float32)


def dot_split(left, right, dims):
    (lh, ll), (rh, rl) = left, right
    return dot(lh, rh, dims) + (dot(ll, rh, dims) + dot(lh, rl, dims))


def radix_transform(x):
    half, quarter = RADIX // 2, RADIX // 4

    def real_transform(values, count):
        if count == 1:
            return [(values[0], None)]
        low = [values[i] + values[i + count // 2] for i in range(count // 2)]
        high = [values[i] - values[i + count // 2] for i in range(count // 2)]
        out = {2 * i: v for i, v in enumerate(real_transform(low, count // 2))}
        if count == 2:
            out[1] = (high[0], None)
        elif count == 4:
            out[1] = (high[0], -high[1])
        else:
            h, q = count // 2, count // 4
            minus = [None] + [high[i] - high[h - i] for i in range(1, q)]
            plus = [None] + [high[i] + high[h - i] for i in range(1, q)]
            for term in range(1, h, 2):
                re, im = high[0], high[q] * (-math.sin(2 * math.pi * q * term / count))
                for i in range(1, q):
                    re = re + minus[i] * math.cos(2 * math.pi * i * term / count)
                    im = im - plus[i] * math.sin(2 * math.pi * i * term / count)
                out[term] = (re, im)
        return [out[i] for i in range(count // 2 + 1)]

    return real_transform(x, RADIX)


def picks(job):
    pair = (0, RADIX // 2) if job == 0 else (job, RADIX - job)
    found = {}
    for slot, residue in enumerate(SLOT_RESIDUES):
        for harmonic in range(1, HARM + 1):
            product = harmonic * residue
            if product % RADIX in pair:
                found.setdefault(slot, []).append(
                    (pair.index(product % RADIX), harmonic, product // RADIX)
                )
    return found


def far_first(count):
    return sorted(range(1, count), key=lambda i: -min(i, count - i))


def sift(bands, groups, slots, differences, marks, out_ref):
    lane = lax.broadcasted_iota(jnp.int32, (slots, LANES), 1)
    live = lane < 3 * groups
    wanted = lane & (groups - 1)
    for d in range(bands):
        mark = marks[d]
        begin = jnp.maximum(mark, 0)
        row, shift = begin >> 7, begin & (LANES - 1)
        parts = [p.astype(jnp.float32) for p in split_exactly(differences[d])]
        parts.append(jnp.zeros((LANES - 3 * groups, LANES), jnp.float32))
        source = jnp.concatenate(parts, axis=0).astype(jnp.bfloat16)
        first = jnp.where(live & (wanted == row), 1.0, 0.0)
        second = jnp.where(live & (wanted == row + 1), 1.0, 0.0)
        choose = jnp.concatenate([first, second], axis=0).astype(jnp.bfloat16)
        pair = dot(choose, source, ((1,), (0,)))
        index = (lane + shift) & (LANES - 1)
        low = jnp.take_along_axis(pair[:slots], index, axis=1, mode="promise_in_bounds")
        high = jnp.take_along_axis(pair[slots:], index, axis=1, mode="promise_in_bounds")
        value = jnp.where(lane + shift < LANES, low, high)
        out_ref[d] = jnp.where(mark >= 0, value, 0.0)


def search_kernel(
    shards, bands, offsets, total,
    x_ref, start_hbm, count_hbm, tab_hbm,
    hsum_ref, out_ref,
    start_ref, count_ref, tab, x_in, y_out, y_in, w_hi, w_lo, g_hi, g_lo, t_cos, t_sin, pw,
    h_out, h_in, st_out, st_in, mk_out, mk_in, pk_out, pk_in,
    send_x, recv_x, send_y, recv_y, send_h, recv_h, send_s, recv_s,
    send_m, recv_m, send_p, recv_p, local_sem, here_shard, here_band,
):
    me = lax.axis_index("tm")
    band = lax.axis_index("dm")
    job, row_kept = me // 2, me % 2
    bins = total // 2
    x_rows = x_in.shape[1]

    barrier = pltpu.get_barrier_semaphore()
    others = [lax.rem(me + i, shards) for i in far_first(shards)]
    other_bands = [lax.rem(band + i, bands) for i in far_first(bands)]

    def rank(index, count):
        return jnp.where(index == 0, count, index)

    def band_order(index):
        return jnp.where((index == 0) & (me == 0), bands, index)

    my_rank, band_rank = rank(me, shards), band_order(band)

    def greet(semaphore, axis, peer, wanted):
        @pl.when(wanted)
        def _():
            pl.semaphore_signal(semaphore, inc=1, device_id={axis: peer}, device_id_type=MESH)

    for peer in others:
        greet(barrier, "tm", peer, rank(peer, shards) > my_rank)
    for peer in other_bands:
        greet(barrier, "dm", peer, band_order(peer) > band_rank)
    lowers = my_rank - 1 + band_rank - jnp.where(me == 0, 1, 0)

    @pl.when(lowers > 0)
    def _():
        pl.semaphore_wait(barrier, lowers)

    for peer in others:
        greet(here_shard.at[me], "tm", peer, rank(peer, shards) < my_rank)

    def remote(src, dst, send, recv, axis, peer):
        return pltpu.make_async_remote_copy(
            src_ref=src, dst_ref=dst, send_sem=send, recv_sem=recv,
            device_id={axis: peer}, device_id_type=MESH,
        )

    def x_copy(peer, slot):
        rows = pl.ds(pl.multiple_of(peer * x_rows, x_rows), x_rows)
        return remote(x_ref.at[rows], x_in.at[slot], send_x.at[peer], recv_x.at[slot], "tm", peer)

    def y_copy(peer, slot):
        rows = pl.ds(pl.multiple_of(slot * 8, 8), 8)
        return remote(y_out.at[peer], y_in.at[:, rows], send_y.at[peer], recv_y.at[slot], "tm", peer)

    def h_copy(peer, slot, rows):
        part = pl.ds(0, rows)
        return remote(
            h_out.at[peer, part], h_in.at[slot, part], send_h.at[peer], recv_h.at[slot], "tm", peer
        )

    def s_copy(peer, slot):
        return remote(st_out, st_in.at[slot], send_s.at[peer], recv_s.at[slot], "tm", peer)

    def m_copy(peer, slot):
        return remote(mk_out.at[peer], mk_in.at[slot], send_m.at[peer], recv_m.at[slot], "dm", peer)

    def p_copy(peer, slot):
        return remote(pk_out, pk_in.at[slot], send_p.at[peer], recv_p.at[slot], "dm", peer)

    for peer in others:

        @pl.when(rank(peer, shards) < my_rank)
        def _(peer=peer):
            x_copy(peer, me).start()

    own_rows = pl.ds(pl.multiple_of(me * x_rows, x_rows), x_rows)
    own_x = pltpu.make_async_copy(x_ref.at[own_rows], x_in.at[me], local_sem.at[0])
    own_x.start()
    get_starts = pltpu.make_async_copy(start_hbm, start_ref, local_sem.at[1])
    get_starts.start()
    get_counts = pltpu.make_async_copy(count_hbm, count_ref, local_sem.at[2])
    get_counts.start()
    get_tab = pltpu.make_async_copy(tab_hbm, tab, local_sem.at[3])
    get_tab.start()

    for peer in other_bands:
        greet(here_band.at[band], "dm", peer, band_order(peer) < band_rank)
    for i in range(1, shards):
        peer = lax.rem(me + i, shards)

        @pl.when(rank(peer, shards) > my_rank)
        def _(peer=peer):
            pl.semaphore_wait(here_shard.at[peer], 1)
            x_copy(peer, me).start()

    slots = start_ref.shape[1]
    get_starts.wait()
    get_counts.wait()
    starts = start_ref[...].astype(jnp.float32)
    starts = jnp.concatenate(
        [starts, jnp.full((bands, LANES - slots), -1.0, jnp.float32)], axis=1
    )
    lane_row = lax.broadcasted_iota(jnp.int32, (1, LANES), 1)
    for d in range(bands):
        mk_out[d] = jnp.where(lane_row < count_ref[d], starts[d : d + 1], -1.0)
    mk_in[band] = mk_out[band]

    get_tab.wait()

    def table(index, rows):
        first = offsets[index]
        return tab[first : first + rows, :]

    def wide(index, rows):
        first = offsets[index]
        return jnp.concatenate(
            [tab[first : first + rows, :], tab[first + rows : first + 2 * rows, :]], axis=1
        )

    def wide_row(index, at):
        first = offsets[index]
        return jnp.concatenate(
            [tab[pl.ds(first + at, 1), :], tab[pl.ds(first + RADIX + at, 1), :]], axis=1
        )

    paired = jnp.where(job == 0, 0.0, 1.0).astype(jnp.float32)
    alone = 1.0 - paired
    residues = (job, jnp.where(job == 0, RADIX // 2, RADIX - job))
    waves = []
    for c, residue in enumerate(residues):
        bc, bs = table(0, LEFT), table(1, LEFT)
        vc = tab[pl.ds(offsets[6] + residue, 1), :]
        vs = tab[pl.ds(offsets[7] + residue, 1), :]
        waves.append((bc * vc - bs * vs, bs * vc + bc * vs))
        bc, bs = wide(2, LEFT), wide(3, LEFT)
        vc, vs = wide_row(8, residue), wide_row(9, residue)
        t_cos[c] = bc * vc - bs * vs
        t_sin[c] = bs * vc + bc * vs
    (ca, sa), (cb, sb) = waves
    blocks = (
        (ca, paired * sa),
        (-sa, paired * ca),
        (paired * cb, alone * cb - paired * sb),
        (-paired * sb, -alone * sb - paired * cb),
    )
    for i, block in enumerate(blocks):
        high, low = split(jnp.concatenate(block, axis=1))
        w_hi[LEFT * i : LEFT * (i + 1), :] = high
        w_lo[LEFT * i : LEFT * (i + 1), :] = low
    gc, gs = wide(4, LEFT), wide(5, LEFT)
    for i, block in enumerate(((gc, gs), (-gs, gc))):
        high, low = split(jnp.concatenate(block, axis=1))
        g_hi[LEFT * i : LEFT * (i + 1), :] = high
        g_lo[LEFT * i : LEFT * (i + 1), :] = low

    own_x.wait()
    for i in range(1, shards):
        slot = lax.rem(me + shards - i, shards)
        x_copy(slot, slot).wait_recv()
    for row in range(2):
        for side in range(RIGHT // LANES):
            pick = pl.ds(2 * side + row, 8, stride=4)
            terms = radix_transform([x_in[t, pick, :] for t in range(shards)])
            lanes = slice(side * LANES, (side + 1) * LANES)
            for j in range(JOBS):
                re, im = (terms[0][0], terms[JOBS][0]) if j == 0 else terms[j]
                y_out[2 * j + row, 0, :, lanes] = re
                y_out[2 * j + row, 1, :, lanes] = im
    for peer in others:
        y_copy(peer, me).start()
    y_in[:, pl.ds(pl.multiple_of(me * 8, 8), 8), :] = y_out[me]

    for i in range(1, shards):
        slot = lax.rem(me + shards - i, shards)
        y_copy(slot, slot).wait_recv()

    y = jnp.concatenate([y_in[0], y_in[1]], axis=0)
    u = dot_split((w_hi[...], w_lo[...]), split(y), ((1,), (0,)))
    turned = []
    for c in range(2):
        ur, ui = u[2 * c * LEFT : (2 * c + 1) * LEFT], u[(2 * c + 1) * LEFT : (2 * c + 2) * LEFT]
        turned.append(
            jnp.concatenate(
                [ur * t_cos[c] + ui * t_sin[c], ui * t_cos[c] - ur * t_sin[c]], axis=1
            )
        )
    v = jnp.concatenate(turned, axis=0)
    z = dot_split((g_hi[...], g_lo[...]), split(v), ((1,), (1,)))
    zr, zi = z[:LEFT], z[LEFT:]
    power = (zr * zr + zi * zi) * (1.0 / total)
    pw[0] = power[:, :LEFT]
    pw[1] = power[:, LEFT:]

    groups = LEFT * LEFT // (HARM * LANES)
    lane = lax.broadcasted_iota(jnp.int32, (groups, LANES), 1)

    def decimate(which, harmonic, offset, cache):
        if (which, harmonic) not in cache:
            cache[which, harmonic] = [
                pw[which, pl.ds(b, groups, stride=harmonic), :] if harmonic > 1 else pw[which, pl.ds(0, groups), :]
                for b in range(harmonic)
            ]
        rows = cache[which, harmonic]
        if harmonic == 1:
            return rows[0]
        place = lane * harmonic + offset
        index, block = place & (LANES - 1), place >> 7
        out = jnp.take_along_axis(rows[0], index, axis=1, mode="promise_in_bounds")
        for b in range(1, harmonic):
            got = jnp.take_along_axis(rows[b], index, axis=1, mode="promise_in_bounds")
            out = jnp.where(block == b, got, out)
        return out

    for j in range(JOBS):

        @pl.when(job == j)
        def _(j=j):
            cache = {}
            found = picks(j)
            slot_count = HALF if j % 2 else len(SLOT_RESIDUES)
            for slot in range(slot_count):
                acc = None
                for which, harmonic, offset in found.get(slot, []):
                    got = decimate(which, harmonic, offset, cache)
                    acc = got if acc is None else acc + got
                if acc is None:
                    acc = jnp.zeros((groups, LANES), jnp.float32)
                h_out[:, slot, :] = acc

    odd = job % 2 == 1

    @pl.when(odd)
    def _():
        for peer in others:
            h_copy(peer, me, HALF).start()
        h_in[me, :HALF] = h_out[me, :HALF]

    @pl.when(jnp.logical_not(odd))
    def _():
        for peer in others:
            h_copy(peer, me, 2 * HALF).start()
        h_in[me] = h_out[me]

    count = 2 * LEFT * LEFT
    mean = jnp.sum(power, keepdims=True).reshape(1, 1) * (1.0 / count)
    away = power - mean
    squares = jnp.sum(away * away, keepdims=True).reshape(1, 1)
    st_out[0:1, :] = jnp.broadcast_to(mean, (1, LANES))
    st_out[1:2, :] = jnp.broadcast_to(squares, (1, LANES))
    for peer in others:
        s_copy(peer, me).start()
    st_in[me] = st_out[...]

    for peer in other_bands:

        @pl.when(band_order(peer) > band_rank)
        def _(peer=peer):
            pl.semaphore_wait(here_band.at[peer], 1)

        m_copy(peer, band).start()

    for v in range(shards):

        @pl.when(v != me)
        def _(v=v):
            h_copy(v, v, HALF if (v // 2) % 2 else 2 * HALF).wait_recv()
            s_copy(v, v).wait_recv()

    rows_out = []
    for row in range(2):
        sources = [2 * j + row for j in range(JOBS)]
        stats = [st_in[v] for v in sources]
        mean = sum(s[0:1] for s in stats) * (1.0 / JOBS)
        squares = sum(s[1:2] for s in stats)
        between = sum((s[0:1] - mean) * (s[0:1] - mean) for s in stats)
        spread = (squares + between * float(count)) * (1.0 / bins)
        scale = 1.0 / jnp.sqrt(spread + EPSILON)
        first = sum(h_in[v, :HALF, :] for v in sources)
        second = sum(h_in[v, HALF:, :] for v in sources if (v // 2) % 2 == 0)
        summed = jnp.concatenate([first, second], axis=0)
        rows_out.append((summed - float(HARM) * mean) * scale)

    both = jnp.concatenate(rows_out, axis=1)
    stacked = jnp.concatenate([p.astype(jnp.float32) for p in split_exactly(both)], axis=0).astype(jnp.bfloat16)
    places = stacked.shape[0]
    slot_at = lax.broadcasted_iota(jnp.int32, (places, LANES), 0) & (RADIX - 1)
    lane_at = lax.broadcasted_iota(jnp.int32, (places, LANES), 1) & (RADIX - 1)
    residue_of = jnp.where(
        slot_at < 8, 2 * slot_at + 1,
        jnp.where(slot_at < 12, 4 * slot_at - 30, jnp.where(slot_at < 14, 8 * slot_at - 92, jnp.where(slot_at == 14, 8, 0))),
    )
    chosen = (residue_of == lane_at).astype(jnp.float32).astype(jnp.bfloat16)
    laid = dot(stacked, chosen, ((0,), (0,)))
    at = lax.broadcasted_iota(jnp.int32, laid.shape, 0) & (LANES // RADIX - 1)
    lane = lax.broadcasted_iota(jnp.int32, laid.shape, 1) >> 4
    laid = jnp.where(at == lane, laid, 0.0)
    laid = jnp.sum(laid.reshape(2 * groups, LANES // RADIX, LANES), axis=1)
    top, low = laid[:groups], laid[groups:]
    pk_out[...] = jnp.maximum(top, low)
    for peer in other_bands:
        p_copy(peer, band).start()
    hsum_ref[pl.ds(0, groups, stride=2), :] = top
    hsum_ref[pl.ds(1, groups, stride=2), :] = low
    level = (top + low) * 0.5
    pk_in[band] = pk_out[...]

    for i in range(1, bands):
        slot = lax.rem(band + bands - i, bands)
        m_copy(slot, slot).wait_recv()
    lane = lax.broadcasted_iota(jnp.int32, (slots, LANES), 1)
    slot_id = lax.broadcasted_iota(jnp.int32, (slots, LANES), 0)
    marks = []
    for d in range(bands):
        spread_row = jnp.broadcast_to(mk_in[d], (slots, LANES))
        column = jnp.sum(jnp.where(lane == slot_id, spread_row, 0.0), axis=1, keepdims=True)
        marks.append(jnp.broadcast_to(column, (slots, LANES)).astype(jnp.int32))

    for peer in others:
        x_copy(peer, me).wait_send()
        y_copy(peer, me).wait_send()
        s_copy(peer, me).wait_send()

    @pl.when(odd)
    def _():
        for peer in others:
            h_copy(peer, me, HALF).wait_send()

    @pl.when(jnp.logical_not(odd))
    def _():
        for peer in others:
            h_copy(peer, me, 2 * HALF).wait_send()

    for peer in other_bands:
        m_copy(peer, band).wait_send()

    for i in range(1, bands):
        slot = lax.rem(band + bands - i, bands)
        p_copy(slot, slot).wait_recv()
    sift(bands, groups, slots, [pk_in[d] - level for d in range(bands)], marks, out_ref)

    for peer in other_bands:
        p_copy(peer, band).wait_send()


def per_device(series, cand_start, cand_count):
    dm_rows, samples = series.shape
    shards, bands = lax.axis_size("tm"), lax.axis_size("dm")
    total = samples * shards
    slots = cand_start.shape[3]
    fundamentals = total // (2 * HARM) // shards
    assert shards == RADIX and dm_rows == 2 and samples == LEFT * RIGHT
    chunks = samples // LANES
    x = series.reshape(dm_rows, chunks, LANES).transpose(1, 0, 2).reshape(dm_rows * chunks, LANES)
    tab, offsets = tables(total)
    groups = fundamentals // LANES
    f32, bf16 = jnp.float32, jnp.bfloat16
    vmem = pl.BlockSpec(memory_space=pltpu.VMEM)
    hbm = pl.BlockSpec(memory_space=pltpu.HBM)
    dma = pltpu.SemaphoreType.DMA
    hsum, sifted = pl.pallas_call(
        functools.partial(search_kernel, shards, bands, tuple(offsets), total),
        name="search",
        out_shape=(
            jax.ShapeDtypeStruct((dm_rows * groups, LANES), f32),
            jax.ShapeDtypeStruct((bands, slots, BW), f32),
        ),
        in_specs=[hbm] * 4,
        out_specs=[vmem] * 2,
        scratch_shapes=[
            pltpu.VMEM((bands, slots), jnp.int32),
            pltpu.SMEM((bands,), jnp.int32),
            pltpu.VMEM(tab.shape, f32),
            pltpu.VMEM((shards, dm_rows * chunks // shards, LANES), f32),
            pltpu.VMEM((shards, 2, LEFT // shards, RIGHT), f32),
            pltpu.VMEM((2, LEFT, RIGHT), f32),
            pltpu.VMEM((4 * LEFT, 2 * LEFT), bf16),
            pltpu.VMEM((4 * LEFT, 2 * LEFT), bf16),
            pltpu.VMEM((2 * LEFT, 2 * RIGHT), bf16),
            pltpu.VMEM((2 * LEFT, 2 * RIGHT), bf16),
            pltpu.VMEM((2, LEFT, RIGHT), f32),
            pltpu.VMEM((2, LEFT, RIGHT), f32),
            pltpu.VMEM((2, LEFT, LEFT), f32),
            pltpu.VMEM((shards, 2 * HALF, LANES), f32),
            pltpu.VMEM((shards, 2 * HALF, LANES), f32),
            pltpu.VMEM((2, LANES), f32),
            pltpu.VMEM((shards, 2, LANES), f32),
            pltpu.VMEM((bands, 1, LANES), f32),
            pltpu.VMEM((bands, 1, LANES), f32),
            pltpu.VMEM((groups, LANES), f32),
            pltpu.VMEM((bands, groups, LANES), f32),
            *[dma((shards,)) for _ in range(8)],
            *[dma((bands,)) for _ in range(4)],
            dma((4,)),
            pltpu.SemaphoreType.REGULAR((shards,)),
            pltpu.SemaphoreType.REGULAR((bands,)),
        ],
        compiler_params=pltpu.CompilerParams(
            collective_id=0, has_side_effects=True, vmem_limit_bytes=24 << 20
        ),
    )(*[pltpu.with_memory_space_constraint(a, pltpu.HBM) for a in (x, cand_start.reshape(bands, slots), cand_count.reshape(bands), jnp.asarray(tab))])
    harmonic = hsum.reshape(groups, dm_rows, LANES).transpose(1, 0, 2)
    return harmonic.reshape(dm_rows, fundamentals), sifted[None, None]


def solution(mesh):
    return jax.shard_map(
        per_device,
        mesh=mesh,
        in_specs=(
            P(("beam", "dm"), "tm"),
            P(("beam", "tm"), "dm", None, None),
            P(("beam", "tm"), "dm", None),
        ),
        out_specs=(P(("beam", "dm"), "tm"), P(("beam", "tm"), "dm", None, None, None)),
        check_vma=False,
    )
```

```python
import functools
import math

import jax
import jax.numpy as jnp
import numpy as np
from jax import lax
from jax.experimental import pallas as pl
from jax.experimental.pallas import tpu as pltpu
from jax.sharding import PartitionSpec as P

HARM = 8
BW = 128
EPSILON = 1e-06
LANES = 128
RADIX = 16
JOBS = RADIX // 2
LEFT, RIGHT = 128, 256
MESH = pl.DeviceIdType.MESH
SLOT_RESIDUES = (1, 3, 5, 7, 9, 11, 13, 15, 2, 6, 10, 14, 4, 12, 8, 0)
HALF = JOBS


def tables(total):
    def wave(left, right, period):
        angle = 2.0 * math.pi * (np.outer(left, right) % period) / period
        return np.cos(angle), np.sin(angle)

    left, right, radix = np.arange(LEFT), np.arange(RIGHT), np.arange(RADIX)
    parts = [
        *wave(left, left, LEFT),
        *wave(left, right, LEFT * RIGHT),
        *wave(left, right, RIGHT),
        *wave(radix, left, RADIX * LEFT),
        *wave(radix, right, total),
    ]
    rows, offsets = [], []
    for part in parts:
        offsets.append(sum(r.shape[0] for r in rows))
        for lane in range(0, part.shape[1], LANES):
            rows.append(part[:, lane : lane + LANES])
    return np.concatenate(rows).astype(np.float32), offsets


def split(value):
    high = value.astype(jnp.bfloat16)
    return high, (value - high.astype(jnp.float32)).astype(jnp.bfloat16)


def split_exactly(value):
    high, rest = value.astype(jnp.bfloat16), None
    rest = value - high.astype(jnp.float32)
    middle = rest.astype(jnp.bfloat16)
    return high, middle, (rest - middle.astype(jnp.float32)).astype(jnp.bfloat16)


def dot(left, right, dims):
    return lax.dot_general(left, right, (dims, ((), ())), preferred_element_type=jnp.float32)


def dot_split(left, right, dims):
    (lh, ll), (rh, rl) = left, right
    (la,), (ra,) = dims
    return dot(jnp.concatenate([lh, ll, lh], axis=la), jnp.concatenate([rh, rh, rl], axis=ra), dims)


def radix_transform(x):
    half, quarter = RADIX // 2, RADIX // 4

    def real_transform(values, count):
        if count == 1:
            return [(values[0], None)]
        low = [values[i] + values[i + count // 2] for i in range(count // 2)]
        high = [values[i] - values[i + count // 2] for i in range(count // 2)]
        out = {2 * i: v for i, v in enumerate(real_transform(low, count // 2))}
        if count == 2:
            out[1] = (high[0], None)
        elif count == 4:
            out[1] = (high[0], -high[1])
        else:
            h, q = count // 2, count // 4
            minus = [None] + [high[i] - high[h - i] for i in range(1, q)]
            plus = [None] + [high[i] + high[h - i] for i in range(1, q)]
            for term in range(1, h, 2):
                re, im = high[0], high[q] * (-math.sin(2 * math.pi * q * term / count))
                for i in range(1, q):
                    re = re + minus[i] * math.cos(2 * math.pi * i * term / count)
                    im = im - plus[i] * math.sin(2 * math.pi * i * term / count)
                out[term] = (re, im)
        return [out[i] for i in range(count // 2 + 1)]

    return real_transform(x, RADIX)


def picks(job):
    pair = (0, RADIX // 2) if job == 0 else (job, RADIX - job)
    found = {}
    for slot, residue in enumerate(SLOT_RESIDUES):
        for harmonic in range(1, HARM + 1):
            product = harmonic * residue
            if product % RADIX in pair:
                found.setdefault(slot, []).append(
                    (pair.index(product % RADIX), harmonic, product // RADIX)
                )
    return found


def far_first(count):
    return sorted(range(1, count), key=lambda i: -min(i, count - i))


def sift(bands, groups, slots, differences, marks, out_ref):
    lane = lax.broadcasted_iota(jnp.int32, (slots, LANES), 1)
    live = lane < 3 * groups
    wanted = lane & (groups - 1)
    for d in range(bands):
        mark = marks[d]
        begin = jnp.maximum(mark, 0)
        row, shift = begin >> 7, begin & (LANES - 1)
        parts = [p.astype(jnp.float32) for p in split_exactly(differences[d])]
        parts.append(jnp.zeros((LANES - 3 * groups, LANES), jnp.float32))
        source = jnp.concatenate(parts, axis=0).astype(jnp.bfloat16)
        first = jnp.where(live & (wanted == row), 1.0, 0.0)
        second = jnp.where(live & (wanted == row + 1), 1.0, 0.0)
        choose = jnp.concatenate([first, second], axis=0).astype(jnp.bfloat16)
        pair = dot(choose, source, ((1,), (0,)))
        index = (lane + shift) & (LANES - 1)
        low = jnp.take_along_axis(pair[:slots], index, axis=1, mode="promise_in_bounds")
        high = jnp.take_along_axis(pair[slots:], index, axis=1, mode="promise_in_bounds")
        value = jnp.where(lane + shift < LANES, low, high)
        out_ref[d] = jnp.where(mark >= 0, value, 0.0)


def search_kernel(
    shards, bands, offsets, total,
    x_ref, start_hbm, count_hbm, tab_hbm,
    hsum_ref, out_ref,
    start_ref, count_ref, tab, x_in, y_out, y_in, w_hi, w_lo, g_hi, g_lo, t_cos, t_sin, pw,
    h_out, h_in, st_out, st_in, mk_out, mk_in, pk_out, pk_in,
    send_x, recv_x, send_y, recv_y, send_h, recv_h, send_s, recv_s,
    send_m, recv_m, send_p, recv_p, local_sem, here_shard, here_band,
):
    me = lax.axis_index("tm")
    band = lax.axis_index("dm")
    job, row_kept = me // 2, me % 2
    bins = total // 2
    x_rows = x_in.shape[1]

    barrier = pltpu.get_barrier_semaphore()
    others = [lax.rem(me + i, shards) for i in far_first(shards)]
    other_bands = [lax.rem(band + i, bands) for i in far_first(bands)]

    def rank(index, count):
        return jnp.where(index == 0, count, index)

    def band_order(index):
        return jnp.where((index == 0) & (me == 0), bands, index)

    my_rank, band_rank = rank(me, shards), band_order(band)

    def greet(semaphore, axis, peer, wanted):
        @pl.when(wanted)
        def _():
            pl.semaphore_signal(semaphore, inc=1, device_id={axis: peer}, device_id_type=MESH)

    for peer in others:
        greet(barrier, "tm", peer, rank(peer, shards) > my_rank)
    for peer in other_bands:
        greet(barrier, "dm", peer, band_order(peer) > band_rank)
    lowers = my_rank - 1 + band_rank - jnp.where(me == 0, 1, 0)

    @pl.when(lowers > 0)
    def _():
        pl.semaphore_wait(barrier, lowers)

    for peer in others:
        greet(here_shard.at[me], "tm", peer, rank(peer, shards) < my_rank)

    def remote(src, dst, send, recv, axis, peer):
        return pltpu.make_async_remote_copy(
            src_ref=src, dst_ref=dst, send_sem=send, recv_sem=recv,
            device_id={axis: peer}, device_id_type=MESH,
        )

    def x_copy(peer, slot):
        rows = pl.ds(pl.multiple_of(peer * x_rows, x_rows), x_rows)
        return remote(x_ref.at[rows], x_in.at[slot], send_x.at[peer], recv_x.at[slot], "tm", peer)

    def y_copy(peer, slot):
        rows = pl.ds(pl.multiple_of(slot * 8, 8), 8)
        return remote(y_out.at[peer], y_in.at[:, rows], send_y.at[peer], recv_y.at[slot], "tm", peer)

    def h_copy(peer, slot, rows):
        part = pl.ds(0, rows)
        return remote(
            h_out.at[peer, part], h_in.at[slot, part], send_h.at[peer], recv_h.at[slot], "tm", peer
        )

    def s_copy(peer, slot):
        return remote(st_out, st_in.at[slot], send_s.at[peer], recv_s.at[slot], "tm", peer)

    def m_copy(peer, slot):
        return remote(mk_out.at[peer], mk_in.at[slot], send_m.at[peer], recv_m.at[slot], "dm", peer)

    def p_copy(peer, slot):
        return remote(pk_out, pk_in.at[slot], send_p.at[peer], recv_p.at[slot], "dm", peer)

    for peer in others:

        @pl.when(rank(peer, shards) < my_rank)
        def _(peer=peer):
            x_copy(peer, me).start()

    own_rows = pl.ds(pl.multiple_of(me * x_rows, x_rows), x_rows)
    own_x = pltpu.make_async_copy(x_ref.at[own_rows], x_in.at[me], local_sem.at[0])
    own_x.start()
    get_starts = pltpu.make_async_copy(start_hbm, start_ref, local_sem.at[1])
    get_starts.start()
    get_counts = pltpu.make_async_copy(count_hbm, count_ref, local_sem.at[2])
    get_counts.start()
    get_tab = pltpu.make_async_copy(tab_hbm, tab, local_sem.at[3])
    get_tab.start()

    for peer in other_bands:
        greet(here_band.at[band], "dm", peer, band_order(peer) < band_rank)
    for i in range(1, shards):
        peer = lax.rem(me + i, shards)

        @pl.when(rank(peer, shards) > my_rank)
        def _(peer=peer):
            pl.semaphore_wait(here_shard.at[peer], 1)
            x_copy(peer, me).start()

    slots = start_ref.shape[1]
    get_starts.wait()
    get_counts.wait()
    starts = start_ref[...].astype(jnp.float32)
    starts = jnp.concatenate(
        [starts, jnp.full((bands, LANES - slots), -1.0, jnp.float32)], axis=1
    )
    lane_row = lax.broadcasted_iota(jnp.int32, (1, LANES), 1)
    for d in range(bands):
        mk_out[d] = jnp.where(lane_row < count_ref[d], starts[d : d + 1], -1.0)
    mk_in[band] = mk_out[band]

    get_tab.wait()

    def table(index, rows):
        first = offsets[index]
        return tab[first : first + rows, :]

    def wide(index, rows):
        first = offsets[index]
        return jnp.concatenate(
            [tab[first : first + rows, :], tab[first + rows : first + 2 * rows, :]], axis=1
        )

    def wide_row(index, at):
        first = offsets[index]
        return jnp.concatenate(
            [tab[pl.ds(first + at, 1), :], tab[pl.ds(first + RADIX + at, 1), :]], axis=1
        )

    paired = jnp.where(job == 0, 0.0, 1.0).astype(jnp.float32)
    alone = 1.0 - paired
    residues = (job, jnp.where(job == 0, RADIX // 2, RADIX - job))
    waves = []
    for c, residue in enumerate(residues):
        bc, bs = table(0, LEFT), table(1, LEFT)
        vc = tab[pl.ds(offsets[6] + residue, 1), :]
        vs = tab[pl.ds(offsets[7] + residue, 1), :]
        waves.append((bc * vc - bs * vs, bs * vc + bc * vs))
        bc, bs = wide(2, LEFT), wide(3, LEFT)
        vc, vs = wide_row(8, residue), wide_row(9, residue)
        t_cos[c] = bc * vc - bs * vs
        t_sin[c] = bs * vc + bc * vs
    (ca, sa), (cb, sb) = waves
    blocks = (
        (ca, paired * sa),
        (-sa, paired * ca),
        (paired * cb, alone * cb - paired * sb),
        (-paired * sb, -alone * sb - paired * cb),
    )
    for i, block in enumerate(blocks):
        high, low = split(jnp.concatenate(block, axis=1))
        w_hi[LEFT * i : LEFT * (i + 1), :] = high
        w_lo[LEFT * i : LEFT * (i + 1), :] = low
    gc, gs = wide(4, LEFT), wide(5, LEFT)
    for i, block in enumerate(((gc, gs), (-gs, gc))):
        high, low = split(jnp.concatenate(block, axis=1))
        g_hi[LEFT * i : LEFT * (i + 1), :] = high
        g_lo[LEFT * i : LEFT * (i + 1), :] = low

    own_x.wait()
    for i in range(1, shards):
        slot = lax.rem(me + shards - i, shards)
        x_copy(slot, slot).wait_recv()
    for row in range(2):
        for side in range(RIGHT // LANES):
            pick = pl.ds(2 * side + row, 8, stride=4)
            terms = radix_transform([x_in[t, pick, :] for t in range(shards)])
            lanes = slice(side * LANES, (side + 1) * LANES)
            for j in range(JOBS):
                re, im = (terms[0][0], terms[JOBS][0]) if j == 0 else terms[j]
                y_out[2 * j + row, 0, :, lanes] = re
                y_out[2 * j + row, 1, :, lanes] = im
    for peer in others:
        y_copy(peer, me).start()
    y_in[:, pl.ds(pl.multiple_of(me * 8, 8), 8), :] = y_out[me]

    for i in range(1, shards):
        slot = lax.rem(me + shards - i, shards)
        y_copy(slot, slot).wait_recv()

    y = jnp.concatenate([y_in[0], y_in[1]], axis=0)
    u = dot_split((w_hi[...], w_lo[...]), split(y), ((1,), (0,)))
    turned = []
    for c in range(2):
        ur, ui = u[2 * c * LEFT : (2 * c + 1) * LEFT], u[(2 * c + 1) * LEFT : (2 * c + 2) * LEFT]
        turned.append(
            jnp.concatenate(
                [ur * t_cos[c] + ui * t_sin[c], ui * t_cos[c] - ur * t_sin[c]], axis=1
            )
        )
    v = jnp.concatenate(turned, axis=0)
    z = dot_split((g_hi[...], g_lo[...]), split(v), ((1,), (1,)))
    zr, zi = z[:LEFT], z[LEFT:]
    power = (zr * zr + zi * zi) * (1.0 / total)
    pw[0] = power[:, :LEFT]
    pw[1] = power[:, LEFT:]

    groups = LEFT * LEFT // (HARM * LANES)
    lane = lax.broadcasted_iota(jnp.int32, (groups, LANES), 1)

    def decimate(which, harmonic, offset, cache):
        if (which, harmonic) not in cache:
            cache[which, harmonic] = [
                pw[which, pl.ds(b, groups, stride=harmonic), :] if harmonic > 1 else pw[which, pl.ds(0, groups), :]
                for b in range(harmonic)
            ]
        rows = cache[which, harmonic]
        if harmonic == 1:
            return rows[0]
        place = lane * harmonic + offset
        index, block = place & (LANES - 1), place >> 7
        out = jnp.take_along_axis(rows[0], index, axis=1, mode="promise_in_bounds")
        for b in range(1, harmonic):
            got = jnp.take_along_axis(rows[b], index, axis=1, mode="promise_in_bounds")
            out = jnp.where(block == b, got, out)
        return out

    for j in range(JOBS):

        @pl.when(job == j)
        def _(j=j):
            cache = {}
            found = picks(j)
            slot_count = HALF if j % 2 else len(SLOT_RESIDUES)
            for slot in range(slot_count):
                acc = None
                for which, harmonic, offset in found.get(slot, []):
                    got = decimate(which, harmonic, offset, cache)
                    acc = got if acc is None else acc + got
                if acc is None:
                    acc = jnp.zeros((groups, LANES), jnp.float32)
                h_out[:, slot, :] = acc

    odd = job % 2 == 1

    @pl.when(odd)
    def _():
        for peer in others:
            h_copy(peer, me, HALF).start()
        h_in[me, :HALF] = h_out[me, :HALF]

    @pl.when(jnp.logical_not(odd))
    def _():
        for peer in others:
            h_copy(peer, me, 2 * HALF).start()
        h_in[me] = h_out[me]

    count = 2 * LEFT * LEFT
    mean = jnp.sum(power, keepdims=True).reshape(1, 1) * (1.0 / count)
    away = power - mean
    squares = jnp.sum(away * away, keepdims=True).reshape(1, 1)
    st_out[0:1, :] = jnp.broadcast_to(mean, (1, LANES))
    st_out[1:2, :] = jnp.broadcast_to(squares, (1, LANES))
    for peer in others:
        s_copy(peer, me).start()
    st_in[me] = st_out[...]

    for peer in other_bands:

        @pl.when(band_order(peer) > band_rank)
        def _(peer=peer):
            pl.semaphore_wait(here_band.at[peer], 1)

        m_copy(peer, band).start()

    for v in range(shards):

        @pl.when(v != me)
        def _(v=v):
            h_copy(v, v, HALF if (v // 2) % 2 else 2 * HALF).wait_recv()
            s_copy(v, v).wait_recv()

    rows_out = []
    for row in range(2):
        sources = [2 * j + row for j in range(JOBS)]
        stats = [st_in[v] for v in sources]
        mean = sum(s[0:1] for s in stats) * (1.0 / JOBS)
        squares = sum(s[1:2] for s in stats)
        between = sum((s[0:1] - mean) * (s[0:1] - mean) for s in stats)
        spread = (squares + between * float(count)) * (1.0 / bins)
        scale = 1.0 / jnp.sqrt(spread + EPSILON)
        first = sum(h_in[v, :HALF, :] for v in sources)
        second = sum(h_in[v, HALF:, :] for v in sources if (v // 2) % 2 == 0)
        summed = jnp.concatenate([first, second], axis=0)
        rows_out.append((summed - float(HARM) * mean) * scale)

    both = jnp.concatenate(rows_out, axis=1)
    stacked = jnp.concatenate([p.astype(jnp.float32) for p in split_exactly(both)], axis=0).astype(jnp.bfloat16)
    places = stacked.shape[0]
    slot_at = lax.broadcasted_iota(jnp.int32, (places, LANES), 0) & (RADIX - 1)
    lane_at = lax.broadcasted_iota(jnp.int32, (places, LANES), 1) & (RADIX - 1)
    residue_of = jnp.where(
        slot_at < 8, 2 * slot_at + 1,
        jnp.where(slot_at < 12, 4 * slot_at - 30, jnp.where(slot_at < 14, 8 * slot_at - 92, jnp.where(slot_at == 14, 8, 0))),
    )
    chosen = (residue_of == lane_at).astype(jnp.float32).astype(jnp.bfloat16)
    laid = dot(stacked, chosen, ((0,), (0,)))
    at = lax.broadcasted_iota(jnp.int32, laid.shape, 0) & (LANES // RADIX - 1)
    lane = lax.broadcasted_iota(jnp.int32, laid.shape, 1) >> 4
    laid = jnp.where(at == lane, laid, 0.0)
    laid = jnp.sum(laid.reshape(2 * groups, LANES // RADIX, LANES), axis=1)
    top, low = laid[:groups], laid[groups:]
    pk_out[...] = jnp.maximum(top, low)
    for peer in other_bands:
        p_copy(peer, band).start()
    hsum_ref[pl.ds(0, groups, stride=2), :] = top
    hsum_ref[pl.ds(1, groups, stride=2), :] = low
    level = (top + low) * 0.5
    pk_in[band] = pk_out[...]

    for i in range(1, bands):
        slot = lax.rem(band + bands - i, bands)
        m_copy(slot, slot).wait_recv()
    lane = lax.broadcasted_iota(jnp.int32, (slots, LANES), 1)
    slot_id = lax.broadcasted_iota(jnp.int32, (slots, LANES), 0)
    marks = []
    for d in range(bands):
        spread_row = jnp.broadcast_to(mk_in[d], (slots, LANES))
        column = jnp.sum(jnp.where(lane == slot_id, spread_row, 0.0), axis=1, keepdims=True)
        marks.append(jnp.broadcast_to(column, (slots, LANES)).astype(jnp.int32))

    for peer in others:
        x_copy(peer, me).wait_send()
        y_copy(peer, me).wait_send()
        s_copy(peer, me).wait_send()

    @pl.when(odd)
    def _():
        for peer in others:
            h_copy(peer, me, HALF).wait_send()

    @pl.when(jnp.logical_not(odd))
    def _():
        for peer in others:
            h_copy(peer, me, 2 * HALF).wait_send()

    for peer in other_bands:
        m_copy(peer, band).wait_send()

    for i in range(1, bands):
        slot = lax.rem(band + bands - i, bands)
        p_copy(slot, slot).wait_recv()
    sift(bands, groups, slots, [pk_in[d] - level for d in range(bands)], marks, out_ref)

    for peer in other_bands:
        p_copy(peer, band).wait_send()


def per_device(series, cand_start, cand_count):
    dm_rows, samples = series.shape
    shards, bands = lax.axis_size("tm"), lax.axis_size("dm")
    total = samples * shards
    slots = cand_start.shape[3]
    fundamentals = total // (2 * HARM) // shards
    assert shards == RADIX and dm_rows == 2 and samples == LEFT * RIGHT
    chunks = samples // LANES
    x = series.reshape(dm_rows, chunks, LANES).transpose(1, 0, 2).reshape(dm_rows * chunks, LANES)
    tab, offsets = tables(total)
    groups = fundamentals // LANES
    f32, bf16 = jnp.float32, jnp.bfloat16
    vmem = pl.BlockSpec(memory_space=pltpu.VMEM)
    hbm = pl.BlockSpec(memory_space=pltpu.HBM)
    dma = pltpu.SemaphoreType.DMA
    hsum, sifted = pl.pallas_call(
        functools.partial(search_kernel, shards, bands, tuple(offsets), total),
        name="search",
        out_shape=(
            jax.ShapeDtypeStruct((dm_rows * groups, LANES), f32),
            jax.ShapeDtypeStruct((bands, slots, BW), f32),
        ),
        in_specs=[hbm] * 4,
        out_specs=[vmem] * 2,
        scratch_shapes=[
            pltpu.VMEM((bands, slots), jnp.int32),
            pltpu.SMEM((bands,), jnp.int32),
            pltpu.VMEM(tab.shape, f32),
            pltpu.VMEM((shards, dm_rows * chunks // shards, LANES), f32),
            pltpu.VMEM((shards, 2, LEFT // shards, RIGHT), f32),
            pltpu.VMEM((2, LEFT, RIGHT), f32),
            pltpu.VMEM((4 * LEFT, 2 * LEFT), bf16),
            pltpu.VMEM((4 * LEFT, 2 * LEFT), bf16),
            pltpu.VMEM((2 * LEFT, 2 * RIGHT), bf16),
            pltpu.VMEM((2 * LEFT, 2 * RIGHT), bf16),
            pltpu.VMEM((2, LEFT, RIGHT), f32),
            pltpu.VMEM((2, LEFT, RIGHT), f32),
            pltpu.VMEM((2, LEFT, LEFT), f32),
            pltpu.VMEM((shards, 2 * HALF, LANES), f32),
            pltpu.VMEM((shards, 2 * HALF, LANES), f32),
            pltpu.VMEM((2, LANES), f32),
            pltpu.VMEM((shards, 2, LANES), f32),
            pltpu.VMEM((bands, 1, LANES), f32),
            pltpu.VMEM((bands, 1, LANES), f32),
            pltpu.VMEM((groups, LANES), f32),
            pltpu.VMEM((bands, groups, LANES), f32),
            *[dma((shards,)) for _ in range(8)],
            *[dma((bands,)) for _ in range(4)],
            dma((4,)),
            pltpu.SemaphoreType.REGULAR((shards,)),
            pltpu.SemaphoreType.REGULAR((bands,)),
        ],
        compiler_params=pltpu.CompilerParams(
            collective_id=0, has_side_effects=True, vmem_limit_bytes=24 << 20
        ),
    )(*[pltpu.with_memory_space_constraint(a, pltpu.HBM) for a in (x, cand_start.reshape(bands, slots), cand_count.reshape(bands), jnp.asarray(tab))])
    harmonic = hsum.reshape(groups, dm_rows, LANES).transpose(1, 0, 2)
    return harmonic.reshape(dm_rows, fundamentals), sifted[None, None]


def solution(mesh):
    return jax.shard_map(
        per_device,
        mesh=mesh,
        in_specs=(
            P(("beam", "dm"), "tm"),
            P(("beam", "tm"), "dm", None, None),
            P(("beam", "tm"), "dm", None),
        ),
        out_specs=(P(("beam", "dm"), "tm"), P(("beam", "tm"), "dm", None, None, None)),
        check_vma=False,
    )
```
